256 devices in a mesh: band: 64 (over z, y, core), sub: 4 (over x).
Axes of the slice: x: 4, y: 4, z: 8, core: 2. Of those that a mesh axis runs over, the one named last changes fastest.
Arguments:
- grid_x: bfloat16 [227, 131072], P(None, ('band', 'sub')), may hold values from -6 to 6
- mesh_in: bfloat16 [16384, 512], P(('band', 'sub')), may hold values from -6 to 6
- w_embed: bfloat16 [227, 512], replicated, may hold values from -0.375 to 0.375
- w_src: bfloat16 [512, 512], replicated, may hold values from -0.25 to 0.25
- w_dst: bfloat16 [512, 512], replicated, may hold values from -0.25 to 0.25
- w_edge: bfloat16 [512, 512], replicated, may hold values from -0.25 to 0.25
- w_proc: bfloat16 [512, 512], replicated, may hold values from -0.25 to 0.25
- w_recv: bfloat16 [512, 512], replicated, may hold values from -0.25 to 0.25
- g2m_src: int32 [16384, 40], P(('band', 'sub')), may hold values from 0 to 131071, as said below
- mesh_src: int32 [16384, 6], P(('band', 'sub')), may hold values from 0 to 16383, as said below
- cotangent: bfloat16 [16384, 512], P(('band', 'sub')), may hold values from -6 to 6
Outputs:
- mesh_out: bfloat16 [16384, 512], P(('band', 'sub'))
- grid_grad: float32 [227, 131072], P(None, ('band', 'sub'))
- src_grad: float32 [512, 512], replicated
- edge_grad: float32 [512, 512], replicated
The draws below stay inside these ranges and needn't reach their ends.
Inputs may be any that keep to these rules, and one draw needn't show every extreme that they name: Grid node g belongs to band g // (512 * 4), mesh node m to band m // (64 * 4); g2m_src[m, k] lies in the band of mesh node m, or among the 512 grid nodes of an adjacent band that stand next to that band in index order. mesh_src[m, j] lies in the band of mesh node m, or among the 64 mesh nodes of an adjacent band that stand next to that band in index order.
All inputs are finite; a program needn't handle non-finite values.
Results may differ from the reference program's by a relative error of at most 0.015.
Values may be sent and summed in bfloat16 or wider, within the bound.
No kernel may reach another device: no remote copies, remote signals or barrier semaphores. Data moves between devices by JAX's collectives and lax.ppermute only.
A program may use at most 128 MiB of HBM per device.

```python
import math
import jax
import jax.numpy as jnp
from jax import lax

LATENT = 512
CHANNELS = 227
GRID_DEV = 512
MESH_DEV = 64
ENC_EDGES = 40
MESH_EDGES = 6
GRID = 131072
MESH = 16384
N_BAND = 64
N_SUB = 4


def band_sources(key, count, edges, node_dev, source_dev):
    node_band = jnp.arange(count, dtype=jnp.int32) // (node_dev * N_SUB)
    width = source_dev * N_SUB
    total = width * N_BAND
    lowest = jnp.maximum(node_band * width - source_dev, 0)
    highest = jnp.minimum((node_band + 1) * width + source_dev, total)
    return jax.random.randint(key, (count, edges), lowest[:, None], highest[:, None], dtype=jnp.int32)


def draw_g2m_src(key, part):
    return band_sources(jax.random.fold_in(key, 11), MESH, ENC_EDGES, MESH_DEV, GRID_DEV)


def draw_mesh_src(key, part):
    return band_sources(jax.random.fold_in(key, 23), MESH, MESH_EDGES, MESH_DEV, MESH_DEV)


def block_scale(own_key, extent, shards, low, largest):
    gain, own = 1.0, jax.random.fold_in(own_key, 6)
    for position, blocks in shards:
        draws = jnp.exp(jax.random.uniform(jax.random.fold_in(own, position), (blocks,), jnp.float32, low / len(shards), largest / len(shards)))
        gain = gain * jnp.repeat(draws, extent[position] // blocks).reshape([-1 if axis == position else 1 for axis in range(len(extent))])
    return gain


def noise(own_key, shape, scale, reach, shards=(), kind=jnp.bfloat16):
    values = jax.random.normal(own_key, shape, jnp.float32) * scale
    if len(shards) > 0:
        values = block_scale(own_key, shape, shards, -0.22, 0.18) * values
    return jnp.clip(values, min=-reach, max=reach).astype(kind)


def setup_inputs(seed: int = 0) -> dict:
    arg_keys = jax.random.split(jax.random.key(seed), 12)
    return {
        "grid_x": noise(arg_keys[0], (CHANNELS, GRID), 1.0, 6.0, ((1, 256),)),
        "mesh_in": noise(arg_keys[1], (MESH, LATENT), 1.0, 6.0, ((0, 256),)),
        "w_embed": noise(arg_keys[2], (CHANNELS, LATENT), CHANNELS ** -0.5, 0.375),
        "w_src": noise(arg_keys[3], (LATENT, LATENT), LATENT ** -0.5, 0.25),
        "w_dst": noise(arg_keys[4], (LATENT, LATENT), LATENT ** -0.5, 0.25),
        "w_edge": noise(arg_keys[5], (LATENT, LATENT), LATENT ** -0.5, 0.25),
        "w_proc": noise(arg_keys[6], (LATENT, LATENT), LATENT ** -0.5, 0.25),
        "w_recv": noise(arg_keys[7], (LATENT, LATENT), LATENT ** -0.5, 0.25),
        "g2m_src": draw_g2m_src(jax.random.fold_in(arg_keys[11], 71), 0),
        "mesh_src": draw_mesh_src(jax.random.fold_in(arg_keys[11], 71), 0),
        "cotangent": noise(arg_keys[10], (MESH, LATENT), 1.0, 6.0, ((0, 256),)),
    }


EPSILON = 1e-05

def silu_slope(value):
    sigma = jax.nn.sigmoid(value)
    return sigma * (1.0 + value * (1.0 - sigma))

def normalize(value):
    centred = value - lax.optimization_barrier(jnp.mean(value, axis=-1, keepdims=True))
    spread = jnp.sqrt(lax.optimization_barrier(jnp.mean(centred * centred, axis=-1, keepdims=True)) + EPSILON)
    return (centred / spread, spread)

def times_transpose(left, right):
    return lax.dot_general(left, right, (((1,), (1,)), ((), ())), preferred_element_type=jnp.float32)

def first_contract(left, right):
    return lax.dot_general(left, right, (((0,), (0,)), ((), ())), preferred_element_type=jnp.float32)

def encoder_edges(projected, indices, dest_term, w_edge):
    rows = dest_term.shape[0]
    before = jnp.take(projected, indices, axis=0).astype(jnp.float32)
    before = (before.reshape(rows, ENC_EDGES, LATENT) + dest_term[:, None, :]).reshape(rows * ENC_EDGES, LATENT)
    active = jax.nn.silu(before).astype(jnp.bfloat16)
    normed, spread = normalize(jnp.dot(active, w_edge, preferred_element_type=jnp.float32))
    return (before, active, normed, spread)

def reference(grid_x, mesh_in, w_embed, w_src, w_dst, w_edge, w_proc, w_recv, g2m_src, mesh_src, cotangent):
    blocks = MESH // MESH_DEV
    hidden_pre = first_contract(grid_x, w_embed)
    hidden_grid = jax.nn.silu(hidden_pre).astype(jnp.bfloat16)
    projected = jnp.dot(hidden_grid, w_src, preferred_element_type=jnp.float32).astype(jnp.bfloat16)
    dest_term = jnp.dot(mesh_in, w_dst, preferred_element_type=jnp.float32)
    index_blocks = g2m_src.reshape(blocks, MESH_DEV * ENC_EDGES)
    dest_blocks = dest_term.reshape(blocks, MESH_DEV, LATENT)

    def encode(pair):
        before, active, normed, spread = encoder_edges(projected, pair[0], pair[1], w_edge)
        return lax.optimization_barrier(jnp.sum(normed.reshape(MESH_DEV, ENC_EDGES, LATENT), axis=1))
    encoded = lax.map(encode, (index_blocks, dest_blocks)).reshape(MESH, LATENT)
    hidden_mesh = (mesh_in.astype(jnp.float32) + encoded / math.sqrt(ENC_EDGES)).astype(jnp.bfloat16)
    query = jnp.dot(hidden_mesh, w_proc, preferred_element_type=jnp.float32).astype(jnp.bfloat16)
    receiver = jnp.dot(hidden_mesh, w_recv, preferred_element_type=jnp.float32)
    flat_mesh = mesh_src.reshape(-1)
    mesh_before = jnp.take(query, flat_mesh, axis=0).astype(jnp.float32).reshape(MESH, MESH_EDGES, LATENT)
    mesh_before = mesh_before + receiver[:, None, :]
    summed = lax.optimization_barrier(jnp.sum(jax.nn.silu(mesh_before), axis=1))
    mesh_out = (hidden_mesh.astype(jnp.float32) + summed / math.sqrt(MESH_EDGES)).astype(jnp.bfloat16)
    upstream = cotangent.astype(jnp.float32)
    mesh_slope = (upstream / math.sqrt(MESH_EDGES))[:, None, :] * silu_slope(mesh_before)
    receiver_grad = lax.optimization_barrier(jnp.sum(mesh_slope, axis=1))
    query_grad = jnp.zeros((MESH, LATENT), jnp.float32).at[flat_mesh].add(mesh_slope.reshape(-1, LATENT))
    mesh_grad = upstream + times_transpose(query_grad.astype(jnp.bfloat16), w_proc)
    mesh_grad = mesh_grad + times_transpose(receiver_grad.astype(jnp.bfloat16), w_recv)
    grad_blocks = (mesh_grad / math.sqrt(ENC_EDGES)).reshape(blocks, MESH_DEV, LATENT)

    def backward(carry, triple):
        projected_grad, edge_total = carry
        indices, dest, upper = triple
        before, active, normed, spread = encoder_edges(projected, indices, dest, w_edge)
        incoming = jnp.broadcast_to(upper[:, None, :], (MESH_DEV, ENC_EDGES, LATENT)).reshape(-1, LATENT)
        centred_grad = incoming - lax.optimization_barrier(jnp.mean(incoming, axis=-1, keepdims=True))
        centred_grad = centred_grad - normed * lax.optimization_barrier(jnp.mean(incoming * normed, axis=-1, keepdims=True))
        norm_grad = (centred_grad / spread).astype(jnp.bfloat16)
        edge_total = edge_total + first_contract(active, norm_grad)
        before_grad = times_transpose(norm_grad, w_edge) * silu_slope(before)
        projected_grad = projected_grad.at[indices].add(before_grad)
        return ((projected_grad, edge_total), None)
    start = (jnp.zeros((GRID, LATENT), jnp.float32), jnp.zeros((LATENT, LATENT), jnp.float32))
    (projected_grad, edge_grad), _ = lax.scan(backward, start, (index_blocks, dest_blocks, grad_blocks))
    projected_low = projected_grad.astype(jnp.bfloat16)
    src_grad = first_contract(hidden_grid, projected_low)
    hidden_grad = (times_transpose(projected_low, w_src) * silu_slope(hidden_pre)).astype(jnp.bfloat16)
    grid_grad = times_transpose(w_embed, hidden_grad)
    return (mesh_out, grid_grad, src_grad, edge_grad)
```

```python
import functools
import math

import jax
import jax.numpy as jnp
from jax import lax
from jax.experimental import pallas as pl
from jax.experimental.pallas import tpu as pltpu
from jax.sharding import Mesh
from jax.sharding import PartitionSpec as P

BAND = ("band_0", "band_1", "band_2")
ALL = ("band_0", "band_1", "band_2", "sub")
NEAR = ("band_1", "band_2", "sub")
FAR = "band_0"

EPSILON = 1e-05
BF = jnp.bfloat16
F32 = jnp.float32
VMEM = 48 * 1024 * 1024


def sigmoid(value):
    return 0.5 * jnp.tanh(0.5 * value) + 0.5


def silu_and_slope(value):
    sigma = sigmoid(value)
    active = value * sigma
    return active, sigma + active * (1.0 - sigma)


def dot(left, right):
    return jnp.dot(left, right, preferred_element_type=F32)


def dot_t(left, right):
    return lax.dot_general(left, right, (((1,), (1,)), ((), ())), preferred_element_type=F32)


def t_dot(left, right):
    return lax.dot_general(left, right, (((0,), (0,)), ((), ())), preferred_element_type=F32)


def selection(column, width, base):
    lanes = lax.broadcasted_iota(jnp.int32, (column.shape[0], width), 1)
    return jnp.where(column - base == lanes, 1.0, 0.0).astype(BF)


def selection_t(row, height):
    lines = lax.broadcasted_iota(jnp.int32, (height, row.shape[1]), 0)
    return jnp.where(row == lines, 1.0, 0.0).astype(BF)


def padded_rows(ref, scratch):
    rows = ref.shape[0]
    scratch[...] = jnp.zeros_like(scratch)
    scratch[:rows, :] = ref[...]
    return scratch[...]


def forward_kernel(
    scale,
    index_ref, low_ref, band_ref, high_ref, mesh_ref, embed_ref, src_ref, dst_ref, edge_ref,
    hidden_ref, hslope_ref, active_ref, bslope_ref, normed_ref, inverse_ref, mesh_out_ref,
    table, pad, embed, dest, total,
):
    step = pl.program_id(0)
    nodes = low_ref.shape[1]
    blocks = band_ref.shape[0] + 2
    rows = mesh_ref.shape[0]

    @pl.when(step == 0)
    def _():
        for block in range(blocks):
            if block == 0:
                source = low_ref
            elif block == blocks - 1:
                source = high_ref
            else:
                source = band_ref.at[block - 1]
            table[block * nodes : (block + 1) * nodes, :] = padded_rows(source, pad).T
        embed[...] = padded_rows(embed_ref, pad)
        dest[...] = dot(mesh_ref[...], dst_ref[...])
        total[...] = jnp.zeros_like(total)

    column = index_ref[...]
    edges = column.shape[0]
    picked = jnp.zeros((edges, table.shape[1]), F32)
    for block in range(blocks):
        part = table[block * nodes : (block + 1) * nodes, :]
        picked += dot(selection(column, nodes, block * nodes), part)
    hidden, hslope = silu_and_slope(dot(picked.astype(BF), embed[...]))
    hidden = hidden.astype(BF)
    hidden_ref[...] = hidden
    hslope_ref[...] = hslope.astype(BF)
    projected = dot(hidden, src_ref[...]).astype(BF).astype(F32)
    before = (projected.reshape(-1, rows, projected.shape[1]) + dest[...][None]).reshape(projected.shape)
    active, bslope = silu_and_slope(before)
    active = active.astype(BF)
    active_ref[...] = active
    bslope_ref[...] = bslope.astype(BF)
    out = dot(active, edge_ref[...])
    centred = out - jnp.mean(out, axis=-1, keepdims=True)
    inverse = lax.rsqrt(jnp.mean(centred * centred, axis=-1, keepdims=True) + EPSILON)
    normed = centred * inverse
    normed_ref[...] = normed.astype(BF)
    inverse_ref[...] = inverse
    total[...] += jnp.sum(normed.reshape(-1, rows, normed.shape[1]), axis=0)

    @pl.when(step == pl.num_programs(0) - 1)
    def _():
        mesh_out_ref[...] = (mesh_ref[...].astype(F32) + total[...] * scale).astype(BF)


def mesh_kernel(
    mesh_scale, scale,
    own_ref, band_ref, far_ref, edge_ref, cot_ref, cots_ref, index_ref, column_ref, row_ref,
    proc_ref, recv_ref, active_ref, normed_ref, inverse_ref,
    out_ref, ngrad_ref, wgrad_ref,
    receiver_all, query_grad, upper_ref, total,
):
    step = pl.program_id(0)
    own = own_ref[...]
    rows, latent = own_ref.shape

    @pl.when(step == 0)
    def _():
        proc = proc_ref[...]
        recv = recv_ref[...]
        window = jnp.concatenate([band_ref[...], far_ref[...], edge_ref[...]], axis=0)
        query = dot(window, proc).astype(BF)
        receiver = dot(own, recv)
        count = index_ref.shape[0] // rows
        sent = dot(selection(index_ref[...], window.shape[0], 0), query)
        before = sent.reshape(count, rows, latent) + receiver[None]
        active, slope = silu_and_slope(before)
        summed = jnp.sum(active, axis=0)
        out_ref[...] = (own.astype(F32) + summed * mesh_scale).astype(BF)
        upstream = cot_ref[...].astype(F32)
        receiver_grad = upstream * mesh_scale * jnp.sum(slope, axis=0)

        wide = band_ref.shape[0]
        receiver_all[:wide, :] = dot(band_ref[...], recv)
        receiver_all[wide:, :] = dot(far_ref[...], recv)
        own_query = dot(own, proc).astype(BF)
        query_grad[...] = jnp.zeros_like(query_grad)

        def one(j, carry):
            value = dot(selection(column_ref[j], rows, 0), own_query) + receiver_all[...]
            _, slopes = silu_and_slope(value)
            slopes = (cots_ref[...].astype(F32) * mesh_scale * slopes).astype(BF)
            query_grad[...] += dot(selection_t(row_ref[j], rows), slopes)
            return carry

        lax.fori_loop(0, count, one, 0)
        mesh_grad = upstream + dot_t(query_grad[...].astype(BF), proc)
        mesh_grad = mesh_grad + dot_t(receiver_grad.astype(BF), recv)
        upper_ref[...] = mesh_grad * scale
        total[...] = jnp.zeros_like(total)

    upper = upper_ref[...]
    centred = upper - jnp.mean(upper, axis=-1, keepdims=True)
    normed = normed_ref[...].astype(F32).reshape(-1, rows, latent)
    inverse = inverse_ref[...].reshape(-1, rows, 1)
    along = jnp.mean(upper[None] * normed, axis=-1, keepdims=True)
    ngrad = ((centred[None] - normed * along) * inverse).reshape(-1, latent).astype(BF)
    ngrad_ref[...] = ngrad
    total[...] += t_dot(active_ref[...], ngrad)

    @pl.when(step == pl.num_programs(0) - 1)
    def _():
        wgrad_ref[...] = total[...].astype(BF)


def source_kernel(
    edge_ref, ngrad_ref, bslope_ref, hidden_ref,
    bgrad_ref, wgrad_ref,
    total,
):
    step = pl.program_id(0)

    @pl.when(step == 0)
    def _():
        total[...] = jnp.zeros_like(total)

    bgrad = (dot_t(ngrad_ref[...], edge_ref[...]) * bslope_ref[...].astype(F32)).astype(BF)
    bgrad_ref[...] = bgrad
    total[...] += t_dot(hidden_ref[...], bgrad)

    @pl.when(step == pl.num_programs(0) - 1)
    def _():
        wgrad_ref[...] = total[...].astype(BF)


def grid_kernel(
    index_ref, src_ref, embed_ref, bgrad_ref, hslope_ref,
    low_ref, band_ref, high_ref,
    pad, total,
):
    step = pl.program_id(0)
    channels, nodes = low_ref.shape
    blocks = band_ref.shape[0] + 2

    @pl.when(step == 0)
    def _():
        padded_rows(embed_ref, pad)
        total[...] = jnp.zeros_like(total)

    hgrad = (dot_t(bgrad_ref[...], src_ref[...]) * hslope_ref[...].astype(F32)).astype(BF)
    ggrad = dot_t(pad[...], hgrad).astype(BF)
    column = index_ref[...]
    for block in range(blocks):
        total[block] += dot(ggrad, selection(column, nodes, block * nodes))

    @pl.when(step == pl.num_programs(0) - 1)
    def _():
        for block in range(blocks):
            done = total[block][:channels].astype(BF)
            if block == 0:
                low_ref[...] = done
            elif block == blocks - 1:
                high_ref[...] = done
            else:
                band_ref[block - 1] = done


def whole(shape):
    return pl.BlockSpec(shape, lambda i, n=len(shape): (0,) * n)


def tiled(edges, width):
    return pl.BlockSpec((edges, width), lambda i: (i, 0))


def params():
    return pltpu.CompilerParams(dimension_semantics=("arbitrary",), vmem_limit_bytes=VMEM)


def from_everyone(shard, axis):
    devices = lax.axis_size(axis)
    return lax.all_to_all(
        jnp.broadcast_to(shard[None], (devices, *shard.shape)), axis, 0, 0, tiled=True
    )


def bands_up(value):
    count = lax.axis_size(BAND)
    return lax.ppermute(value, BAND, [(i, i + 1) for i in range(count - 1)])


def bands_down(value):
    count = lax.axis_size(BAND)
    return lax.ppermute(value, BAND, [(i + 1, i) for i in range(count - 1)])


def outwards(value, near):
    bands, subs = lax.axis_size(BAND), lax.axis_size("sub")
    pairs = []
    for band in range(bands):
        for sub in range(subs):
            up = (sub < subs // 2) == near
            to = band + 1 if up else band - 1
            if 0 <= to < bands:
                pairs.append((band * subs + sub, to * subs + sub))
    return lax.ppermute(value, ALL, pairs)


def weight_sum(part):
    near = lax.axis_size(NEAR)
    rows, width = part.shape
    parts = lax.all_to_all(part.reshape(near, rows // near, width), NEAR, 0, 0, tiled=True)
    mine = jnp.sum(parts.astype(F32), axis=0).astype(BF)
    mine = jnp.sum(from_everyone(mine, FAR).astype(F32), axis=0).astype(BF)
    return from_everyone(mine, NEAR).reshape(rows, width).astype(F32)


def body(
    grid_x, mesh_in, w_embed, w_src, w_dst, w_edge, w_proc, w_recv, g2m_src, mesh_src, cotangent
):
    channels, nodes = grid_x.shape
    latent = w_src.shape[0]
    rows, enc_count = g2m_src.shape
    mesh_count = mesh_src.shape[1]
    subs = lax.axis_size("sub")
    band = lax.axis_index(BAND)
    sub = lax.axis_index("sub")
    wide = -(-channels // 128) * 128
    blocks = subs + 2
    edges = rows * enc_count
    steps = 4
    tile = edges // steps
    scale = 1.0 / math.sqrt(enc_count)
    mesh_scale = 1.0 / math.sqrt(mesh_count)

    grid_band = lax.all_gather(grid_x, "sub", axis=0)
    grid_low = bands_up(grid_band[subs - 1])
    grid_high = bands_down(grid_band[0])
    grid_local = (g2m_src - (band * (nodes * subs) - nodes)).T.reshape(edges, 1)

    band_cot = from_everyone(cotangent, "sub").reshape(subs * rows, latent)
    band_src = from_everyone(mesh_src, "sub").reshape(subs * rows, mesh_count)
    far_cot = outwards(band_cot, True)
    far_src = outwards(band_src, True)
    all_cot = jnp.concatenate([band_cot, far_cot])
    own_base = (band * subs + sub) * rows
    all_src = (jnp.concatenate([band_src, far_src]) - own_base).T
    column_src = all_src[:, :, None]
    row_src = all_src[:, None, :]
    lower = sub < subs // 2
    local = mesh_src - band * (rows * subs)
    width = rows * subs
    below = jnp.where(lower, local + 2 * width, local + rows + 2 * width)
    above = jnp.where(lower, local - width + 2 * width, local)
    place = jnp.where(local < 0, below, jnp.where(local >= width, above, local))
    place = place.T.reshape(rows * mesh_count, 1)

    hidden, hslope, active, bslope, normed, inverse, hidden_mesh = pl.pallas_call(
        functools.partial(forward_kernel, scale),
        grid=(steps,),
        in_specs=[
            tiled(tile, 1),
            whole((channels, nodes)),
            whole((subs, channels, nodes)),
            whole((channels, nodes)),
            whole((rows, latent)),
            whole((channels, latent)),
            whole((latent, latent)),
            whole((latent, latent)),
            whole((latent, latent)),
        ],
        out_specs=[tiled(tile, latent)] * 5 + [tiled(tile, 1), whole((rows, latent))],
        out_shape=[jax.ShapeDtypeStruct((edges, latent), BF)] * 5
        + [jax.ShapeDtypeStruct((edges, 1), F32), jax.ShapeDtypeStruct((rows, latent), BF)],
        scratch_shapes=[
            pltpu.VMEM((blocks * nodes, wide), BF),
            pltpu.VMEM((wide, nodes), BF),
            pltpu.VMEM((wide, latent), BF),
            pltpu.VMEM((rows, latent), F32),
            pltpu.VMEM((rows, latent), F32),
        ],
        compiler_params=params(),
        name="encode",
    )(grid_local, grid_low, grid_band, grid_high, mesh_in, w_embed, w_src, w_dst, w_edge)

    mesh_band = from_everyone(hidden_mesh, "sub").reshape(subs * rows, latent)
    mesh_far = outwards(mesh_band, True)
    border = jnp.where(lower, mesh_band[:rows], mesh_band[-rows:])
    mesh_edge = outwards(border, False)

    mesh_out, ngrad, edge_part = pl.pallas_call(
        functools.partial(mesh_kernel, mesh_scale, scale),
        grid=(steps,),
        in_specs=[
            whole((rows, latent)),
            whole((width, latent)),
            whole((width, latent)),
            whole((rows, latent)),
            whole((rows, latent)),
            whole((2 * width, latent)),
            whole((rows * mesh_count, 1)),
            whole((mesh_count, 2 * width, 1)),
            whole((mesh_count, 1, 2 * width)),
            whole((latent, latent)),
            whole((latent, latent)),
            tiled(tile, latent),
            tiled(tile, latent),
            tiled(tile, 1),
        ],
        out_specs=[whole((rows, latent)), tiled(tile, latent), whole((latent, latent))],
        out_shape=[
            jax.ShapeDtypeStruct((rows, latent), BF),
            jax.ShapeDtypeStruct((edges, latent), BF),
            jax.ShapeDtypeStruct((latent, latent), BF),
        ],
        scratch_shapes=[
            pltpu.VMEM((2 * width, latent), F32),
            pltpu.VMEM((rows, latent), F32),
            pltpu.VMEM((rows, latent), F32),
            pltpu.VMEM((latent, latent), F32),
        ],
        compiler_params=params(),
        name="process",
    )(
        hidden_mesh, mesh_band, mesh_far, mesh_edge, cotangent, all_cot, place, column_src, row_src,
        w_proc, w_recv, active, normed, inverse,
    )

    bgrad, src_part = pl.pallas_call(
        source_kernel,
        grid=(steps,),
        in_specs=[whole((latent, latent))] + [tiled(tile, latent)] * 3,
        out_specs=[tiled(tile, latent), whole((latent, latent))],
        out_shape=[
            jax.ShapeDtypeStruct((edges, latent), BF),
            jax.ShapeDtypeStruct((latent, latent), BF),
        ],
        scratch_shapes=[pltpu.VMEM((latent, latent), F32)],
        compiler_params=params(),
        name="source",
    )(w_edge, ngrad, bslope, hidden)

    part_low, part_band, part_high = pl.pallas_call(
        grid_kernel,
        grid=(steps,),
        in_specs=[
            tiled(tile, 1),
            whole((latent, latent)),
            whole((channels, latent)),
            tiled(tile, latent),
            tiled(tile, latent),
        ],
        out_specs=[
            whole((channels, nodes)),
            whole((subs, channels, nodes)),
            whole((channels, nodes)),
        ],
        out_shape=[
            jax.ShapeDtypeStruct((channels, nodes), BF),
            jax.ShapeDtypeStruct((subs, channels, nodes), BF),
            jax.ShapeDtypeStruct((channels, nodes), BF),
        ],
        scratch_shapes=[pltpu.VMEM((wide, latent), BF), pltpu.VMEM((blocks, wide, nodes), F32)],
        compiler_params=params(),
        name="channels",
    )(grid_local, w_src, w_embed, bgrad, hslope)

    edge_grad = weight_sum(edge_part)
    src_grad = weight_sum(src_part)
    from_above = bands_down(part_low)
    from_below = bands_up(part_high)
    first = (part_band[0].astype(F32) + from_below.astype(F32)).astype(BF)
    last = (part_band[subs - 1].astype(F32) + from_above.astype(F32)).astype(BF)
    part = jnp.concatenate([first[None], part_band[1 : subs - 1], last[None]])
    arrived = lax.all_to_all(part, "sub", 0, 0, tiled=True)
    grid_grad = jnp.sum(arrived.astype(F32), axis=0)
    return (mesh_out, grid_grad, src_grad, edge_grad)


def solution(mesh):
    torus = Mesh(mesh.devices.reshape(8, 4, 2, mesh.shape["sub"]), ALL)
    return jax.shard_map(
        body,
        mesh=torus,
        in_specs=(
            P(None, ALL),
            P(ALL, None),
            P(),
            P(),
            P(),
            P(),
            P(),
            P(),
            P(ALL, None),
            P(ALL, None),
            P(ALL, None),
        ),
        out_specs=(P(ALL, None), P(None, ALL), P(), P()),
        check_vma=False,
    )
```

```python
import functools
import math

import jax
import jax.numpy as jnp
from jax import lax
from jax.experimental import pallas as pl
from jax.experimental.pallas import tpu as pltpu
from jax.sharding import Mesh
from jax.sharding import PartitionSpec as P

BAND = ("band_0", "band_1", "band_2")
ALL = ("band_0", "band_1", "band_2", "sub")
NEAR = ("band_1", "band_2", "sub")
FAR = "band_0"
SUBS = 4

EPSILON = 1e-05
BF = jnp.bfloat16
F32 = jnp.float32
VMEM = 60 * 1024 * 1024


def sigmoid(value):
    return 0.5 * jnp.tanh(0.5 * value) + 0.5


def silu_and_slope(value):
    sigma = sigmoid(value)
    active = value * sigma
    return active, sigma + active * (1.0 - sigma)


def dot(left, right):
    return jnp.dot(left, right, preferred_element_type=F32)


def dot_t(left, right):
    return lax.dot_general(left, right, (((1,), (1,)), ((), ())), preferred_element_type=F32)


def t_dot(left, right):
    return lax.dot_general(left, right, (((0,), (0,)), ((), ())), preferred_element_type=F32)


def selection(column, width):
    lanes = lax.broadcasted_iota(jnp.int32, (column.shape[0], width), 1)
    return jnp.where(column == lanes, 1.0, 0.0).astype(BF)


def selection_t(row, height):
    lines = lax.broadcasted_iota(jnp.int32, (height, row.shape[1]), 0)
    return jnp.where(row == lines, 1.0, 0.0).astype(BF)


def padded_rows(ref, scratch):
    rows = ref.shape[0]
    scratch[...] = jnp.zeros_like(scratch)
    scratch[:rows, :] = ref[...]
    return scratch[...]


def forward_kernel(
    scale,
    sub_ref, index_ref, own_ref, one_ref, two_ref, three_ref, low_ref, high_ref,
    mesh_ref, embed_ref, src_ref, dst_ref, edge_ref,
    hidden_ref, hslope_ref, active_ref, bslope_ref, normed_ref, inverse_ref, mesh_out_ref,
    table, pad, embed, dest, total,
):
    step = pl.program_id(0)
    sources = (own_ref, one_ref, two_ref, three_ref, low_ref, high_ref)
    nodes = low_ref.shape[1]
    rows = mesh_ref.shape[0]
    sub = sub_ref[0]
    bases = [(lax.rem(sub + SUBS - k, SUBS) + 1) * nodes for k in range(SUBS)]
    bases += [0, (SUBS + 1) * nodes]

    @pl.when(step == 0)
    def _():
        for block, source in enumerate(sources):
            table[block * nodes : (block + 1) * nodes, :] = padded_rows(source, pad).T
        embed[...] = padded_rows(embed_ref, pad)
        dest[...] = dot(mesh_ref[...], dst_ref[...])
        total[...] = jnp.zeros_like(total)

    column = index_ref[...]
    edges = column.shape[0]
    picked = jnp.zeros((edges, table.shape[1]), F32)
    for block, base in enumerate(bases):
        part = table[block * nodes : (block + 1) * nodes, :]
        picked += dot(selection(column - base, nodes), part)
    hidden, hslope = silu_and_slope(dot(picked.astype(BF), embed[...]))
    hidden = hidden.astype(BF)
    hidden_ref[...] = hidden
    hslope_ref[...] = hslope.astype(BF)
    projected = dot(hidden, src_ref[...]).astype(BF).astype(F32)
    before = (projected.reshape(-1, rows, projected.shape[1]) + dest[...][None]).reshape(projected.shape)
    active, bslope = silu_and_slope(before)
    active = active.astype(BF)
    active_ref[...] = active
    bslope_ref[...] = bslope.astype(BF)
    out = dot(active, edge_ref[...])
    centred = out - jnp.mean(out, axis=-1, keepdims=True)
    inverse = lax.rsqrt(jnp.mean(centred * centred, axis=-1, keepdims=True) + EPSILON)
    normed = centred * inverse
    normed_ref[...] = normed.astype(BF)
    inverse_ref[...] = inverse
    total[...] += jnp.sum(normed.reshape(-1, rows, normed.shape[1]), axis=0)

    @pl.when(step == pl.num_programs(0) - 1)
    def _():
        mesh_out_ref[...] = (mesh_ref[...].astype(F32) + total[...] * scale).astype(BF)


def mesh_kernel(
    mesh_scale, scale, count,
    sub_ref, band_ref, far_ref, side_ref, pay_ref, far_pay_ref, proc_ref, recv_ref, edge_ref,
    active_ref, normed_ref, inverse_ref, bslope_ref, hidden_ref,
    out_ref, bgrad_ref, wgrad_ref,
    receiver_all, cots, columns, lines, query_grad, upper_ref, edge_total, src_total,
):
    step = pl.program_id(0)
    rows, latent = side_ref.shape
    wide = band_ref.shape[0]

    @pl.when(step == 0)
    def _():
        sub = sub_ref[0]
        lower = sub < SUBS // 2
        proc = proc_ref[...]
        recv = recv_ref[...]
        own = band_ref[:rows, :]
        window = jnp.concatenate([band_ref[...], far_ref[...], side_ref[...]], axis=0)
        query = dot(window, proc).astype(BF)
        receiver_all[:wide, :] = dot(band_ref[...], recv)
        receiver_all[wide:, :] = dot(far_ref[...], recv)
        receiver = receiver_all[:rows, :]

        tail = pay_ref[:, latent:].astype(F32).astype(jnp.int32)
        far_tail = far_pay_ref[:, latent:].astype(F32).astype(jnp.int32)
        turn = tail.shape[1] // 2
        block, line = tail[:, :turn], tail[:, turn:]
        far_block, far_line = far_tail[:, :turn], far_tail[:, turn:]
        far_wanted = jnp.where(lower, SUBS + 1 + sub, sub - SUBS + 1)
        columns[:wide, :turn] = (block - (sub + 1)) * rows + line
        columns[wide:, :turn] = (far_block - far_wanted) * rows + far_line
        own_block, own_line = block[:rows], line[:rows]
        inside = lax.rem(sub + SUBS + 1 - own_block, SUBS) * rows
        below = jnp.where(lower, wide + lax.rem(sub + 1, SUBS) * rows, 2 * wide)
        above = jnp.where(lower, 2 * wide, wide + sub * rows)
        place = jnp.where(own_block == 0, below, jnp.where(own_block == SUBS + 1, above, inside))
        place = place + own_line
        columns[:, turn:] = jnp.zeros_like(columns[:, turn:])
        lines[...] = columns[...].T
        cots[:wide, :] = pay_ref[:, :latent].astype(F32) * mesh_scale
        cots[wide:, :] = far_pay_ref[:, :latent].astype(F32) * mesh_scale

        summed = jnp.zeros((rows, latent), F32)
        slopes = jnp.zeros((rows, latent), F32)
        for j in range(count):
            sent = dot(selection(place[:, j : j + 1], window.shape[0]), query)
            active, slope = silu_and_slope(sent + receiver)
            summed += active
            slopes += slope
        out_ref[...] = (own.astype(F32) + summed * mesh_scale).astype(BF)
        receiver_grad = cots[:rows, :] * slopes

        own_query = query[:rows]
        query_grad[...] = jnp.zeros_like(query_grad)
        lanes = lax.broadcasted_iota(jnp.int32, columns.shape, 1)

        def one(j, carry):
            column = jnp.sum(jnp.where(lanes == j, columns[...], 0), axis=1, keepdims=True)
            value = dot(selection(column, rows), own_query) + receiver_all[...]
            _, slopes = silu_and_slope(value)
            slopes = (cots[...] * slopes).astype(BF)
            query_grad[...] += dot(selection_t(lines[pl.ds(j, 1), :], rows), slopes)
            return carry

        lax.fori_loop(0, count, one, 0)
        mesh_grad = pay_ref[:rows, :latent].astype(F32) + dot_t(query_grad[...].astype(BF), proc)
        mesh_grad = mesh_grad + dot_t(receiver_grad.astype(BF), recv)
        upper_ref[...] = mesh_grad * scale
        edge_total[...] = jnp.zeros_like(edge_total)
        src_total[...] = jnp.zeros_like(src_total)

    upper = upper_ref[...]
    centred = upper - jnp.mean(upper, axis=-1, keepdims=True)
    normed = normed_ref[...].astype(F32).reshape(-1, rows, latent)
    inverse = inverse_ref[...].reshape(-1, rows, 1)
    along = jnp.mean(upper[None] * normed, axis=-1, keepdims=True)
    ngrad = ((centred[None] - normed * along) * inverse).reshape(-1, latent).astype(BF)
    edge_total[...] += t_dot(active_ref[...], ngrad)
    bgrad = (dot_t(ngrad, edge_ref[...]) * bslope_ref[...].astype(F32)).astype(BF)
    bgrad_ref[...] = bgrad
    src_total[...] += t_dot(hidden_ref[...], bgrad)

    @pl.when(step == pl.num_programs(0) - 1)
    def _():
        wgrad_ref[:latent, :] = edge_total[...].astype(BF)
        wgrad_ref[latent:, :] = src_total[...].astype(BF)


def grid_kernel(
    sub_ref, index_ref, src_ref, embed_ref, bgrad_ref, hslope_ref,
    own_ref, one_ref, two_ref, three_ref, low_ref, high_ref,
    pad, total,
):
    step = pl.program_id(0)
    channels, nodes = low_ref.shape
    targets = (own_ref, one_ref, two_ref, three_ref, low_ref, high_ref)
    sub = sub_ref[0]
    bases = [(lax.rem(sub + k, SUBS) + 1) * nodes for k in range(SUBS)]
    bases += [0, (SUBS + 1) * nodes]

    @pl.when(step == 0)
    def _():
        padded_rows(embed_ref, pad)
        total[...] = jnp.zeros_like(total)

    hgrad = (dot_t(bgrad_ref[...], src_ref[...]) * hslope_ref[...].astype(F32)).astype(BF)
    ggrad = dot_t(pad[...], hgrad).astype(BF)
    column = index_ref[...]
    for block, base in enumerate(bases):
        total[block] += dot(ggrad, selection(column - base, nodes))

    @pl.when(step == pl.num_programs(0) - 1)
    def _():
        for block, target in enumerate(targets):
            target[...] = total[block][:channels].astype(BF)


def whole(shape):
    return pl.BlockSpec(shape, lambda i, n=len(shape): (0,) * n)


def tiled(edges, width):
    return pl.BlockSpec((edges, width), lambda i: (i, 0))


def scalar():
    return pl.BlockSpec(memory_space=pltpu.SMEM)


def params():
    return pltpu.CompilerParams(dimension_semantics=("arbitrary",), vmem_limit_bytes=VMEM)


def from_everyone(shard, axis):
    devices = lax.axis_size(axis)
    return lax.all_to_all(
        jnp.broadcast_to(shard[None], (devices, *shard.shape)), axis, 0, 0, tiled=True
    )


def bands_up(value):
    count = lax.axis_size(BAND)
    return lax.ppermute(value, BAND, [(i, i + 1) for i in range(count - 1)])


def bands_down(value):
    count = lax.axis_size(BAND)
    return lax.ppermute(value, BAND, [(i + 1, i) for i in range(count - 1)])


def outwards(value, near):
    bands, subs = lax.axis_size(BAND), lax.axis_size("sub")
    pairs = []
    for band in range(bands):
        for sub in range(subs):
            up = (sub < subs // 2) == near
            to = band + 1 if up else band - 1
            if 0 <= to < bands:
                pairs.append((band * subs + sub, to * subs + sub))
    return lax.ppermute(value, ALL, pairs)


def along_sub(value, steps):
    count = lax.axis_size("sub")
    return lax.ppermute(value, "sub", [(i, (i + steps) % count) for i in range(count)])


def weight_sum(part):
    near = lax.axis_size(NEAR)
    rows, width = part.shape
    parts = lax.all_to_all(part.reshape(near, rows // near, width), NEAR, 0, 0, tiled=True)
    mine = jnp.sum(parts.astype(F32), axis=0).astype(BF)
    mine = jnp.sum(from_everyone(mine, FAR).astype(F32), axis=0).astype(BF)
    return from_everyone(mine, NEAR).reshape(rows, width)


def body(
    grid_x, mesh_in, w_embed, w_src, w_dst, w_edge, w_proc, w_recv, g2m_src, mesh_src, cotangent
):
    channels, nodes = grid_x.shape
    latent = w_src.shape[0]
    rows, enc_count = g2m_src.shape
    mesh_count = mesh_src.shape[1]
    band = lax.axis_index(BAND)
    sub = lax.axis_index("sub")
    sub_scalar = sub.astype(jnp.int32).reshape(1)
    wide = -(-channels // 128) * 128
    edges = rows * enc_count
    steps = 4
    tile = edges // steps
    width = SUBS * rows
    scale = 1.0 / math.sqrt(enc_count)
    mesh_scale = 1.0 / math.sqrt(mesh_count)

    grid = [grid_x] + [along_sub(grid_x, k) for k in range(1, SUBS)]
    last = lax.select_n(lax.rem(sub + 1, SUBS), *grid)
    first = lax.select_n(sub, *grid)
    grid_low = bands_up(last)
    grid_high = bands_down(first)
    grid_local = (g2m_src - (band * (nodes * SUBS) - nodes)).T.reshape(edges, 1)

    place = mesh_src - (band * width - rows)
    half = 64
    spare = jnp.zeros((rows, half - mesh_count), BF)
    pay = jnp.concatenate(
        [cotangent, (place // rows).astype(BF), spare, (place % rows).astype(BF), spare], axis=1
    )
    pay, _ = lax.optimization_barrier((pay, last))
    pay = jnp.concatenate([pay] + [along_sub(pay, k) for k in range(1, SUBS)])
    far_pay = outwards(pay, True)

    hidden, hslope, active, bslope, normed, inverse, hidden_mesh = pl.pallas_call(
        functools.partial(forward_kernel, scale),
        grid=(steps,),
        in_specs=[scalar(), tiled(tile, 1)]
        + [whole((channels, nodes))] * (SUBS + 2)
        + [
            whole((rows, latent)),
            whole((channels, latent)),
            whole((latent, latent)),
            whole((latent, latent)),
            whole((latent, latent)),
        ],
        out_specs=[tiled(tile, latent)] * 5 + [tiled(tile, 1), whole((rows, latent))],
        out_shape=[jax.ShapeDtypeStruct((edges, latent), BF)] * 5
        + [jax.ShapeDtypeStruct((edges, 1), F32), jax.ShapeDtypeStruct((rows, latent), BF)],
        scratch_shapes=[
            pltpu.VMEM(((SUBS + 2) * nodes, wide), BF),
            pltpu.VMEM((wide, nodes), BF),
            pltpu.VMEM((wide, latent), BF),
            pltpu.VMEM((rows, latent), F32),
            pltpu.VMEM((rows, latent), F32),
        ],
        compiler_params=params(),
        name="encode",
    )(sub_scalar, grid_local, *grid, grid_low, grid_high, mesh_in, w_embed, w_src, w_dst, w_edge)

    mesh_band = jnp.concatenate([hidden_mesh] + [along_sub(hidden_mesh, k) for k in range(1, SUBS)])
    mesh_far = outwards(mesh_band, True)
    at = jnp.where(sub < SUBS // 2, sub, lax.rem(sub + 1, SUBS)) * rows
    mesh_side = outwards(lax.dynamic_slice_in_dim(mesh_band, at, rows), False)

    mesh_out, bgrad, part = pl.pallas_call(
        functools.partial(mesh_kernel, mesh_scale, scale, mesh_count),
        grid=(steps,),
        in_specs=[
            scalar(),
            whole((width, latent)),
            whole((width, latent)),
            whole((rows, latent)),
            whole((width, latent + 2 * half)),
            whole((width, latent + 2 * half)),
            whole((latent, latent)),
            whole((latent, latent)),
            whole((latent, latent)),
            tiled(tile, latent),
            tiled(tile, latent),
            tiled(tile, 1),
            tiled(tile, latent),
            tiled(tile, latent),
        ],
        out_specs=[whole((rows, latent)), tiled(tile, latent), whole((2 * latent, latent))],
        out_shape=[
            jax.ShapeDtypeStruct((rows, latent), BF),
            jax.ShapeDtypeStruct((edges, latent), BF),
            jax.ShapeDtypeStruct((2 * latent, latent), BF),
        ],
        scratch_shapes=[
            pltpu.VMEM((2 * width, latent), F32),
            pltpu.VMEM((2 * width, latent), F32),
            pltpu.VMEM((2 * width, 2 * half), jnp.int32),
            pltpu.VMEM((2 * half, 2 * width), jnp.int32),
            pltpu.VMEM((rows, latent), F32),
            pltpu.VMEM((rows, latent), F32),
            pltpu.VMEM((latent, latent), F32),
            pltpu.VMEM((latent, latent), F32),
        ],
        compiler_params=params(),
        name="process",
    )(
        sub_scalar, mesh_band, mesh_far, mesh_side, pay, far_pay, w_proc, w_recv, w_edge,
        active, normed, inverse, bslope, hidden,
    )

    *parts, part_low, part_high = pl.pallas_call(
        grid_kernel,
        grid=(steps,),
        in_specs=[
            scalar(),
            tiled(tile, 1),
            whole((latent, latent)),
            whole((channels, latent)),
            tiled(tile, latent),
            tiled(tile, latent),
        ],
        out_specs=[whole((channels, nodes))] * (SUBS + 2),
        out_shape=[jax.ShapeDtypeStruct((channels, nodes), BF)] * (SUBS + 2),
        scratch_shapes=[pltpu.VMEM((wide, latent), BF), pltpu.VMEM((SUBS + 2, wide, nodes), F32)],
        compiler_params=params(),
        name="channels",
    )(sub_scalar, grid_local, w_src, w_embed, bgrad, hslope)

    weights = weight_sum(part)
    from_above = bands_down(part_low)
    from_below = bands_up(part_high)
    arrived = None
    for k in range(SUBS):
        block = lax.rem(sub + k, SUBS)
        value = parts[k].astype(F32)
        value += jnp.where(block == 0, from_below, jnp.zeros_like(from_below)).astype(F32)
        value += jnp.where(block == SUBS - 1, from_above, jnp.zeros_like(from_above)).astype(F32)
        if k == 0:
            arrived = value
        else:
            arrived += along_sub(value.astype(BF), k).astype(F32)
    src_grad, edge_grad = weights[latent:].astype(F32), weights[:latent].astype(F32)
    return (mesh_out, arrived, src_grad, edge_grad)


def solution(mesh):
    torus = Mesh(mesh.devices.reshape(8, 4, 2, mesh.shape["sub"]), ALL)
    return jax.shard_map(
        body,
        mesh=torus,
        in_specs=(
            P(None, ALL),
            P(ALL, None),
            P(),
            P(),
            P(),
            P(),
            P(),
            P(),
            P(ALL, None),
            P(ALL, None),
            P(ALL, None),
        ),
        out_specs=(P(ALL, None), P(None, ALL), P(), P()),
        check_vma=False,
    )
```

```python
import functools
import math

import jax
import jax.numpy as jnp
from jax import lax
from jax.experimental import pallas as pl
from jax.experimental.pallas import tpu as pltpu
from jax.sharding import Mesh
from jax.sharding import PartitionSpec as P

BAND = ("band_0", "band_1", "band_2")
ALL = ("band_0", "band_1", "band_2", "sub")
NEAR = ("band_1", "band_2", "sub")
FAR = "band_0"
SUBS = 4

EPSILON = 1e-05
BF = jnp.bfloat16
F32 = jnp.float32
VMEM = 60 * 1024 * 1024


def sigmoid(value):
    return 0.5 * jnp.tanh(0.5 * value) + 0.5


def silu_and_slope(value):
    sigma = sigmoid(value)
    active = value * sigma
    return active, sigma + active * (1.0 - sigma)


def dot(left, right):
    return jnp.dot(left, right, preferred_element_type=F32)


def dot_t(left, right):
    return lax.dot_general(left, right, (((1,), (1,)), ((), ())), preferred_element_type=F32)


def t_dot(left, right):
    return lax.dot_general(left, right, (((0,), (0,)), ((), ())), preferred_element_type=F32)


def selection(column, width):
    lanes = lax.broadcasted_iota(jnp.int32, (column.shape[0], width), 1)
    return jnp.where(column == lanes, 1.0, 0.0).astype(BF)


def selection_t(row, height):
    lines = lax.broadcasted_iota(jnp.int32, (height, row.shape[1]), 0)
    return jnp.where(row == lines, 1.0, 0.0).astype(BF)


def padded_rows(ref, scratch):
    rows = ref.shape[0]
    scratch[...] = jnp.zeros_like(scratch)
    scratch[:rows, :] = ref[...]
    return scratch[...]


def forward_kernel(
    scale,
    sub_ref, index_ref, own_ref, one_ref, two_ref, three_ref, low_ref, high_ref,
    mesh_ref, embed_ref, src_ref, dst_ref, edge_ref,
    hidden_ref, hslope_ref, active_ref, bslope_ref, normed_ref, inverse_ref, mesh_out_ref,
    table, pad, embed, dest, total,
):
    step = pl.program_id(0)
    sources = (own_ref, one_ref, two_ref, three_ref, low_ref, high_ref)
    nodes = low_ref.shape[1]
    rows = mesh_ref.shape[0]
    sub = sub_ref[0]
    bases = [(lax.rem(sub + SUBS - k, SUBS) + 1) * nodes for k in range(SUBS)]
    bases += [0, (SUBS + 1) * nodes]

    @pl.when(step == 0)
    def _():
        for block, source in enumerate(sources):
            table[block * nodes : (block + 1) * nodes, :] = padded_rows(source, pad).T
        embed[...] = padded_rows(embed_ref, pad)
        dest[...] = dot(mesh_ref[...], dst_ref[...])
        total[...] = jnp.zeros_like(total)

    column = index_ref[...]
    edges = column.shape[0]
    picked = jnp.zeros((edges, table.shape[1]), F32)
    for block, base in enumerate(bases):
        part = table[block * nodes : (block + 1) * nodes, :]
        picked += dot(selection(column - base, nodes), part)
    hidden, hslope = silu_and_slope(dot(picked.astype(BF), embed[...]))
    hidden = hidden.astype(BF)
    hidden_ref[...] = hidden
    hslope_ref[...] = hslope.astype(BF)
    projected = dot(hidden, src_ref[...]).astype(BF).astype(F32)
    before = (projected.reshape(-1, rows, projected.shape[1]) + dest[...][None]).reshape(projected.shape)
    active, bslope = silu_and_slope(before)
    active = active.astype(BF)
    active_ref[...] = active
    bslope_ref[...] = bslope.astype(BF)
    out = dot(active, edge_ref[...])
    centred = out - jnp.mean(out, axis=-1, keepdims=True)
    inverse = lax.rsqrt(jnp.mean(centred * centred, axis=-1, keepdims=True) + EPSILON)
    normed = centred * inverse
    normed_ref[...] = normed.astype(BF)
    inverse_ref[...] = inverse
    total[...] += jnp.sum(normed.reshape(-1, rows, normed.shape[1]), axis=0)

    @pl.when(step == pl.num_programs(0) - 1)
    def _():
        mesh_out_ref[...] = (mesh_ref[...].astype(F32) + total[...] * scale).astype(BF)


def mesh_kernel(
    mesh_scale, scale, count,
    sub_ref, band_ref, far_ref, side_ref, pay_ref, far_pay_ref, proc_ref, recv_ref, edge_ref,
    active_ref, normed_ref, inverse_ref, bslope_ref, hidden_ref,
    out_ref, bgrad_ref, wgrad_ref,
    receiver_all, cots, columns, lines, query_grad, upper_ref, edge_total, src_total,
):
    step = pl.program_id(0)
    rows, latent = side_ref.shape
    wide = band_ref.shape[0]

    @pl.when(step == 0)
    def _():
        sub = sub_ref[0]
        lower = sub < SUBS // 2
        proc = proc_ref[...]
        recv = recv_ref[...]
        own = band_ref[:rows, :]
        window = jnp.concatenate([band_ref[...], far_ref[...], side_ref[...]], axis=0)
        query = dot(window, proc).astype(BF)
        receiver_all[:wide, :] = dot(band_ref[...], recv)
        receiver_all[wide:, :] = dot(far_ref[...], recv)
        receiver = receiver_all[:rows, :]

        tail = pay_ref[:, latent:].astype(F32).astype(jnp.int32)
        far_tail = far_pay_ref[:, latent:].astype(F32).astype(jnp.int32)
        turn = tail.shape[1] // 2
        block, line = tail[:, :turn], tail[:, turn:]
        far_block, far_line = far_tail[:, :turn], far_tail[:, turn:]
        far_wanted = jnp.where(lower, SUBS + 1 + sub, sub - SUBS + 1)
        columns[:wide, :turn] = (block - (sub + 1)) * rows + line
        columns[wide:, :turn] = (far_block - far_wanted) * rows + far_line
        own_block, own_line = block[:rows], line[:rows]
        inside = lax.rem(sub + SUBS + 1 - own_block, SUBS) * rows
        below = jnp.where(lower, wide + lax.rem(sub + 1, SUBS) * rows, 2 * wide)
        above = jnp.where(lower, 2 * wide, wide + sub * rows)
        place = jnp.where(own_block == 0, below, jnp.where(own_block == SUBS + 1, above, inside))
        place = place + own_line
        columns[:, turn:] = jnp.zeros_like(columns[:, turn:])
        lines[...] = columns[...].T
        cots[:wide, :] = pay_ref[:, :latent].astype(F32) * mesh_scale
        cots[wide:, :] = far_pay_ref[:, :latent].astype(F32) * mesh_scale

        summed = jnp.zeros((rows, latent), F32)
        slopes = jnp.zeros((rows, latent), F32)
        for j in range(count):
            sent = dot(selection(place[:, j : j + 1], window.shape[0]), query)
            active, slope = silu_and_slope(sent + receiver)
            summed += active
            slopes += slope
        out_ref[...] = (own.astype(F32) + summed * mesh_scale).astype(BF)
        receiver_grad = cots[:rows, :] * slopes

        own_query = query[:rows]
        query_grad[...] = jnp.zeros_like(query_grad)
        lanes = lax.broadcasted_iota(jnp.int32, columns.shape, 1)

        def one(j, carry):
            column = jnp.sum(jnp.where(lanes == j, columns[...], 0), axis=1, keepdims=True)
            value = dot(selection(column, rows), own_query) + receiver_all[...]
            _, slopes = silu_and_slope(value)
            slopes = (cots[...] * slopes).astype(BF)
            query_grad[...] += dot(selection_t(lines[pl.ds(j, 1), :], rows), slopes)
            return carry

        lax.fori_loop(0, count, one, 0)
        mesh_grad = pay_ref[:rows, :latent].astype(F32) + dot_t(query_grad[...].astype(BF), proc)
        mesh_grad = mesh_grad + dot_t(receiver_grad.astype(BF), recv)
        upper_ref[...] = mesh_grad * scale
        edge_total[...] = jnp.zeros_like(edge_total)
        src_total[...] = jnp.zeros_like(src_total)

    upper = upper_ref[...]
    centred = upper - jnp.mean(upper, axis=-1, keepdims=True)
    normed = normed_ref[...].astype(F32).reshape(-1, rows, latent)
    inverse = inverse_ref[...].reshape(-1, rows, 1)
    along = jnp.mean(upper[None] * normed, axis=-1, keepdims=True)
    ngrad = ((centred[None] - normed * along) * inverse).reshape(-1, latent).astype(BF)
    edge_total[...] += t_dot(active_ref[...], ngrad)
    bgrad = (dot_t(ngrad, edge_ref[...]) * bslope_ref[...].astype(F32)).astype(BF)
    bgrad_ref[...] = bgrad
    src_total[...] += t_dot(hidden_ref[...], bgrad)

    @pl.when(step == pl.num_programs(0) - 1)
    def _():
        wgrad_ref[:latent, :] = edge_total[...].astype(BF)
        wgrad_ref[latent:, :] = src_total[...].astype(BF)


def grid_kernel(
    sub_ref, index_ref, src_ref, embed_ref, bgrad_ref, hslope_ref,
    own_ref, one_ref, two_ref, three_ref, low_ref, high_ref,
    pad, total,
):
    step = pl.program_id(0)
    channels, nodes = low_ref.shape
    targets = (own_ref, one_ref, two_ref, three_ref, low_ref, high_ref)
    sub = sub_ref[0]
    bases = [(lax.rem(sub + k, SUBS) + 1) * nodes for k in range(SUBS)]
    bases += [0, (SUBS + 1) * nodes]

    @pl.when(step == 0)
    def _():
        padded_rows(embed_ref, pad)
        total[...] = jnp.zeros_like(total)

    hgrad = (dot_t(bgrad_ref[...], src_ref[...]) * hslope_ref[...].astype(F32)).astype(BF)
    ggrad = dot_t(pad[...], hgrad).astype(BF)
    column = index_ref[...]
    for block, base in enumerate(bases):
        total[block] += dot(ggrad, selection(column - base, nodes))

    @pl.when(step == pl.num_programs(0) - 1)
    def _():
        for block, target in enumerate(targets):
            target[...] = total[block][:channels].astype(BF)


def whole(shape):
    return pl.BlockSpec(shape, lambda i, n=len(shape): (0,) * n)


def tiled(edges, width):
    return pl.BlockSpec((edges, width), lambda i: (i, 0))


def scalar():
    return pl.BlockSpec(memory_space=pltpu.SMEM)


def params():
    return pltpu.CompilerParams(dimension_semantics=("arbitrary",), vmem_limit_bytes=VMEM)


def from_everyone(shard, axis):
    devices = lax.axis_size(axis)
    return lax.all_to_all(
        jnp.broadcast_to(shard[None], (devices, *shard.shape)), axis, 0, 0, tiled=True
    )


def bands_up(value):
    count = lax.axis_size(BAND)
    return lax.ppermute(value, BAND, [(i, i + 1) for i in range(count - 1)])


def bands_down(value):
    count = lax.axis_size(BAND)
    return lax.ppermute(value, BAND, [(i + 1, i) for i in range(count - 1)])


def outwards(value, near):
    bands, subs = lax.axis_size(BAND), lax.axis_size("sub")
    pairs = []
    for band in range(bands):
        for sub in range(subs):
            up = (sub < subs // 2) == near
            to = band + 1 if up else band - 1
            if 0 <= to < bands:
                pairs.append((band * subs + sub, to * subs + sub))
    return lax.ppermute(value, ALL, pairs)


def along_sub(value, steps):
    count = lax.axis_size("sub")
    return lax.ppermute(value, "sub", [(i, (i + steps) % count) for i in range(count)])


def summed(parts):
    return jnp.sum(parts.astype(F32), axis=0).astype(BF)


def body(
    grid_x, mesh_in, w_embed, w_src, w_dst, w_edge, w_proc, w_recv, g2m_src, mesh_src, cotangent
):
    channels, nodes = grid_x.shape
    latent = w_src.shape[0]
    rows, enc_count = g2m_src.shape
    mesh_count = mesh_src.shape[1]
    band = lax.axis_index(BAND)
    sub = lax.axis_index("sub")
    sub_scalar = sub.astype(jnp.int32).reshape(1)
    wide = -(-channels // 128) * 128
    edges = rows * enc_count
    steps = 4
    tile = edges // steps
    width = SUBS * rows
    scale = 1.0 / math.sqrt(enc_count)
    mesh_scale = 1.0 / math.sqrt(mesh_count)

    grid = [grid_x] + [along_sub(grid_x, k) for k in range(1, SUBS)]
    last = lax.select_n(lax.rem(sub + 1, SUBS), *grid)
    first = lax.select_n(sub, *grid)
    grid_low = bands_up(last)
    grid_high = bands_down(first)
    grid_local = (g2m_src - (band * (nodes * SUBS) - nodes)).T.reshape(edges, 1)

    place = mesh_src - (band * width - rows)
    half = 64
    spare = jnp.zeros((rows, half - mesh_count), BF)
    pay = jnp.concatenate(
        [cotangent, (place // rows).astype(BF), spare, (place % rows).astype(BF), spare], axis=1
    )
    pay, _ = lax.optimization_barrier((pay, last))
    pay = jnp.concatenate([pay] + [along_sub(pay, k) for k in range(1, SUBS)])
    far_pay = outwards(pay, True)

    hidden, hslope, active, bslope, normed, inverse, hidden_mesh = pl.pallas_call(
        functools.partial(forward_kernel, scale),
        grid=(steps,),
        in_specs=[scalar(), tiled(tile, 1)]
        + [whole((channels, nodes))] * (SUBS + 2)
        + [
            whole((rows, latent)),
            whole((channels, latent)),
            whole((latent, latent)),
            whole((latent, latent)),
            whole((latent, latent)),
        ],
        out_specs=[tiled(tile, latent)] * 5 + [tiled(tile, 1), whole((rows, latent))],
        out_shape=[jax.ShapeDtypeStruct((edges, latent), BF)] * 5
        + [jax.ShapeDtypeStruct((edges, 1), F32), jax.ShapeDtypeStruct((rows, latent), BF)],
        scratch_shapes=[
            pltpu.VMEM(((SUBS + 2) * nodes, wide), BF),
            pltpu.VMEM((wide, nodes), BF),
            pltpu.VMEM((wide, latent), BF),
            pltpu.VMEM((rows, latent), F32),
            pltpu.VMEM((rows, latent), F32),
        ],
        compiler_params=params(),
        name="encode",
    )(sub_scalar, grid_local, *grid, grid_low, grid_high, mesh_in, w_embed, w_src, w_dst, w_edge)

    mesh_band = jnp.concatenate([hidden_mesh] + [along_sub(hidden_mesh, k) for k in range(1, SUBS)])
    mesh_far = outwards(mesh_band, True)
    at = jnp.where(sub < SUBS // 2, sub, lax.rem(sub + 1, SUBS)) * rows
    mesh_side = outwards(lax.dynamic_slice_in_dim(mesh_band, at, rows), False)

    mesh_out, bgrad, part = pl.pallas_call(
        functools.partial(mesh_kernel, mesh_scale, scale, mesh_count),
        grid=(steps,),
        in_specs=[
            scalar(),
            whole((width, latent)),
            whole((width, latent)),
            whole((rows, latent)),
            whole((width, latent + 2 * half)),
            whole((width, latent + 2 * half)),
            whole((latent, latent)),
            whole((latent, latent)),
            whole((latent, latent)),
            tiled(tile, latent),
            tiled(tile, latent),
            tiled(tile, 1),
            tiled(tile, latent),
            tiled(tile, latent),
        ],
        out_specs=[whole((rows, latent)), tiled(tile, latent), whole((2 * latent, latent))],
        out_shape=[
            jax.ShapeDtypeStruct((rows, latent), BF),
            jax.ShapeDtypeStruct((edges, latent), BF),
            jax.ShapeDtypeStruct((2 * latent, latent), BF),
        ],
        scratch_shapes=[
            pltpu.VMEM((2 * width, latent), F32),
            pltpu.VMEM((2 * width, latent), F32),
            pltpu.VMEM((2 * width, 2 * half), jnp.int32),
            pltpu.VMEM((2 * half, 2 * width), jnp.int32),
            pltpu.VMEM((rows, latent), F32),
            pltpu.VMEM((rows, latent), F32),
            pltpu.VMEM((latent, latent), F32),
            pltpu.VMEM((latent, latent), F32),
        ],
        compiler_params=params(),
        name="process",
    )(
        sub_scalar, mesh_band, mesh_far, mesh_side, pay, far_pay, w_proc, w_recv, w_edge,
        active, normed, inverse, bslope, hidden,
    )

    *parts, part_low, part_high = pl.pallas_call(
        grid_kernel,
        grid=(steps,),
        in_specs=[
            scalar(),
            tiled(tile, 1),
            whole((latent, latent)),
            whole((channels, latent)),
            tiled(tile, latent),
            tiled(tile, latent),
        ],
        out_specs=[whole((channels, nodes))] * (SUBS + 2),
        out_shape=[jax.ShapeDtypeStruct((channels, nodes), BF)] * (SUBS + 2),
        scratch_shapes=[pltpu.VMEM((wide, latent), BF), pltpu.VMEM((SUBS + 2, wide, nodes), F32)],
        compiler_params=params(),
        name="channels",
    )(sub_scalar, grid_local, w_src, w_embed, bgrad, hslope)

    near = lax.axis_size(NEAR)
    pieces = lax.all_to_all(part.reshape(near, -1, latent), NEAR, 0, 0, tiled=True)
    pieces, parts, part_low, part_high = lax.optimization_barrier((pieces, parts, part_low, part_high))
    pieces = from_everyone(summed(pieces), FAR)
    from_above = bands_down(part_low)
    from_below = bands_up(part_high)
    pieces, from_above, from_below = lax.optimization_barrier((pieces, from_above, from_below))
    weights = from_everyone(summed(pieces), NEAR).reshape(2 * latent, latent)
    arrived = []
    for k in range(SUBS):
        block = lax.rem(sub + k, SUBS)
        value = parts[k].astype(F32)
        value += jnp.where(block == 0, from_below, jnp.zeros_like(from_below)).astype(F32)
        value += jnp.where(block == SUBS - 1, from_above, jnp.zeros_like(from_above)).astype(F32)
        arrived.append(along_sub(value.astype(BF), k) if k else value)
    weights, *arrived = lax.optimization_barrier((weights, *arrived))
    grid_grad = functools.reduce(jnp.add, [value.astype(F32) for value in arrived])
    src_grad, edge_grad = weights[latent:].astype(F32), weights[:latent].astype(F32)
    return (mesh_out, grid_grad, src_grad, edge_grad)


def solution(mesh):
    torus = Mesh(mesh.devices.reshape(8, 4, 2, mesh.shape["sub"]), ALL)
    return jax.shard_map(
        body,
        mesh=torus,
        in_specs=(
            P(None, ALL),
            P(ALL, None),
            P(),
            P(),
            P(),
            P(),
            P(),
            P(),
            P(ALL, None),
            P(ALL, None),
            P(ALL, None),
        ),
        out_specs=(P(ALL, None), P(None, ALL), P(), P()),
        check_vma=False,
    )
```

```python
import functools
import math

import jax
import jax.numpy as jnp
from jax import lax
from jax.experimental import pallas as pl
from jax.experimental.pallas import tpu as pltpu
from jax.sharding import Mesh
from jax.sharding import PartitionSpec as P

BAND = ("band_0", "band_1", "band_2")
ALL = ("band_0", "band_1", "band_2", "sub")
NEAR = ("band_1", "band_2", "sub")
FAR = "band_0"
SUBS = 4

EPSILON = 1e-05
BF = jnp.bfloat16
F32 = jnp.float32
VMEM = 60 * 1024 * 1024


def sigmoid(value):
    return 0.5 * jnp.tanh(0.5 * value) + 0.5


def silu_and_slope(value):
    sigma = sigmoid(value)
    active = value * sigma
    return active, sigma + active * (1.0 - sigma)


def dot(left, right):
    return jnp.dot(left, right, preferred_element_type=F32)


def dot_t(left, right):
    return lax.dot_general(left, right, (((1,), (1,)), ((), ())), preferred_element_type=F32)


def t_dot(left, right):
    return lax.dot_general(left, right, (((0,), (0,)), ((), ())), preferred_element_type=F32)


def selection(column, width):
    lanes = lax.broadcasted_iota(jnp.int32, (column.shape[0], width), 1)
    return jnp.where(column == lanes, 1.0, 0.0).astype(BF)


def selection_t(row, height):
    lines = lax.broadcasted_iota(jnp.int32, (height, row.shape[1]), 0)
    return jnp.where(row == lines, 1.0, 0.0).astype(BF)


def padded_rows(ref, scratch):
    rows = ref.shape[0]
    scratch[...] = jnp.zeros_like(scratch)
    scratch[:rows, :] = ref[...]
    return scratch[...]


def forward_kernel(
    scale,
    sub_ref, index_ref, own_ref, one_ref, two_ref, three_ref, low_ref, high_ref,
    mesh_ref, embed_ref, src_ref, dst_ref, edge_ref,
    hidden_ref, hslope_ref, active_ref, bslope_ref, normed_ref, inverse_ref, mesh_out_ref,
    table, pad, embed, dest, total,
):
    step = pl.program_id(0)
    sources = (own_ref, one_ref, two_ref, three_ref, low_ref, high_ref)
    nodes = low_ref.shape[1]
    rows = mesh_ref.shape[0]
    sub = sub_ref[0]
    bases = [(lax.rem(sub + SUBS - k, SUBS) + 1) * nodes for k in range(SUBS)]
    bases += [0, (SUBS + 1) * nodes]

    @pl.when(step == 0)
    def _():
        for block, source in enumerate(sources):
            table[block * nodes : (block + 1) * nodes, :] = padded_rows(source, pad).T
        embed[...] = padded_rows(embed_ref, pad)
        dest[...] = dot(mesh_ref[...], dst_ref[...])
        total[...] = jnp.zeros_like(total)

    column = index_ref[...]
    edges = column.shape[0]
    picked = jnp.zeros((edges, table.shape[1]), F32)
    for block, base in enumerate(bases):
        part = table[block * nodes : (block + 1) * nodes, :]
        picked += dot(selection(column - base, nodes), part)
    hidden, hslope = silu_and_slope(dot(picked.astype(BF), embed[...]))
    hidden = hidden.astype(BF)
    hidden_ref[...] = hidden
    hslope_ref[...] = hslope.astype(BF)
    projected = dot(hidden, src_ref[...]).astype(BF).astype(F32)
    before = (projected.reshape(-1, rows, projected.shape[1]) + dest[...][None]).reshape(projected.shape)
    active, bslope = silu_and_slope(before)
    active = active.astype(BF)
    active_ref[...] = active
    bslope_ref[...] = bslope.astype(BF)
    out = dot(active, edge_ref[...])
    centred = out - jnp.mean(out, axis=-1, keepdims=True)
    inverse = lax.rsqrt(jnp.mean(centred * centred, axis=-1, keepdims=True) + EPSILON)
    normed = centred * inverse
    normed_ref[...] = normed.astype(BF)
    inverse_ref[...] = inverse
    total[...] += jnp.sum(normed.reshape(-1, rows, normed.shape[1]), axis=0)

    @pl.when(step == pl.num_programs(0) - 1)
    def _():
        mesh_out_ref[...] = (mesh_ref[...].astype(F32) + total[...] * scale).astype(BF)


def product_kernel(edge_ref, normed_ref, product_ref):
    product_ref[...] = dot_t(normed_ref[...], edge_ref[...]).astype(BF)


def mesh_kernel(
    mesh_scale, scale, count,
    sub_ref, band_ref, far_ref, side_ref, pay_ref, far_pay_ref, proc_ref, recv_ref, edge_ref,
    active_ref, normed_ref, product_ref, inverse_ref, bslope_ref, hidden_ref,
    out_ref, bgrad_ref, wgrad_ref,
    receiver_all, cots, columns, lines, query_grad, centred_ref, upper_ref, through_ref, edge_total, src_total,
):
    step = pl.program_id(0)
    rows, latent = side_ref.shape
    wide = band_ref.shape[0]

    @pl.when(step == 0)
    def _():
        sub = sub_ref[0]
        lower = sub < SUBS // 2
        proc = proc_ref[...]
        recv = recv_ref[...]
        own = band_ref[:rows, :]
        window = jnp.concatenate([band_ref[...], far_ref[...], side_ref[...]], axis=0)
        query = dot(window, proc).astype(BF)
        receiver_all[:wide, :] = dot(band_ref[...], recv)
        receiver_all[wide:, :] = dot(far_ref[...], recv)
        receiver = receiver_all[:rows, :]

        tail = pay_ref[:, latent:].astype(F32).astype(jnp.int32)
        far_tail = far_pay_ref[:, latent:].astype(F32).astype(jnp.int32)
        turn = tail.shape[1] // 2
        block, line = tail[:, :turn], tail[:, turn:]
        far_block, far_line = far_tail[:, :turn], far_tail[:, turn:]
        far_wanted = jnp.where(lower, SUBS + 1 + sub, sub - SUBS + 1)
        columns[:wide, :turn] = (block - (sub + 1)) * rows + line
        columns[wide:, :turn] = (far_block - far_wanted) * rows + far_line
        own_block, own_line = block[:rows], line[:rows]
        inside = lax.rem(sub + SUBS + 1 - own_block, SUBS) * rows
        below = jnp.where(lower, wide + lax.rem(sub + 1, SUBS) * rows, 2 * wide)
        above = jnp.where(lower, 2 * wide, wide + sub * rows)
        place = jnp.where(own_block == 0, below, jnp.where(own_block == SUBS + 1, above, inside))
        place = place + own_line
        columns[:, turn:] = jnp.zeros_like(columns[:, turn:])
        lines[...] = columns[...].T
        cots[:wide, :] = pay_ref[:, :latent].astype(F32) * mesh_scale
        cots[wide:, :] = far_pay_ref[:, :latent].astype(F32) * mesh_scale

        summed = jnp.zeros((rows, latent), F32)
        slopes = jnp.zeros((rows, latent), F32)
        for j in range(count):
            sent = dot(selection(place[:, j : j + 1], window.shape[0]), query)
            active, slope = silu_and_slope(sent + receiver)
            summed += active
            slopes += slope
        out_ref[...] = (own.astype(F32) + summed * mesh_scale).astype(BF)
        receiver_grad = cots[:rows, :] * slopes

        own_query = query[:rows]
        query_grad[...] = jnp.zeros_like(query_grad)
        lanes = lax.broadcasted_iota(jnp.int32, columns.shape, 1)

        def one(j, carry):
            column = jnp.sum(jnp.where(lanes == j, columns[...], 0), axis=1, keepdims=True)
            value = dot(selection(column, rows), own_query) + receiver_all[...]
            _, slopes = silu_and_slope(value)
            slopes = (cots[...] * slopes).astype(BF)
            query_grad[...] += dot(selection_t(lines[pl.ds(j, 1), :], rows), slopes)
            return carry

        lax.fori_loop(0, count, one, 0)
        mesh_grad = pay_ref[:rows, :latent].astype(F32) + dot_t(query_grad[...].astype(BF), proc)
        mesh_grad = mesh_grad + dot_t(receiver_grad.astype(BF), recv)
        upper = mesh_grad * scale
        upper_ref[...] = upper
        centred_ref[...] = upper - jnp.mean(upper, axis=-1, keepdims=True)
        through_ref[...] = dot_t(centred_ref[...].astype(BF), edge_ref[...])
        edge_total[...] = jnp.zeros_like(edge_total)
        src_total[...] = jnp.zeros_like(src_total)

    normed = normed_ref[...].astype(F32).reshape(-1, rows, latent)
    product = product_ref[...].astype(F32).reshape(-1, rows, latent)
    inverse = inverse_ref[...].reshape(-1, rows, 1)
    along = jnp.mean(upper_ref[...][None] * normed, axis=-1, keepdims=True)
    ngrad = ((centred_ref[...][None] - normed * along) * inverse).reshape(-1, latent).astype(BF)
    edge_total[...] += t_dot(active_ref[...], ngrad)
    bgrad = ((through_ref[...][None] - product * along) * inverse).reshape(-1, latent)
    bgrad = (bgrad * bslope_ref[...].astype(F32)).astype(BF)
    bgrad_ref[...] = bgrad
    src_total[...] += t_dot(hidden_ref[...], bgrad)

    @pl.when(step == pl.num_programs(0) - 1)
    def _():
        wgrad_ref[:latent, :] = edge_total[...].astype(BF)
        wgrad_ref[latent:, :] = src_total[...].astype(BF)


def grid_kernel(
    sub_ref, index_ref, src_ref, embed_ref, bgrad_ref, hslope_ref,
    own_ref, one_ref, two_ref, three_ref, low_ref, high_ref,
    pad, total,
):
    step = pl.program_id(0)
    channels, nodes = low_ref.shape
    targets = (own_ref, one_ref, two_ref, three_ref, low_ref, high_ref)
    sub = sub_ref[0]
    bases = [(lax.rem(sub + k, SUBS) + 1) * nodes for k in range(SUBS)]
    bases += [0, (SUBS + 1) * nodes]

    @pl.when(step == 0)
    def _():
        padded_rows(embed_ref, pad)
        total[...] = jnp.zeros_like(total)

    hgrad = (dot_t(bgrad_ref[...], src_ref[...]) * hslope_ref[...].astype(F32)).astype(BF)
    ggrad = dot_t(pad[...], hgrad).astype(BF)
    column = index_ref[...]
    for block, base in enumerate(bases):
        total[block] += dot(ggrad, selection(column - base, nodes))

    @pl.when(step == pl.num_programs(0) - 1)
    def _():
        for block, target in enumerate(targets):
            target[...] = total[block][:channels].astype(BF)


def whole(shape):
    return pl.BlockSpec(shape, lambda i, n=len(shape): (0,) * n)


def tiled(edges, width):
    return pl.BlockSpec((edges, width), lambda i: (i, 0))


def scalar():
    return pl.BlockSpec(memory_space=pltpu.SMEM)


def params():
    return pltpu.CompilerParams(dimension_semantics=("arbitrary",), vmem_limit_bytes=VMEM)


def from_everyone(shard, axis):
    devices = lax.axis_size(axis)
    return lax.all_to_all(
        jnp.broadcast_to(shard[None], (devices, *shard.shape)), axis, 0, 0, tiled=True
    )


def bands_up(value):
    count = lax.axis_size(BAND)
    return lax.ppermute(value, BAND, [(i, i + 1) for i in range(count - 1)])


def bands_down(value):
    count = lax.axis_size(BAND)
    return lax.ppermute(value, BAND, [(i + 1, i) for i in range(count - 1)])


def outwards(value, near):
    bands, subs = lax.axis_size(BAND), lax.axis_size("sub")
    pairs = []
    for band in range(bands):
        for sub in range(subs):
            up = (sub < subs // 2) == near
            to = band + 1 if up else band - 1
            if 0 <= to < bands:
                pairs.append((band * subs + sub, to * subs + sub))
    return lax.ppermute(value, ALL, pairs)


def along_sub(value, steps):
    count = lax.axis_size("sub")
    return lax.ppermute(value, "sub", [(i, (i + steps) % count) for i in range(count)])


def summed(parts):
    return jnp.sum(parts.astype(F32), axis=0).astype(BF)


def body(
    grid_x, mesh_in, w_embed, w_src, w_dst, w_edge, w_proc, w_recv, g2m_src, mesh_src, cotangent
):
    channels, nodes = grid_x.shape
    latent = w_src.shape[0]
    rows, enc_count = g2m_src.shape
    mesh_count = mesh_src.shape[1]
    band = lax.axis_index(BAND)
    sub = lax.axis_index("sub")
    sub_scalar = sub.astype(jnp.int32).reshape(1)
    wide = -(-channels // 128) * 128
    edges = rows * enc_count
    steps = 4
    tile = edges // steps
    width = SUBS * rows
    scale = 1.0 / math.sqrt(enc_count)
    mesh_scale = 1.0 / math.sqrt(mesh_count)

    grid = [grid_x] + [along_sub(grid_x, k) for k in range(1, SUBS)]
    last = lax.select_n(lax.rem(sub + 1, SUBS), *grid)
    first = lax.select_n(sub, *grid)
    grid_low = bands_up(last)
    grid_high = bands_down(first)
    grid_local = (g2m_src - (band * (nodes * SUBS) - nodes)).T.reshape(edges, 1)

    place = mesh_src - (band * width - rows)
    half = 64
    spare = jnp.zeros((rows, half - mesh_count), BF)
    cot_then, _ = lax.optimization_barrier((cotangent, last))
    pay = jnp.concatenate(
        [cot_then, (place // rows).astype(BF), spare, (place % rows).astype(BF), spare], axis=1
    )
    pay = jnp.concatenate([pay] + [along_sub(pay, k) for k in range(1, SUBS)])

    hidden, hslope, active, bslope, normed, inverse, hidden_mesh = pl.pallas_call(
        functools.partial(forward_kernel, scale),
        grid=(steps,),
        in_specs=[scalar(), tiled(tile, 1)]
        + [whole((channels, nodes))] * (SUBS + 2)
        + [
            whole((rows, latent)),
            whole((channels, latent)),
            whole((latent, latent)),
            whole((latent, latent)),
            whole((latent, latent)),
        ],
        out_specs=[tiled(tile, latent)] * 5 + [tiled(tile, 1), whole((rows, latent))],
        out_shape=[jax.ShapeDtypeStruct((edges, latent), BF)] * 5
        + [jax.ShapeDtypeStruct((edges, 1), F32), jax.ShapeDtypeStruct((rows, latent), BF)],
        scratch_shapes=[
            pltpu.VMEM(((SUBS + 2) * nodes, wide), BF),
            pltpu.VMEM((wide, nodes), BF),
            pltpu.VMEM((wide, latent), BF),
            pltpu.VMEM((rows, latent), F32),
            pltpu.VMEM((rows, latent), F32),
        ],
        compiler_params=params(),
        name="encode",
    )(sub_scalar, grid_local, *grid, grid_low, grid_high, mesh_in, w_embed, w_src, w_dst, w_edge)

    pay, _ = lax.optimization_barrier((pay, hidden_mesh))
    far_pay = outwards(pay, True)
    mesh_band = jnp.concatenate([hidden_mesh] + [along_sub(hidden_mesh, k) for k in range(1, SUBS)])
    mesh_far = outwards(mesh_band, True)
    at = jnp.where(sub < SUBS // 2, sub, lax.rem(sub + 1, SUBS)) * rows
    mesh_side = outwards(lax.dynamic_slice_in_dim(mesh_band, at, rows), False)

    normed_then, _ = lax.optimization_barrier((normed, mesh_band))
    product = pl.pallas_call(
        product_kernel,
        grid=(2,),
        in_specs=[whole((latent, latent)), tiled(edges // 2, latent)],
        out_specs=tiled(edges // 2, latent),
        out_shape=jax.ShapeDtypeStruct((edges, latent), BF),
        compiler_params=params(),
        cost_estimate=pl.CostEstimate(
            flops=2 * edges * latent * latent, bytes_accessed=4 * edges * latent, transcendentals=0
        ),
        name="product",
    )(w_edge, normed_then)

    mesh_out, bgrad, part = pl.pallas_call(
        functools.partial(mesh_kernel, mesh_scale, scale, mesh_count),
        grid=(steps,),
        in_specs=[
            scalar(),
            whole((width, latent)),
            whole((width, latent)),
            whole((rows, latent)),
            whole((width, latent + 2 * half)),
            whole((width, latent + 2 * half)),
            whole((latent, latent)),
            whole((latent, latent)),
            whole((latent, latent)),
            tiled(tile, latent),
            tiled(tile, latent),
            tiled(tile, latent),
            tiled(tile, 1),
            tiled(tile, latent),
            tiled(tile, latent),
        ],
        out_specs=[whole((rows, latent)), tiled(tile, latent), whole((2 * latent, latent))],
        out_shape=[
            jax.ShapeDtypeStruct((rows, latent), BF),
            jax.ShapeDtypeStruct((edges, latent), BF),
            jax.ShapeDtypeStruct((2 * latent, latent), BF),
        ],
        scratch_shapes=[
            pltpu.VMEM((2 * width, latent), F32),
            pltpu.VMEM((2 * width, latent), F32),
            pltpu.VMEM((2 * width, 2 * half), jnp.int32),
            pltpu.VMEM((2 * half, 2 * width), jnp.int32),
            pltpu.VMEM((rows, latent), F32),
            pltpu.VMEM((rows, latent), F32),
            pltpu.VMEM((rows, latent), F32),
            pltpu.VMEM((rows, latent), F32),
            pltpu.VMEM((latent, latent), F32),
            pltpu.VMEM((latent, latent), F32),
        ],
        compiler_params=params(),
        name="process",
    )(
        sub_scalar, mesh_band, mesh_far, mesh_side, pay, far_pay, w_proc, w_recv, w_edge,
        active, normed, product, inverse, bslope, hidden,
    )

    *parts, part_low, part_high = pl.pallas_call(
        grid_kernel,
        grid=(steps,),
        in_specs=[
            scalar(),
            tiled(tile, 1),
            whole((latent, latent)),
            whole((channels, latent)),
            tiled(tile, latent),
            tiled(tile, latent),
        ],
        out_specs=[whole((channels, nodes))] * (SUBS + 2),
        out_shape=[jax.ShapeDtypeStruct((channels, nodes), BF)] * (SUBS + 2),
        scratch_shapes=[pltpu.VMEM((wide, latent), BF), pltpu.VMEM((SUBS + 2, wide, nodes), F32)],
        compiler_params=params(),
        name="channels",
    )(sub_scalar, grid_local, w_src, w_embed, bgrad, hslope)

    near = lax.axis_size(NEAR)
    pieces = lax.all_to_all(part.reshape(near, -1, latent), NEAR, 0, 0, tiled=True)
    from_above = bands_down(part_low)
    from_below = bands_up(part_high)
    pieces, from_above, from_below = lax.optimization_barrier((pieces, from_above, from_below))
    pieces = from_everyone(summed(pieces), FAR)
    arrived = []
    for k in range(SUBS):
        block = lax.rem(sub + k, SUBS)
        value = parts[k].astype(F32)
        value += jnp.where(block == 0, from_below, jnp.zeros_like(from_below)).astype(F32)
        value += jnp.where(block == SUBS - 1, from_above, jnp.zeros_like(from_above)).astype(F32)
        arrived.append(along_sub(value.astype(BF), k) if k else value)
    pieces, *arrived = lax.optimization_barrier((pieces, *arrived))
    weights = from_everyone(summed(pieces), NEAR).reshape(2 * latent, latent)
    grid_grad = functools.reduce(jnp.add, [value.astype(F32) for value in arrived])
    src_grad, edge_grad = weights[latent:].astype(F32), weights[:latent].astype(F32)
    return (mesh_out, grid_grad, src_grad, edge_grad)


def solution(mesh):
    torus = Mesh(mesh.devices.reshape(8, 4, 2, mesh.shape["sub"]), ALL)
    return jax.shard_map(
        body,
        mesh=torus,
        in_specs=(
            P(None, ALL),
            P(ALL, None),
            P(),
            P(),
            P(),
            P(),
            P(),
            P(),
            P(ALL, None),
            P(ALL, None),
            P(ALL, None),
        ),
        out_specs=(P(ALL, None), P(None, ALL), P(), P()),
        check_vma=False,
    )
```

```python
import functools
import math

import jax
import jax.numpy as jnp
from jax import lax
from jax.experimental import pallas as pl
from jax.experimental.pallas import tpu as pltpu
from jax.sharding import Mesh
from jax.sharding import PartitionSpec as P

BAND = ("band_0", "band_1", "band_2")
ALL = ("band_0", "band_1", "band_2", "sub")
NEAR = ("band_1", "band_2", "sub")
FAR = "band_0"
SUBS = 4

EPSILON = 1e-05
BF = jnp.bfloat16
F32 = jnp.float32
VMEM = 60 * 1024 * 1024


def sigmoid(value):
    return 0.5 * jnp.tanh(0.5 * value) + 0.5


def silu_and_slope(value):
    sigma = sigmoid(value)
    active = value * sigma
    return active, sigma + active * (1.0 - sigma)


def dot(left, right):
    return jnp.dot(left, right, preferred_element_type=F32)


def dot_t(left, right):
    return lax.dot_general(left, right, (((1,), (1,)), ((), ())), preferred_element_type=F32)


def t_dot(left, right):
    return lax.dot_general(left, right, (((0,), (0,)), ((), ())), preferred_element_type=F32)


def selection(column, width):
    lanes = lax.broadcasted_iota(jnp.int32, (column.shape[0], width), 1)
    return jnp.where(column == lanes, 1.0, 0.0).astype(BF)


def selection_t(row, height):
    lines = lax.broadcasted_iota(jnp.int32, (height, row.shape[1]), 0)
    return jnp.where(row == lines, 1.0, 0.0).astype(BF)


def padded_rows(ref, scratch):
    rows = ref.shape[0]
    scratch[...] = jnp.zeros_like(scratch)
    scratch[:rows, :] = ref[...]
    return scratch[...]


def gather_kernel(blocks, sub_ref, index_ref, *refs):
    *sources, picked_ref, table, pad = refs
    nodes = sources[0].shape[1]
    sub = sub_ref[0]

    @pl.when(pl.program_id(0) == 0)
    def _():
        for place, source in enumerate(sources):
            table[place * nodes : (place + 1) * nodes, :] = padded_rows(source, pad).T

    column = index_ref[...]
    chosen = [
        selection(column - (lax.rem(sub + SUBS - k, SUBS) + 1) * nodes, nodes) for k in blocks
    ]
    picked_ref[...] = dot(jnp.concatenate(chosen, axis=1), table[...]).astype(BF)


def forward_kernel(
    scale,
    sub_ref, index_ref, picked_ref, two_ref, low_ref, high_ref,
    mesh_ref, embed_ref, src_ref, dst_ref, edge_ref,
    hidden_ref, hslope_ref, active_ref, bslope_ref, normed_ref, inverse_ref, mesh_out_ref,
    table, pad, embed, dest, total,
):
    step = pl.program_id(0)
    sources = (two_ref, low_ref, high_ref)
    nodes = low_ref.shape[1]
    rows = mesh_ref.shape[0]
    sub = sub_ref[0]
    bases = [(lax.rem(sub + SUBS - 2, SUBS) + 1) * nodes, 0, (SUBS + 1) * nodes]

    @pl.when(step == 0)
    def _():
        for block, source in enumerate(sources):
            table[block * nodes : (block + 1) * nodes, :] = padded_rows(source, pad).T
        embed[...] = padded_rows(embed_ref, pad)
        dest[...] = dot(mesh_ref[...], dst_ref[...])
        total[...] = jnp.zeros_like(total)

    column = index_ref[...]
    chosen = [selection(column - base, nodes) for base in bases]
    picked = dot(jnp.concatenate(chosen, axis=1), table[...]).astype(BF) + picked_ref[...]
    hidden, hslope = silu_and_slope(dot(picked, embed[...]))
    hidden = hidden.astype(BF)
    hidden_ref[...] = hidden
    hslope_ref[...] = hslope.astype(BF)
    projected = dot(hidden, src_ref[...]).astype(BF).astype(F32)
    before = (projected.reshape(-1, rows, projected.shape[1]) + dest[...][None]).reshape(projected.shape)
    active, bslope = silu_and_slope(before)
    active = active.astype(BF)
    active_ref[...] = active
    bslope_ref[...] = bslope.astype(BF)
    out = dot(active, edge_ref[...])
    centred = out - jnp.mean(out, axis=-1, keepdims=True)
    inverse = lax.rsqrt(jnp.mean(centred * centred, axis=-1, keepdims=True) + EPSILON)
    normed = centred * inverse
    normed_ref[...] = normed.astype(BF)
    inverse_ref[...] = inverse
    total[...] += jnp.sum(normed.reshape(-1, rows, normed.shape[1]), axis=0)

    @pl.when(step == pl.num_programs(0) - 1)
    def _():
        mesh_out_ref[...] = (mesh_ref[...].astype(F32) + total[...] * scale).astype(BF)


def product_kernel(edge_ref, normed_ref, product_ref):
    product_ref[...] = dot_t(normed_ref[...], edge_ref[...]).astype(BF)


def mesh_kernel(
    mesh_scale, scale, count,
    sub_ref, band_all, far_all, side_ref, proc_ref, recv_ref, edge_ref,
    active_ref, normed_ref, product_ref, inverse_ref, bslope_ref, hidden_ref,
    out_ref, bgrad_ref, wgrad_ref,
    receiver_all, cots, columns, lines, query_grad, centred_ref, upper_ref, through_ref, edge_total, src_total,
):
    step = pl.program_id(0)
    rows, latent = side_ref.shape
    wide = band_all.shape[0]
    band_ref, far_ref = band_all.at[:, :latent], far_all.at[:, :latent]
    pay_ref, far_pay_ref = band_all.at[:, latent:], far_all.at[:, latent:]

    @pl.when(step == 0)
    def _():
        sub = sub_ref[0]
        lower = sub < SUBS // 2
        proc = proc_ref[...]
        recv = recv_ref[...]
        own = band_ref[:rows, :]
        window = jnp.concatenate([band_ref[...], far_ref[...], side_ref[...]], axis=0)
        query = dot(window, proc).astype(BF)
        receiver_all[:wide, :] = dot(band_ref[...], recv)
        receiver_all[wide:, :] = dot(far_ref[...], recv)
        receiver = receiver_all[:rows, :]

        tail = pay_ref[:, latent:].astype(F32).astype(jnp.int32)
        far_tail = far_pay_ref[:, latent:].astype(F32).astype(jnp.int32)
        turn = tail.shape[1] // 2
        block, line = tail[:, :turn], tail[:, turn:]
        far_block, far_line = far_tail[:, :turn], far_tail[:, turn:]
        far_wanted = jnp.where(lower, SUBS + 1 + sub, sub - SUBS + 1)
        columns[:wide, :turn] = (block - (sub + 1)) * rows + line
        columns[wide:, :turn] = (far_block - far_wanted) * rows + far_line
        own_block, own_line = block[:rows], line[:rows]
        inside = lax.rem(sub + SUBS + 1 - own_block, SUBS) * rows
        below = jnp.where(lower, wide + lax.rem(sub + 1, SUBS) * rows, 2 * wide)
        above = jnp.where(lower, 2 * wide, wide + sub * rows)
        place = jnp.where(own_block == 0, below, jnp.where(own_block == SUBS + 1, above, inside))
        place = place + own_line
        columns[:, turn:] = jnp.zeros_like(columns[:, turn:])
        lines[...] = columns[...].T
        cots[:wide, :] = pay_ref[:, :latent].astype(F32) * mesh_scale
        cots[wide:, :] = far_pay_ref[:, :latent].astype(F32) * mesh_scale

        summed = jnp.zeros((rows, latent), F32)
        slopes = jnp.zeros((rows, latent), F32)
        for j in range(count):
            sent = dot(selection(place[:, j : j + 1], window.shape[0]), query)
            active, slope = silu_and_slope(sent + receiver)
            summed += active
            slopes += slope
        out_ref[...] = (own.astype(F32) + summed * mesh_scale).astype(BF)
        receiver_grad = cots[:rows, :] * slopes

        own_query = query[:rows]
        query_grad[...] = jnp.zeros_like(query_grad)
        lanes = lax.broadcasted_iota(jnp.int32, columns.shape, 1)

        def one(j, carry):
            column = jnp.sum(jnp.where(lanes == j, columns[...], 0), axis=1, keepdims=True)
            value = dot(selection(column, rows), own_query) + receiver_all[...]
            _, slopes = silu_and_slope(value)
            slopes = (cots[...] * slopes).astype(BF)
            query_grad[...] += dot(selection_t(lines[pl.ds(j, 1), :], rows), slopes)
            return carry

        lax.fori_loop(0, count, one, 0)
        mesh_grad = pay_ref[:rows, :latent].astype(F32) + dot_t(query_grad[...].astype(BF), proc)
        mesh_grad = mesh_grad + dot_t(receiver_grad.astype(BF), recv)
        upper = mesh_grad * scale
        upper_ref[...] = upper
        centred_ref[...] = upper - jnp.mean(upper, axis=-1, keepdims=True)
        through_ref[...] = dot_t(centred_ref[...].astype(BF), edge_ref[...])
        edge_total[...] = jnp.zeros_like(edge_total)
        src_total[...] = jnp.zeros_like(src_total)

    normed = normed_ref[...].astype(F32).reshape(-1, rows, latent)
    product = product_ref[...].astype(F32).reshape(-1, rows, latent)
    inverse = inverse_ref[...].reshape(-1, rows, 1)
    along = jnp.mean(upper_ref[...][None] * normed, axis=-1, keepdims=True)
    ngrad = ((centred_ref[...][None] - normed * along) * inverse).reshape(-1, latent).astype(BF)
    edge_total[...] += t_dot(active_ref[...], ngrad)
    bgrad = ((through_ref[...][None] - product * along) * inverse).reshape(-1, latent)
    bgrad = (bgrad * bslope_ref[...].astype(F32)).astype(BF)
    bgrad_ref[...] = bgrad
    src_total[...] += t_dot(hidden_ref[...], bgrad)

    @pl.when(step == pl.num_programs(0) - 1)
    def _():
        wgrad_ref[:latent, :] = edge_total[...].astype(BF)
        wgrad_ref[latent:, :] = src_total[...].astype(BF)


def grid_kernel(
    sub_ref, index_ref, src_ref, embed_ref, bgrad_ref, hslope_ref,
    own_ref, one_ref, two_ref, three_ref, low_ref, high_ref,
    pad, total,
):
    step = pl.program_id(0)
    channels, nodes = low_ref.shape
    targets = (own_ref, one_ref, two_ref, three_ref, low_ref, high_ref)
    sub = sub_ref[0]
    bases = [(lax.rem(sub + k, SUBS) + 1) * nodes for k in range(SUBS)]
    bases += [0, (SUBS + 1) * nodes]

    @pl.when(step == 0)
    def _():
        padded_rows(embed_ref, pad)
        total[...] = jnp.zeros_like(total)

    hgrad = (dot_t(bgrad_ref[...], src_ref[...]) * hslope_ref[...].astype(F32)).astype(BF)
    ggrad = dot_t(pad[...], hgrad).astype(BF)
    column = index_ref[...]
    for block, base in enumerate(bases):
        total[block] += dot(ggrad, selection(column - base, nodes))

    @pl.when(step == pl.num_programs(0) - 1)
    def _():
        for block, target in enumerate(targets):
            target[...] = total[block][:channels].astype(BF)


def whole(shape):
    return pl.BlockSpec(shape, lambda i, n=len(shape): (0,) * n)


def tiled(edges, width):
    return pl.BlockSpec((edges, width), lambda i: (i, 0))


def scalar():
    return pl.BlockSpec(memory_space=pltpu.SMEM)


def params():
    return pltpu.CompilerParams(dimension_semantics=("arbitrary",), vmem_limit_bytes=VMEM)


def from_everyone(shard, axis):
    devices = lax.axis_size(axis)
    return lax.all_to_all(
        jnp.broadcast_to(shard[None], (devices, *shard.shape)), axis, 0, 0, tiled=True
    )


def bands_up(value):
    count = lax.axis_size(BAND)
    return lax.ppermute(value, BAND, [(i, i + 1) for i in range(count - 1)])


def bands_down(value):
    count = lax.axis_size(BAND)
    return lax.ppermute(value, BAND, [(i + 1, i) for i in range(count - 1)])


def outwards(value, near):
    bands, subs = lax.axis_size(BAND), lax.axis_size("sub")
    pairs = []
    for band in range(bands):
        for sub in range(subs):
            up = (sub < subs // 2) == near
            to = band + 1 if up else band - 1
            if 0 <= to < bands:
                pairs.append((band * subs + sub, to * subs + sub))
    return lax.ppermute(value, ALL, pairs)


def along_sub(value, steps):
    count = lax.axis_size("sub")
    return lax.ppermute(value, "sub", [(i, (i + steps) % count) for i in range(count)])


def summed(parts):
    return jnp.sum(parts.astype(F32), axis=0).astype(BF)


def body(
    grid_x, mesh_in, w_embed, w_src, w_dst, w_edge, w_proc, w_recv, g2m_src, mesh_src, cotangent
):
    channels, nodes = grid_x.shape
    latent = w_src.shape[0]
    rows, enc_count = g2m_src.shape
    mesh_count = mesh_src.shape[1]
    band = lax.axis_index(BAND)
    sub = lax.axis_index("sub")
    sub_scalar = sub.astype(jnp.int32).reshape(1)
    wide = -(-channels // 128) * 128
    edges = rows * enc_count
    steps = 4
    tile = edges // steps
    width = SUBS * rows
    scale = 1.0 / math.sqrt(enc_count)
    mesh_scale = 1.0 / math.sqrt(mesh_count)

    grid = [grid_x] + [along_sub(grid_x, k) for k in range(1, SUBS)]
    grid_local = (g2m_src - (band * (nodes * SUBS) - nodes)).T.reshape(edges, 1)

    nearest = (0, 1, 3)
    picked = pl.pallas_call(
        functools.partial(gather_kernel, nearest),
        grid=(2,),
        in_specs=[scalar(), tiled(edges // 2, 1)] + [whole((channels, nodes))] * len(nearest),
        out_specs=tiled(edges // 2, wide),
        out_shape=jax.ShapeDtypeStruct((edges, wide), BF),
        scratch_shapes=[
            pltpu.VMEM((len(nearest) * nodes, wide), BF),
            pltpu.VMEM((wide, nodes), BF),
        ],
        compiler_params=params(),
        cost_estimate=pl.CostEstimate(
            flops=2 * edges * wide * nodes * len(nearest),
            bytes_accessed=2 * edges * wide,
            transcendentals=0,
        ),
        name="gather",
    )(sub_scalar, grid_local, *[grid[k] for k in nearest])

    grid[2], picked = lax.optimization_barrier((grid[2], picked))
    last = lax.select_n(lax.rem(sub + 1, SUBS), *grid)
    first = lax.select_n(sub, *grid)
    grid_low = bands_up(last)
    grid_high = bands_down(first)

    place = mesh_src - (band * width - rows)
    half = 64
    spare = jnp.zeros((rows, half - mesh_count), BF)
    cot_then, _ = lax.optimization_barrier((cotangent, last))
    pay = jnp.concatenate(
        [cot_then, (place // rows).astype(BF), spare, (place % rows).astype(BF), spare], axis=1
    )
    pay = jnp.concatenate([pay] + [along_sub(pay, k) for k in range(1, SUBS)])

    hidden, hslope, active, bslope, normed, inverse, hidden_mesh = pl.pallas_call(
        functools.partial(forward_kernel, scale),
        grid=(steps,),
        in_specs=[scalar(), tiled(tile, 1), tiled(tile, wide)]
        + [whole((channels, nodes))] * 3
        + [
            whole((rows, latent)),
            whole((channels, latent)),
            whole((latent, latent)),
            whole((latent, latent)),
            whole((latent, latent)),
        ],
        out_specs=[tiled(tile, latent)] * 5 + [tiled(tile, 1), whole((rows, latent))],
        out_shape=[jax.ShapeDtypeStruct((edges, latent), BF)] * 5
        + [jax.ShapeDtypeStruct((edges, 1), F32), jax.ShapeDtypeStruct((rows, latent), BF)],
        scratch_shapes=[
            pltpu.VMEM((3 * nodes, wide), BF),
            pltpu.VMEM((wide, nodes), BF),
            pltpu.VMEM((wide, latent), BF),
            pltpu.VMEM((rows, latent), F32),
            pltpu.VMEM((rows, latent), F32),
        ],
        compiler_params=params(),
        name="encode",
    )(sub_scalar, grid_local, picked, grid[2], grid_low, grid_high, mesh_in, w_embed, w_src, w_dst, w_edge)

    mesh_band = jnp.concatenate([hidden_mesh] + [along_sub(hidden_mesh, k) for k in range(1, SUBS)])
    mesh_band = jnp.concatenate([mesh_band, pay], axis=1)
    mesh_far = outwards(mesh_band, True)
    at = jnp.where(sub < SUBS // 2, sub, lax.rem(sub + 1, SUBS)) * rows
    mesh_side = outwards(lax.dynamic_slice(mesh_band, (at, 0), (rows, latent)), False)

    normed_then, _ = lax.optimization_barrier((normed, mesh_band))
    product = pl.pallas_call(
        product_kernel,
        grid=(2,),
        in_specs=[whole((latent, latent)), tiled(edges // 2, latent)],
        out_specs=tiled(edges // 2, latent),
        out_shape=jax.ShapeDtypeStruct((edges, latent), BF),
        compiler_params=params(),
        cost_estimate=pl.CostEstimate(
            flops=2 * edges * latent * latent, bytes_accessed=4 * edges * latent, transcendentals=0
        ),
        name="product",
    )(w_edge, normed_then)

    mesh_out, bgrad, part = pl.pallas_call(
        functools.partial(mesh_kernel, mesh_scale, scale, mesh_count),
        grid=(steps,),
        in_specs=[
            scalar(),
            whole((width, 2 * latent + 2 * half)),
            whole((width, 2 * latent + 2 * half)),
            whole((rows, latent)),
            whole((latent, latent)),
            whole((latent, latent)),
            whole((latent, latent)),
            tiled(tile, latent),
            tiled(tile, latent),
            tiled(tile, latent),
            tiled(tile, 1),
            tiled(tile, latent),
            tiled(tile, latent),
        ],
        out_specs=[whole((rows, latent)), tiled(tile, latent), whole((2 * latent, latent))],
        out_shape=[
            jax.ShapeDtypeStruct((rows, latent), BF),
            jax.ShapeDtypeStruct((edges, latent), BF),
            jax.ShapeDtypeStruct((2 * latent, latent), BF),
        ],
        scratch_shapes=[
            pltpu.VMEM((2 * width, latent), F32),
            pltpu.VMEM((2 * width, latent), F32),
            pltpu.VMEM((2 * width, 2 * half), jnp.int32),
            pltpu.VMEM((2 * half, 2 * width), jnp.int32),
            pltpu.VMEM((rows, latent), F32),
            pltpu.VMEM((rows, latent), F32),
            pltpu.VMEM((rows, latent), F32),
            pltpu.VMEM((rows, latent), F32),
            pltpu.VMEM((latent, latent), F32),
            pltpu.VMEM((latent, latent), F32),
        ],
        compiler_params=params(),
        name="process",
    )(
        sub_scalar, mesh_band, mesh_far, mesh_side, w_proc, w_recv, w_edge,
        active, normed, product, inverse, bslope, hidden,
    )

    *parts, part_low, part_high = pl.pallas_call(
        grid_kernel,
        grid=(steps,),
        in_specs=[
            scalar(),
            tiled(tile, 1),
            whole((latent, latent)),
            whole((channels, latent)),
            tiled(tile, latent),
            tiled(tile, latent),
        ],
        out_specs=[whole((channels, nodes))] * (SUBS + 2),
        out_shape=[jax.ShapeDtypeStruct((channels, nodes), BF)] * (SUBS + 2),
        scratch_shapes=[pltpu.VMEM((wide, latent), BF), pltpu.VMEM((SUBS + 2, wide, nodes), F32)],
        compiler_params=params(),
        name="channels",
    )(sub_scalar, grid_local, w_src, w_embed, bgrad, hslope)

    near = lax.axis_size(NEAR)
    pieces = lax.all_to_all(part.reshape(near, -1, latent), NEAR, 0, 0, tiled=True)
    from_above = bands_down(part_low)
    from_below = bands_up(part_high)
    values = []
    for k in range(SUBS):
        block = lax.rem(sub + k, SUBS)
        value = parts[k].astype(F32)
        value += jnp.where(block == 0, from_below, jnp.zeros_like(from_below)).astype(F32)
        value += jnp.where(block == SUBS - 1, from_above, jnp.zeros_like(from_above)).astype(F32)
        values.append(value.astype(BF) if k else value)
    arrived = values[:1] + [along_sub(values[k], k) for k in range(1, SUBS)]
    pieces = from_everyone(summed(pieces), FAR)
    pieces, arrived[1], arrived[3] = lax.optimization_barrier((pieces, arrived[1], arrived[3]))
    weights = from_everyone(summed(pieces), NEAR).reshape(2 * latent, latent)
    grid_grad = functools.reduce(jnp.add, [value.astype(F32) for value in arrived])
    src_grad, edge_grad = weights[latent:].astype(F32), weights[:latent].astype(F32)
    return (mesh_out, grid_grad, src_grad, edge_grad)


def solution(mesh):
    torus = Mesh(mesh.devices.reshape(8, 4, 2, mesh.shape["sub"]), ALL)
    return jax.shard_map(
        body,
        mesh=torus,
        in_specs=(
            P(None, ALL),
            P(ALL, None),
            P(),
            P(),
            P(),
            P(),
            P(),
            P(),
            P(ALL, None),
            P(ALL, None),
            P(ALL, None),
        ),
        out_specs=(P(ALL, None), P(None, ALL), P(), P()),
        check_vma=False,
    )
```

```python
import functools
import math

import jax
import jax.numpy as jnp
from jax import lax
from jax.experimental import pallas as pl
from jax.experimental.pallas import tpu as pltpu
from jax.sharding import Mesh
from jax.sharding import PartitionSpec as P

BAND = ("band_0", "band_1", "band_2")
ALL = ("band_0", "band_1", "band_2", "sub")
NEAR = ("band_1", "band_2", "sub")
FAR = "band_0"
SUBS = 4

EPSILON = 1e-05
BF = jnp.bfloat16
F32 = jnp.float32
VMEM = 60 * 1024 * 1024


def sigmoid(value):
    return 0.5 * jnp.tanh(0.5 * value) + 0.5


def silu_and_slope(value):
    sigma = sigmoid(value)
    active = value * sigma
    return active, sigma + active * (1.0 - sigma)


def dot(left, right):
    return jnp.dot(left, right, preferred_element_type=F32)


def dot_t(left, right):
    return lax.dot_general(left, right, (((1,), (1,)), ((), ())), preferred_element_type=F32)


def t_dot(left, right):
    return lax.dot_general(left, right, (((0,), (0,)), ((), ())), preferred_element_type=F32)


def selection(column, width):
    lanes = lax.broadcasted_iota(jnp.int32, (column.shape[0], width), 1)
    return jnp.where(column == lanes, 1.0, 0.0).astype(BF)


def selection_t(row, height):
    lines = lax.broadcasted_iota(jnp.int32, (height, row.shape[1]), 0)
    return jnp.where(row == lines, 1.0, 0.0).astype(BF)


def padded_rows(ref, scratch):
    rows = ref.shape[0]
    scratch[...] = jnp.zeros_like(scratch)
    scratch[:rows, :] = ref[...]
    return scratch[...]


def gather_kernel(blocks, sub_ref, index_ref, *refs):
    *sources, picked_ref, table, pad = refs
    nodes = sources[0].shape[1]
    sub = sub_ref[0]

    @pl.when(pl.program_id(0) == 0)
    def _():
        for place, source in enumerate(sources):
            table[place * nodes : (place + 1) * nodes, :] = padded_rows(source, pad).T

    column = index_ref[...]
    chosen = [
        selection(column - (lax.rem(sub + SUBS - k, SUBS) + 1) * nodes, nodes) for k in blocks
    ]
    picked_ref[...] = dot(jnp.concatenate(chosen, axis=1), table[...]).astype(BF)


def forward_kernel(
    scale,
    sub_ref, index_ref, picked_ref, two_ref, low_ref, high_ref,
    mesh_ref, pay_ref, embed_ref, src_ref, dst_ref, edge_ref,
    hidden_ref, hslope_ref, active_ref, bslope_ref, normed_ref, inverse_ref, mesh_out_ref,
    table, pad, embed, dest, total,
):
    step = pl.program_id(0)
    sources = (two_ref, low_ref, high_ref)
    nodes = low_ref.shape[1]
    rows = mesh_ref.shape[0]
    sub = sub_ref[0]
    bases = [(lax.rem(sub + SUBS - 2, SUBS) + 1) * nodes, 0, (SUBS + 1) * nodes]

    @pl.when(step == 0)
    def _():
        for block, source in enumerate(sources):
            table[block * nodes : (block + 1) * nodes, :] = padded_rows(source, pad).T
        embed[...] = padded_rows(embed_ref, pad)
        dest[...] = dot(mesh_ref[...], dst_ref[...])
        total[...] = jnp.zeros_like(total)

    column = index_ref[...]
    chosen = [selection(column - base, nodes) for base in bases]
    picked = dot(jnp.concatenate(chosen, axis=1), table[...]).astype(BF) + picked_ref[...]
    hidden, hslope = silu_and_slope(dot(picked, embed[...]))
    hidden = hidden.astype(BF)
    hidden_ref[...] = hidden
    hslope_ref[...] = hslope.astype(BF)
    projected = dot(hidden, src_ref[...]).astype(BF).astype(F32)
    before = (projected.reshape(-1, rows, projected.shape[1]) + dest[...][None]).reshape(projected.shape)
    active, bslope = silu_and_slope(before)
    active = active.astype(BF)
    active_ref[...] = active
    bslope_ref[...] = bslope.astype(BF)
    out = dot(active, edge_ref[...])
    centred = out - jnp.mean(out, axis=-1, keepdims=True)
    inverse = lax.rsqrt(jnp.mean(centred * centred, axis=-1, keepdims=True) + EPSILON)
    normed = centred * inverse
    normed_ref[...] = normed.astype(BF)
    inverse_ref[...] = inverse
    total[...] += jnp.sum(normed.reshape(-1, rows, normed.shape[1]), axis=0)

    @pl.when(step == pl.num_programs(0) - 1)
    def _():
        latent = mesh_ref.shape[1]
        mesh_out_ref[:, :latent] = (mesh_ref[...].astype(F32) + total[...] * scale).astype(BF)
        mesh_out_ref[:, latent:] = pay_ref[...]


def product_kernel(edge_ref, normed_ref, product_ref):
    product_ref[...] = dot_t(normed_ref[...], edge_ref[...]).astype(BF)


def mesh_kernel(
    mesh_scale, scale, count,
    sub_ref, band_all, far_all, side_ref, proc_ref, recv_ref, edge_ref,
    active_ref, normed_ref, product_ref, inverse_ref, bslope_ref, hidden_ref,
    out_ref, bgrad_ref, wgrad_ref,
    receiver_all, cots, columns, lines, query_grad, centred_ref, upper_ref, through_ref, edge_total, src_total,
):
    step = pl.program_id(0)
    rows, latent = side_ref.shape
    wide = band_all.shape[0]
    band_ref, far_ref = band_all.at[:, :latent], far_all.at[:, :latent]
    pay_ref, far_pay_ref = band_all.at[:, latent:], far_all.at[:, latent:]

    @pl.when(step == 0)
    def _():
        sub = sub_ref[0]
        lower = sub < SUBS // 2
        proc = proc_ref[...]
        recv = recv_ref[...]
        own = band_ref[:rows, :]
        window = jnp.concatenate([band_ref[...], far_ref[...], side_ref[...]], axis=0)
        query = dot(window, proc).astype(BF)
        receiver_all[:wide, :] = dot(band_ref[...], recv)
        receiver_all[wide:, :] = dot(far_ref[...], recv)
        receiver = receiver_all[:rows, :]

        tail = pay_ref[:, latent:].astype(F32).astype(jnp.int32)
        far_tail = far_pay_ref[:, latent:].astype(F32).astype(jnp.int32)
        turn = tail.shape[1] // 2
        block, line = tail[:, :turn], tail[:, turn:]
        far_block, far_line = far_tail[:, :turn], far_tail[:, turn:]
        far_wanted = jnp.where(lower, SUBS + 1 + sub, sub - SUBS + 1)
        columns[:wide, :turn] = (block - (sub + 1)) * rows + line
        columns[wide:, :turn] = (far_block - far_wanted) * rows + far_line
        own_block, own_line = block[:rows], line[:rows]
        inside = lax.rem(sub + SUBS + 1 - own_block, SUBS) * rows
        below = jnp.where(lower, wide + lax.rem(sub + 1, SUBS) * rows, 2 * wide)
        above = jnp.where(lower, 2 * wide, wide + sub * rows)
        place = jnp.where(own_block == 0, below, jnp.where(own_block == SUBS + 1, above, inside))
        place = place + own_line
        columns[:, turn:] = jnp.zeros_like(columns[:, turn:])
        lines[...] = columns[...].T
        cots[:wide, :] = pay_ref[:, :latent].astype(F32) * mesh_scale
        cots[wide:, :] = far_pay_ref[:, :latent].astype(F32) * mesh_scale

        summed = jnp.zeros((rows, latent), F32)
        slopes = jnp.zeros((rows, latent), F32)
        for j in range(count):
            sent = dot(selection(place[:, j : j + 1], window.shape[0]), query)
            active, slope = silu_and_slope(sent + receiver)
            summed += active
            slopes += slope
        out_ref[...] = (own.astype(F32) + summed * mesh_scale).astype(BF)
        receiver_grad = cots[:rows, :] * slopes

        own_query = query[:rows]
        query_grad[...] = jnp.zeros_like(query_grad)
        lanes = lax.broadcasted_iota(jnp.int32, columns.shape, 1)

        def one(j, carry):
            column = jnp.sum(jnp.where(lanes == j, columns[...], 0), axis=1, keepdims=True)
            value = dot(selection(column, rows), own_query) + receiver_all[...]
            _, slopes = silu_and_slope(value)
            slopes = (cots[...] * slopes).astype(BF)
            query_grad[...] += dot(selection_t(lines[pl.ds(j, 1), :], rows), slopes)
            return carry

        lax.fori_loop(0, count, one, 0)
        mesh_grad = pay_ref[:rows, :latent].astype(F32) + dot_t(query_grad[...].astype(BF), proc)
        mesh_grad = mesh_grad + dot_t(receiver_grad.astype(BF), recv)
        upper = mesh_grad * scale
        upper_ref[...] = upper
        centred_ref[...] = upper - jnp.mean(upper, axis=-1, keepdims=True)
        through_ref[...] = dot_t(centred_ref[...].astype(BF), edge_ref[...])
        edge_total[...] = jnp.zeros_like(edge_total)
        src_total[...] = jnp.zeros_like(src_total)

    normed = normed_ref[...].astype(F32).reshape(-1, rows, latent)
    product = product_ref[...].astype(F32).reshape(-1, rows, latent)
    inverse = inverse_ref[...].reshape(-1, rows, 1)
    along = jnp.mean(upper_ref[...][None] * normed, axis=-1, keepdims=True)
    ngrad = ((centred_ref[...][None] - normed * along) * inverse).reshape(-1, latent).astype(BF)
    edge_total[...] += t_dot(active_ref[...], ngrad)
    bgrad = ((through_ref[...][None] - product * along) * inverse).reshape(-1, latent)
    bgrad = (bgrad * bslope_ref[...].astype(F32)).astype(BF)
    bgrad_ref[...] = bgrad
    src_total[...] += t_dot(hidden_ref[...], bgrad)

    @pl.when(step == pl.num_programs(0) - 1)
    def _():
        wgrad_ref[:latent, :] = edge_total[...].astype(BF)
        wgrad_ref[latent:, :] = src_total[...].astype(BF)


def grid_kernel(
    sub_ref, index_ref, src_ref, embed_ref, bgrad_ref, hslope_ref,
    own_ref, one_ref, two_ref, three_ref, low_ref, high_ref,
    pad, total,
):
    step = pl.program_id(0)
    channels, nodes = low_ref.shape
    targets = (own_ref, one_ref, two_ref, three_ref, low_ref, high_ref)
    sub = sub_ref[0]
    bases = [(lax.rem(sub + k, SUBS) + 1) * nodes for k in range(SUBS)]
    bases += [0, (SUBS + 1) * nodes]

    @pl.when(step == 0)
    def _():
        padded_rows(embed_ref, pad)
        total[...] = jnp.zeros_like(total)

    hgrad = (dot_t(bgrad_ref[...], src_ref[...]) * hslope_ref[...].astype(F32)).astype(BF)
    ggrad = dot_t(pad[...], hgrad).astype(BF)
    column = index_ref[...]
    for block, base in enumerate(bases):
        total[block] += dot(ggrad, selection(column - base, nodes))

    @pl.when(step == pl.num_programs(0) - 1)
    def _():
        for block, target in enumerate(targets):
            target[...] = total[block][:channels].astype(BF)


def whole(shape):
    return pl.BlockSpec(shape, lambda i, n=len(shape): (0,) * n)


def tiled(edges, width):
    return pl.BlockSpec((edges, width), lambda i: (i, 0))


def scalar():
    return pl.BlockSpec(memory_space=pltpu.SMEM)


def params():
    return pltpu.CompilerParams(dimension_semantics=("arbitrary",), vmem_limit_bytes=VMEM)


def from_everyone(shard, axis):
    devices = lax.axis_size(axis)
    return lax.all_to_all(
        jnp.broadcast_to(shard[None], (devices, *shard.shape)), axis, 0, 0, tiled=True
    )


def bands_up(value):
    count = lax.axis_size(BAND)
    return lax.ppermute(value, BAND, [(i, i + 1) for i in range(count - 1)])


def bands_down(value):
    count = lax.axis_size(BAND)
    return lax.ppermute(value, BAND, [(i + 1, i) for i in range(count - 1)])


def outwards(value, near):
    bands, subs = lax.axis_size(BAND), lax.axis_size("sub")
    pairs = []
    for band in range(bands):
        for sub in range(subs):
            up = (sub < subs // 2) == near
            to = band + 1 if up else band - 1
            if 0 <= to < bands:
                pairs.append((band * subs + sub, to * subs + sub))
    return lax.ppermute(value, ALL, pairs)


def along_sub(value, steps):
    count = lax.axis_size("sub")
    return lax.ppermute(value, "sub", [(i, (i + steps) % count) for i in range(count)])


def summed(parts):
    return jnp.sum(parts.astype(F32), axis=0).astype(BF)


def body(
    grid_x, mesh_in, w_embed, w_src, w_dst, w_edge, w_proc, w_recv, g2m_src, mesh_src, cotangent
):
    channels, nodes = grid_x.shape
    latent = w_src.shape[0]
    rows, enc_count = g2m_src.shape
    mesh_count = mesh_src.shape[1]
    band = lax.axis_index(BAND)
    sub = lax.axis_index("sub")
    sub_scalar = sub.astype(jnp.int32).reshape(1)
    wide = -(-channels // 128) * 128
    edges = rows * enc_count
    steps = 4
    tile = edges // steps
    width = SUBS * rows
    scale = 1.0 / math.sqrt(enc_count)
    mesh_scale = 1.0 / math.sqrt(mesh_count)

    grid = [grid_x] + [along_sub(grid_x, k) for k in range(1, SUBS)]
    grid_local = (g2m_src - (band * (nodes * SUBS) - nodes)).T.reshape(edges, 1)

    nearest = (0, 1, 3)
    picked = pl.pallas_call(
        functools.partial(gather_kernel, nearest),
        grid=(2,),
        in_specs=[scalar(), tiled(edges // 2, 1)] + [whole((channels, nodes))] * len(nearest),
        out_specs=tiled(edges // 2, wide),
        out_shape=jax.ShapeDtypeStruct((edges, wide), BF),
        scratch_shapes=[
            pltpu.VMEM((len(nearest) * nodes, wide), BF),
            pltpu.VMEM((wide, nodes), BF),
        ],
        compiler_params=params(),
        cost_estimate=pl.CostEstimate(
            flops=2 * edges * wide * nodes * len(nearest),
            bytes_accessed=2 * edges * wide,
            transcendentals=0,
        ),
        name="gather",
    )(sub_scalar, grid_local, *[grid[k] for k in nearest])

    grid[2], picked = lax.optimization_barrier((grid[2], picked))
    last = lax.select_n(lax.rem(sub + 1, SUBS), *grid)
    first = lax.select_n(sub, *grid)
    grid_low = bands_up(last)
    grid_high = bands_down(first)

    place = mesh_src - (band * width - rows)
    half = 64
    spare = jnp.zeros((rows, half - mesh_count), BF)
    pay = jnp.concatenate(
        [cotangent, (place // rows).astype(BF), spare, (place % rows).astype(BF), spare], axis=1
    )

    hidden, hslope, active, bslope, normed, inverse, hidden_mesh = pl.pallas_call(
        functools.partial(forward_kernel, scale),
        grid=(steps,),
        in_specs=[scalar(), tiled(tile, 1), tiled(tile, wide)]
        + [whole((channels, nodes))] * 3
        + [
            whole((rows, latent)),
            whole((rows, latent + 2 * half)),
            whole((channels, latent)),
            whole((latent, latent)),
            whole((latent, latent)),
            whole((latent, latent)),
        ],
        out_specs=[tiled(tile, latent)] * 5 + [tiled(tile, 1), whole((rows, 2 * latent + 2 * half))],
        out_shape=[jax.ShapeDtypeStruct((edges, latent), BF)] * 5
        + [
            jax.ShapeDtypeStruct((edges, 1), F32),
            jax.ShapeDtypeStruct((rows, 2 * latent + 2 * half), BF),
        ],
        scratch_shapes=[
            pltpu.VMEM((3 * nodes, wide), BF),
            pltpu.VMEM((wide, nodes), BF),
            pltpu.VMEM((wide, latent), BF),
            pltpu.VMEM((rows, latent), F32),
            pltpu.VMEM((rows, latent), F32),
        ],
        compiler_params=params(),
        name="encode",
    )(sub_scalar, grid_local, picked, grid[2], grid_low, grid_high, mesh_in, pay, w_embed, w_src, w_dst, w_edge)

    mesh_band = jnp.concatenate([hidden_mesh] + [along_sub(hidden_mesh, k) for k in range(1, SUBS)])
    mesh_far = outwards(mesh_band, True)
    at = jnp.where(sub < SUBS // 2, sub, lax.rem(sub + 1, SUBS)) * rows
    mesh_side = outwards(lax.dynamic_slice(mesh_band, (at, 0), (rows, latent)), False)

    normed_then, _ = lax.optimization_barrier((normed, mesh_band))
    product = pl.pallas_call(
        product_kernel,
        grid=(2,),
        in_specs=[whole((latent, latent)), tiled(edges // 2, latent)],
        out_specs=tiled(edges // 2, latent),
        out_shape=jax.ShapeDtypeStruct((edges, latent), BF),
        compiler_params=params(),
        cost_estimate=pl.CostEstimate(
            flops=2 * edges * latent * latent, bytes_accessed=4 * edges * latent, transcendentals=0
        ),
        name="product",
    )(w_edge, normed_then)

    mesh_out, bgrad, part = pl.pallas_call(
        functools.partial(mesh_kernel, mesh_scale, scale, mesh_count),
        grid=(steps,),
        in_specs=[
            scalar(),
            whole((width, 2 * latent + 2 * half)),
            whole((width, 2 * latent + 2 * half)),
            whole((rows, latent)),
            whole((latent, latent)),
            whole((latent, latent)),
            whole((latent, latent)),
            tiled(tile, latent),
            tiled(tile, latent),
            tiled(tile, latent),
            tiled(tile, 1),
            tiled(tile, latent),
            tiled(tile, latent),
        ],
        out_specs=[whole((rows, latent)), tiled(tile, latent), whole((2 * latent, latent))],
        out_shape=[
            jax.ShapeDtypeStruct((rows, latent), BF),
            jax.ShapeDtypeStruct((edges, latent), BF),
            jax.ShapeDtypeStruct((2 * latent, latent), BF),
        ],
        scratch_shapes=[
            pltpu.VMEM((2 * width, latent), F32),
            pltpu.VMEM((2 * width, latent), F32),
            pltpu.VMEM((2 * width, 2 * half), jnp.int32),
            pltpu.VMEM((2 * half, 2 * width), jnp.int32),
            pltpu.VMEM((rows, latent), F32),
            pltpu.VMEM((rows, latent), F32),
            pltpu.VMEM((rows, latent), F32),
            pltpu.VMEM((rows, latent), F32),
            pltpu.VMEM((latent, latent), F32),
            pltpu.VMEM((latent, latent), F32),
        ],
        compiler_params=params(),
        name="process",
    )(
        sub_scalar, mesh_band, mesh_far, mesh_side, w_proc, w_recv, w_edge,
        active, normed, product, inverse, bslope, hidden,
    )

    *parts, part_low, part_high = pl.pallas_call(
        grid_kernel,
        grid=(steps,),
        in_specs=[
            scalar(),
            tiled(tile, 1),
            whole((latent, latent)),
            whole((channels, latent)),
            tiled(tile, latent),
            tiled(tile, latent),
        ],
        out_specs=[whole((channels, nodes))] * (SUBS + 2),
        out_shape=[jax.ShapeDtypeStruct((channels, nodes), BF)] * (SUBS + 2),
        scratch_shapes=[pltpu.VMEM((wide, latent), BF), pltpu.VMEM((SUBS + 2, wide, nodes), F32)],
        compiler_params=params(),
        name="channels",
    )(sub_scalar, grid_local, w_src, w_embed, bgrad, hslope)

    near = lax.axis_size(NEAR)
    pieces = lax.all_to_all(part.reshape(near, -1, latent), NEAR, 0, 0, tiled=True)
    pieces, parts, part_low, part_high = lax.optimization_barrier((pieces, parts, part_low, part_high))
    pieces = from_everyone(summed(pieces), FAR)
    from_above = bands_down(part_low)
    from_below = bands_up(part_high)
    pieces, from_above, from_below = lax.optimization_barrier((pieces, from_above, from_below))
    weights = from_everyone(summed(pieces), NEAR).reshape(2 * latent, latent)
    values = []
    for k in range(SUBS):
        block = lax.rem(sub + k, SUBS)
        value = parts[k].astype(F32)
        value += jnp.where(block == 0, from_below, jnp.zeros_like(from_below)).astype(F32)
        value += jnp.where(block == SUBS - 1, from_above, jnp.zeros_like(from_above)).astype(F32)
        values.append(value)
    one, two = lax.optimization_barrier((values[1].astype(BF), values[2].astype(BF)))
    ahead = along_sub(one, 1)
    relayed = along_sub(two, -1)
    relayed, ahead = lax.optimization_barrier((relayed, ahead))
    behind = along_sub((values[3] + relayed.astype(F32)).astype(BF), -1)
    weights, behind = lax.optimization_barrier((weights, behind))
    grid_grad = values[0] + ahead.astype(F32) + behind.astype(F32)
    src_grad, edge_grad = weights[latent:].astype(F32), weights[:latent].astype(F32)
    return (mesh_out, grid_grad, src_grad, edge_grad)


def solution(mesh):
    torus = Mesh(mesh.devices.reshape(8, 4, 2, mesh.shape["sub"]), ALL)
    return jax.shard_map(
        body,
        mesh=torus,
        in_specs=(
            P(None, ALL),
            P(ALL, None),
            P(),
            P(),
            P(),
            P(),
            P(),
            P(),
            P(ALL, None),
            P(ALL, None),
            P(ALL, None),
        ),
        out_specs=(P(ALL, None), P(None, ALL), P(), P()),
        check_vma=False,
    )
```

```python
import functools
import math

import jax
import jax.numpy as jnp
from jax import lax
from jax.experimental import pallas as pl
from jax.experimental.pallas import tpu as pltpu
from jax.sharding import Mesh
from jax.sharding import PartitionSpec as P

BAND = ("band_0", "band_1", "band_2")
ALL = ("band_0", "band_1", "band_2", "sub")
NEAR = ("band_1", "band_2", "sub")
FAR = "band_0"
SUBS = 4

EPSILON = 1e-05
BF = jnp.bfloat16
F32 = jnp.float32
VMEM = 60 * 1024 * 1024


def sigmoid(value):
    return 0.5 * jnp.tanh(0.5 * value) + 0.5


def silu_and_slope(value):
    sigma = sigmoid(value)
    active = value * sigma
    return active, sigma + active * (1.0 - sigma)


def dot(left, right):
    return jnp.dot(left, right, preferred_element_type=F32)


def dot_t(left, right):
    return lax.dot_general(left, right, (((1,), (1,)), ((), ())), preferred_element_type=F32)


def t_dot(left, right):
    return lax.dot_general(left, right, (((0,), (0,)), ((), ())), preferred_element_type=F32)


def selection(column, width):
    lanes = lax.broadcasted_iota(jnp.int32, (column.shape[0], width), 1)
    return jnp.where(column == lanes, 1.0, 0.0).astype(BF)


def selection_t(row, height):
    lines = lax.broadcasted_iota(jnp.int32, (height, row.shape[1]), 0)
    return jnp.where(row == lines, 1.0, 0.0).astype(BF)


def padded_rows(ref, scratch):
    rows = ref.shape[0]
    scratch[...] = jnp.zeros_like(scratch)
    scratch[:rows, :] = ref[...]
    return scratch[...]


def gather_kernel(blocks, sub_ref, index_ref, *refs):
    *sources, picked_ref, table, pad = refs
    nodes = sources[0].shape[1]
    sub = sub_ref[0]

    @pl.when(pl.program_id(0) == 0)
    def _():
        for place, source in enumerate(sources):
            table[place * nodes : (place + 1) * nodes, :] = padded_rows(source, pad).T

    column = index_ref[...]
    chosen = [
        selection(column - (lax.rem(sub + SUBS - k, SUBS) + 1) * nodes, nodes) for k in blocks
    ]
    picked_ref[...] = dot(jnp.concatenate(chosen, axis=1), table[...]).astype(BF)


def forward_kernel(
    scale,
    sub_ref, index_ref, picked_ref, two_ref, low_ref, high_ref,
    mesh_ref, embed_ref, src_ref, dst_ref, edge_ref,
    hidden_ref, hslope_ref, active_ref, bslope_ref, normed_ref, inverse_ref, mesh_out_ref,
    table, pad, embed, dest, total,
):
    step = pl.program_id(0)
    sources = (two_ref, low_ref, high_ref)
    nodes = low_ref.shape[1]
    rows = mesh_ref.shape[0]
    sub = sub_ref[0]
    bases = [(lax.rem(sub + SUBS - 2, SUBS) + 1) * nodes, 0, (SUBS + 1) * nodes]

    @pl.when(step == 0)
    def _():
        for block, source in enumerate(sources):
            table[block * nodes : (block + 1) * nodes, :] = padded_rows(source, pad).T
        embed[...] = padded_rows(embed_ref, pad)
        dest[...] = dot(mesh_ref[...], dst_ref[...])
        total[...] = jnp.zeros_like(total)

    column = index_ref[...]
    chosen = [selection(column - base, nodes) for base in bases]
    picked = dot(jnp.concatenate(chosen, axis=1), table[...]).astype(BF) + picked_ref[...]
    hidden, hslope = silu_and_slope(dot(picked, embed[...]))
    hidden = hidden.astype(BF)
    hidden_ref[...] = hidden
    hslope_ref[...] = hslope.astype(BF)
    projected = dot(hidden, src_ref[...]).astype(BF).astype(F32)
    before = (projected.reshape(-1, rows, projected.shape[1]) + dest[...][None]).reshape(projected.shape)
    active, bslope = silu_and_slope(before)
    active = active.astype(BF)
    active_ref[...] = active
    bslope_ref[...] = bslope.astype(BF)
    out = dot(active, edge_ref[...])
    centred = out - jnp.mean(out, axis=-1, keepdims=True)
    inverse = lax.rsqrt(jnp.mean(centred * centred, axis=-1, keepdims=True) + EPSILON)
    normed = centred * inverse
    normed_ref[...] = normed.astype(BF)
    inverse_ref[...] = inverse
    total[...] += jnp.sum(normed.reshape(-1, rows, normed.shape[1]), axis=0)

    @pl.when(step == pl.num_programs(0) - 1)
    def _():
        mesh_out_ref[...] = (mesh_ref[...].astype(F32) + total[...] * scale).astype(BF)


def mesh_kernel(
    mesh_scale, scale, count,
    sub_ref, band_all, far_all, side_ref, proc_ref, recv_ref, edge_ref,
    active_ref, normed_ref, inverse_ref, bslope_ref, hidden_ref,
    out_ref, bgrad_ref, wgrad_ref,
    receiver_all, cots, columns, lines, query_grad, centred_ref, upper_ref, edge_total, src_total,
):
    step = pl.program_id(0)
    rows, latent = side_ref.shape
    wide = band_all.shape[0]
    band_ref, far_ref = band_all.at[:, :latent], far_all.at[:, :latent]
    pay_ref, far_pay_ref = band_all.at[:, latent:], far_all.at[:, latent:]

    @pl.when(step == 0)
    def _():
        sub = sub_ref[0]
        lower = sub < SUBS // 2
        proc = proc_ref[...]
        recv = recv_ref[...]
        own = band_ref[:rows, :]
        window = jnp.concatenate([band_ref[...], far_ref[...], side_ref[...]], axis=0)
        query = dot(window, proc).astype(BF)
        receiver_all[:wide, :] = dot(band_ref[...], recv)
        receiver_all[wide:, :] = dot(far_ref[...], recv)
        receiver = receiver_all[:rows, :]

        tail = pay_ref[:, latent:].astype(F32).astype(jnp.int32)
        far_tail = far_pay_ref[:, latent:].astype(F32).astype(jnp.int32)
        turn = tail.shape[1] // 2
        block, line = tail[:, :turn], tail[:, turn:]
        far_block, far_line = far_tail[:, :turn], far_tail[:, turn:]
        far_wanted = jnp.where(lower, SUBS + 1 + sub, sub - SUBS + 1)
        columns[:wide, :turn] = (block - (sub + 1)) * rows + line
        columns[wide:, :turn] = (far_block - far_wanted) * rows + far_line
        own_block, own_line = block[:rows], line[:rows]
        inside = lax.rem(sub + SUBS + 1 - own_block, SUBS) * rows
        below = jnp.where(lower, wide + lax.rem(sub + 1, SUBS) * rows, 2 * wide)
        above = jnp.where(lower, 2 * wide, wide + sub * rows)
        place = jnp.where(own_block == 0, below, jnp.where(own_block == SUBS + 1, above, inside))
        place = place + own_line
        columns[:, turn:] = jnp.zeros_like(columns[:, turn:])
        lines[...] = columns[...].T
        cots[:wide, :] = pay_ref[:, :latent].astype(F32) * mesh_scale
        cots[wide:, :] = far_pay_ref[:, :latent].astype(F32) * mesh_scale

        summed = jnp.zeros((rows, latent), F32)
        slopes = jnp.zeros((rows, latent), F32)
        for j in range(count):
            sent = dot(selection(place[:, j : j + 1], window.shape[0]), query)
            active, slope = silu_and_slope(sent + receiver)
            summed += active
            slopes += slope
        out_ref[...] = (own.astype(F32) + summed * mesh_scale).astype(BF)
        receiver_grad = cots[:rows, :] * slopes

        own_query = query[:rows]
        query_grad[...] = jnp.zeros_like(query_grad)
        lanes = lax.broadcasted_iota(jnp.int32, columns.shape, 1)

        def one(j, carry):
            column = jnp.sum(jnp.where(lanes == j, columns[...], 0), axis=1, keepdims=True)
            value = dot(selection(column, rows), own_query) + receiver_all[...]
            _, slopes = silu_and_slope(value)
            slopes = (cots[...] * slopes).astype(BF)
            query_grad[...] += dot(selection_t(lines[pl.ds(j, 1), :], rows), slopes)
            return carry

        lax.fori_loop(0, count, one, 0)
        mesh_grad = pay_ref[:rows, :latent].astype(F32) + dot_t(query_grad[...].astype(BF), proc)
        mesh_grad = mesh_grad + dot_t(receiver_grad.astype(BF), recv)
        upper = mesh_grad * scale
        upper_ref[...] = upper
        centred_ref[...] = upper - jnp.mean(upper, axis=-1, keepdims=True)
        edge_total[...] = jnp.zeros_like(edge_total)
        src_total[...] = jnp.zeros_like(src_total)

    normed = normed_ref[...].astype(F32).reshape(-1, rows, latent)
    inverse = inverse_ref[...].reshape(-1, rows, 1)
    along = jnp.mean(upper_ref[...][None] * normed, axis=-1, keepdims=True)
    ngrad = ((centred_ref[...][None] - normed * along) * inverse).reshape(-1, latent).astype(BF)
    edge_total[...] += t_dot(active_ref[...], ngrad)
    bgrad = (dot_t(ngrad, edge_ref[...]) * bslope_ref[...].astype(F32)).astype(BF)
    bgrad_ref[...] = bgrad
    src_total[...] += t_dot(hidden_ref[...], bgrad)

    @pl.when(step == pl.num_programs(0) - 1)
    def _():
        wgrad_ref[:latent, :] = edge_total[...].astype(BF)
        wgrad_ref[latent:, :] = src_total[...].astype(BF)


def grid_kernel(
    sub_ref, index_ref, src_ref, embed_ref, bgrad_ref, hslope_ref,
    own_ref, one_ref, two_ref, three_ref, low_ref, high_ref,
    pad, total,
):
    step = pl.program_id(0)
    channels, nodes = low_ref.shape
    targets = (own_ref, one_ref, two_ref, three_ref, low_ref, high_ref)
    sub = sub_ref[0]
    bases = [(lax.rem(sub + k, SUBS) + 1) * nodes for k in range(SUBS)]
    bases += [0, (SUBS + 1) * nodes]

    @pl.when(step == 0)
    def _():
        padded_rows(embed_ref, pad)
        total[...] = jnp.zeros_like(total)

    hgrad = (dot_t(bgrad_ref[...], src_ref[...]) * hslope_ref[...].astype(F32)).astype(BF)
    ggrad = dot_t(pad[...], hgrad).astype(BF)
    column = index_ref[...]
    for block, base in enumerate(bases):
        total[block] += dot(ggrad, selection(column - base, nodes))

    @pl.when(step == pl.num_programs(0) - 1)
    def _():
        for block, target in enumerate(targets):
            target[...] = total[block][:channels].astype(BF)


def whole(shape):
    return pl.BlockSpec(shape, lambda i, n=len(shape): (0,) * n)


def tiled(edges, width):
    return pl.BlockSpec((edges, width), lambda i: (i, 0))


def scalar():
    return pl.BlockSpec(memory_space=pltpu.SMEM)


def params():
    return pltpu.CompilerParams(dimension_semantics=("arbitrary",), vmem_limit_bytes=VMEM)


def from_everyone(shard, axis):
    devices = lax.axis_size(axis)
    return lax.all_to_all(
        jnp.broadcast_to(shard[None], (devices, *shard.shape)), axis, 0, 0, tiled=True
    )


def bands_up(value):
    count = lax.axis_size(BAND)
    return lax.ppermute(value, BAND, [(i, i + 1) for i in range(count - 1)])


def bands_down(value):
    count = lax.axis_size(BAND)
    return lax.ppermute(value, BAND, [(i + 1, i) for i in range(count - 1)])


def outwards(value, near):
    bands, subs = lax.axis_size(BAND), lax.axis_size("sub")
    pairs = []
    for band in range(bands):
        for sub in range(subs):
            up = (sub < subs // 2) == near
            to = band + 1 if up else band - 1
            if 0 <= to < bands:
                pairs.append((band * subs + sub, to * subs + sub))
    return lax.ppermute(value, ALL, pairs)


def along_sub(value, steps):
    count = lax.axis_size("sub")
    return lax.ppermute(value, "sub", [(i, (i + steps) % count) for i in range(count)])


def summed(parts):
    return jnp.sum(parts.astype(F32), axis=0).astype(BF)


def body(
    grid_x, mesh_in, w_embed, w_src, w_dst, w_edge, w_proc, w_recv, g2m_src, mesh_src, cotangent
):
    channels, nodes = grid_x.shape
    latent = w_src.shape[0]
    rows, enc_count = g2m_src.shape
    mesh_count = mesh_src.shape[1]
    band = lax.axis_index(BAND)
    sub = lax.axis_index("sub")
    sub_scalar = sub.astype(jnp.int32).reshape(1)
    wide = -(-channels // 128) * 128
    edges = rows * enc_count
    steps = 4
    tile = edges // steps
    width = SUBS * rows
    scale = 1.0 / math.sqrt(enc_count)
    mesh_scale = 1.0 / math.sqrt(mesh_count)

    grid = [grid_x] + [along_sub(grid_x, k) for k in range(1, SUBS)]
    grid_local = (g2m_src - (band * (nodes * SUBS) - nodes)).T.reshape(edges, 1)

    nearest = (0, 1, 3)
    picked = pl.pallas_call(
        functools.partial(gather_kernel, nearest),
        grid=(2,),
        in_specs=[scalar(), tiled(edges // 2, 1)] + [whole((channels, nodes))] * len(nearest),
        out_specs=tiled(edges // 2, wide),
        out_shape=jax.ShapeDtypeStruct((edges, wide), BF),
        scratch_shapes=[
            pltpu.VMEM((len(nearest) * nodes, wide), BF),
            pltpu.VMEM((wide, nodes), BF),
        ],
        compiler_params=params(),
        cost_estimate=pl.CostEstimate(
            flops=2 * edges * wide * nodes * len(nearest),
            bytes_accessed=2 * edges * wide,
            transcendentals=0,
        ),
        name="gather",
    )(sub_scalar, grid_local, *[grid[k] for k in nearest])

    grid[2], picked = lax.optimization_barrier((grid[2], picked))
    last = lax.select_n(lax.rem(sub + 1, SUBS), *grid)
    first = lax.select_n(sub, *grid)
    grid_low = bands_up(last)
    grid_high = bands_down(first)

    place = mesh_src - (band * width - rows)
    half = 64
    spare = jnp.zeros((rows, half - mesh_count), BF)
    pay = jnp.concatenate(
        [cotangent, (place // rows).astype(BF), spare, (place % rows).astype(BF), spare], axis=1
    )
    pay = jnp.broadcast_to(pay[None], (SUBS, *pay.shape))
    pay, grid_low, grid_high = lax.optimization_barrier((pay, grid_low, grid_high))
    pay = lax.all_to_all(pay, "sub", 0, 0, tiled=True)
    pay = jnp.concatenate(
        [lax.dynamic_index_in_dim(pay, lax.rem(sub + SUBS - k, SUBS), 0, False) for k in range(SUBS)]
    )

    hidden, hslope, active, bslope, normed, inverse, hidden_mesh = pl.pallas_call(
        functools.partial(forward_kernel, scale),
        grid=(steps,),
        in_specs=[scalar(), tiled(tile, 1), tiled(tile, wide)]
        + [whole((channels, nodes))] * 3
        + [
            whole((rows, latent)),
            whole((channels, latent)),
            whole((latent, latent)),
            whole((latent, latent)),
            whole((latent, latent)),
        ],
        out_specs=[tiled(tile, latent)] * 5 + [tiled(tile, 1), whole((rows, latent))],
        out_shape=[jax.ShapeDtypeStruct((edges, latent), BF)] * 5
        + [jax.ShapeDtypeStruct((edges, 1), F32), jax.ShapeDtypeStruct((rows, latent), BF)],
        scratch_shapes=[
            pltpu.VMEM((3 * nodes, wide), BF),
            pltpu.VMEM((wide, nodes), BF),
            pltpu.VMEM((wide, latent), BF),
            pltpu.VMEM((rows, latent), F32),
            pltpu.VMEM((rows, latent), F32),
        ],
        compiler_params=params(),
        name="encode",
    )(sub_scalar, grid_local, picked, grid[2], grid_low, grid_high, mesh_in, w_embed, w_src, w_dst, w_edge)

    mesh_band = jnp.concatenate([hidden_mesh] + [along_sub(hidden_mesh, k) for k in range(1, SUBS)])
    mesh_band = jnp.concatenate([mesh_band, pay], axis=1)
    mesh_far = outwards(mesh_band, True)
    at = jnp.where(sub < SUBS // 2, sub, lax.rem(sub + 1, SUBS)) * rows
    mesh_side = outwards(lax.dynamic_slice(mesh_band, (at, 0), (rows, latent)), False)

    mesh_out, bgrad, part = pl.pallas_call(
        functools.partial(mesh_kernel, mesh_scale, scale, mesh_count),
        grid=(steps,),
        in_specs=[
            scalar(),
            whole((width, 2 * latent + 2 * half)),
            whole((width, 2 * latent + 2 * half)),
            whole((rows, latent)),
            whole((latent, latent)),
            whole((latent, latent)),
            whole((latent, latent)),
            tiled(tile, latent),
            tiled(tile, latent),
            tiled(tile, 1),
            tiled(tile, latent),
            tiled(tile, latent),
        ],
        out_specs=[whole((rows, latent)), tiled(tile, latent), whole((2 * latent, latent))],
        out_shape=[
            jax.ShapeDtypeStruct((rows, latent), BF),
            jax.ShapeDtypeStruct((edges, latent), BF),
            jax.ShapeDtypeStruct((2 * latent, latent), BF),
        ],
        scratch_shapes=[
            pltpu.VMEM((2 * width, latent), F32),
            pltpu.VMEM((2 * width, latent), F32),
            pltpu.VMEM((2 * width, 2 * half), jnp.int32),
            pltpu.VMEM((2 * half, 2 * width), jnp.int32),
            pltpu.VMEM((rows, latent), F32),
            pltpu.VMEM((rows, latent), F32),
            pltpu.VMEM((rows, latent), F32),
            pltpu.VMEM((latent, latent), F32),
            pltpu.VMEM((latent, latent), F32),
        ],
        compiler_params=params(),
        name="process",
    )(
        sub_scalar, mesh_band, mesh_far, mesh_side, w_proc, w_recv, w_edge,
        active, normed, inverse, bslope, hidden,
    )

    *parts, part_low, part_high = pl.pallas_call(
        grid_kernel,
        grid=(steps,),
        in_specs=[
            scalar(),
            tiled(tile, 1),
            whole((latent, latent)),
            whole((channels, latent)),
            tiled(tile, latent),
            tiled(tile, latent),
        ],
        out_specs=[whole((channels, nodes))] * (SUBS + 2),
        out_shape=[jax.ShapeDtypeStruct((channels, nodes), BF)] * (SUBS + 2),
        scratch_shapes=[pltpu.VMEM((wide, latent), BF), pltpu.VMEM((SUBS + 2, wide, nodes), F32)],
        compiler_params=params(),
        name="channels",
    )(sub_scalar, grid_local, w_src, w_embed, bgrad, hslope)

    near = lax.axis_size(NEAR)
    pieces = lax.all_to_all(part.reshape(near, -1, latent), NEAR, 0, 0, tiled=True)
    from_above = bands_down(part_low)
    from_below = bands_up(part_high)
    values = []
    for k in range(SUBS):
        block = lax.rem(sub + k, SUBS)
        value = parts[k].astype(F32)
        value += jnp.where(block == 0, from_below, jnp.zeros_like(from_below)).astype(F32)
        value += jnp.where(block == SUBS - 1, from_above, jnp.zeros_like(from_above)).astype(F32)
        values.append(value.astype(BF) if k else value)
    ahead = along_sub(values[1], 1)
    relayed = along_sub(values[2], -1)
    pieces = from_everyone(summed(pieces), FAR)
    pieces, ahead, relayed = lax.optimization_barrier((pieces, ahead, relayed))
    behind = along_sub((values[3].astype(F32) + relayed.astype(F32)).astype(BF), -1)
    weights = from_everyone(summed(pieces), NEAR).reshape(2 * latent, latent)
    weights, behind = lax.optimization_barrier((weights, behind))
    grid_grad = values[0] + ahead.astype(F32) + behind.astype(F32)
    src_grad, edge_grad = weights[latent:].astype(F32), weights[:latent].astype(F32)
    return (mesh_out, grid_grad, src_grad, edge_grad)


def solution(mesh):
    torus = Mesh(mesh.devices.reshape(8, 4, 2, mesh.shape["sub"]), ALL)
    return jax.shard_map(
        body,
        mesh=torus,
        in_specs=(
            P(None, ALL),
            P(ALL, None),
            P(),
            P(),
            P(),
            P(),
            P(),
            P(),
            P(ALL, None),
            P(ALL, None),
            P(ALL, None),
        ),
        out_specs=(P(ALL, None), P(None, ALL), P(), P()),
        check_vma=False,
    )
```

```python
import functools
import math

import jax
import jax.numpy as jnp
from jax import lax
from jax.experimental import pallas as pl
from jax.experimental.pallas import tpu as pltpu
from jax.sharding import Mesh
from jax.sharding import PartitionSpec as P

BAND = ("band_0", "band_1", "band_2")
ALL = ("band_0", "band_1", "band_2", "sub")
NEAR = ("band_1", "band_2", "sub")
FAR = "band_0"
SUBS = 4

EPSILON = 1e-05
BF = jnp.bfloat16
F32 = jnp.float32
VMEM = 60 * 1024 * 1024


def sigmoid(value):
    return 0.5 * jnp.tanh(0.5 * value) + 0.5


def silu_and_slope(value):
    sigma = sigmoid(value)
    active = value * sigma
    return active, sigma + active * (1.0 - sigma)


def dot(left, right):
    return jnp.dot(left, right, preferred_element_type=F32)


def dot_t(left, right):
    return lax.dot_general(left, right, (((1,), (1,)), ((), ())), preferred_element_type=F32)


def t_dot(left, right):
    return lax.dot_general(left, right, (((0,), (0,)), ((), ())), preferred_element_type=F32)


def selection(column, width):
    lanes = lax.broadcasted_iota(jnp.int32, (column.shape[0], width), 1)
    return jnp.where(column == lanes, 1.0, 0.0).astype(BF)


def selection_t(row, height):
    lines = lax.broadcasted_iota(jnp.int32, (height, row.shape[1]), 0)
    return jnp.where(row == lines, 1.0, 0.0).astype(BF)


def padded_rows(ref, scratch):
    rows = ref.shape[0]
    scratch[...] = jnp.zeros_like(scratch)
    scratch[:rows, :] = ref[...]
    return scratch[...]


def gather_kernel(blocks, sub_ref, index_ref, *refs):
    *sources, picked_ref, table, pad = refs
    nodes = sources[0].shape[1]
    sub = sub_ref[0]

    @pl.when(pl.program_id(0) == 0)
    def _():
        for place, source in enumerate(sources):
            table[place * nodes : (place + 1) * nodes, :] = padded_rows(source, pad).T

    column = index_ref[...]
    chosen = [
        selection(column - (lax.rem(sub + SUBS - k, SUBS) + 1) * nodes, nodes) for k in blocks
    ]
    picked_ref[...] = dot(jnp.concatenate(chosen, axis=1), table[...]).astype(BF)


def forward_kernel(
    scale,
    sub_ref, index_ref, picked_ref, two_ref, low_ref, high_ref,
    mesh_ref, embed_ref, src_ref, dst_ref, edge_ref,
    hidden_ref, hslope_ref, active_ref, bslope_ref, normed_ref, inverse_ref, mesh_out_ref,
    table, pad, embed, dest, total,
):
    step = pl.program_id(0)
    sources = (two_ref, low_ref, high_ref)
    nodes = low_ref.shape[1]
    rows = mesh_ref.shape[0]
    sub = sub_ref[0]
    bases = [(lax.rem(sub + SUBS - 2, SUBS) + 1) * nodes, 0, (SUBS + 1) * nodes]

    @pl.when(step == 0)
    def _():
        for block, source in enumerate(sources):
            table[block * nodes : (block + 1) * nodes, :] = padded_rows(source, pad).T
        embed[...] = padded_rows(embed_ref, pad)
        dest[...] = dot(mesh_ref[...], dst_ref[...])
        total[...] = jnp.zeros_like(total)

    column = index_ref[...]
    chosen = [selection(column - base, nodes) for base in bases]
    picked = dot(jnp.concatenate(chosen, axis=1), table[...]).astype(BF) + picked_ref[...]
    hidden, hslope = silu_and_slope(dot(picked, embed[...]))
    hidden = hidden.astype(BF)
    hidden_ref[...] = hidden
    hslope_ref[...] = hslope.astype(BF)
    projected = dot(hidden, src_ref[...]).astype(BF).astype(F32)
    before = (projected.reshape(-1, rows, projected.shape[1]) + dest[...][None]).reshape(projected.shape)
    active, bslope = silu_and_slope(before)
    active = active.astype(BF)
    active_ref[...] = active
    bslope_ref[...] = bslope.astype(BF)
    out = dot(active, edge_ref[...])
    centred = out - jnp.mean(out, axis=-1, keepdims=True)
    inverse = lax.rsqrt(jnp.mean(centred * centred, axis=-1, keepdims=True) + EPSILON)
    normed = centred * inverse
    normed_ref[...] = normed.astype(BF)
    inverse_ref[...] = inverse
    total[...] += jnp.sum(normed.reshape(-1, rows, normed.shape[1]), axis=0)

    @pl.when(step == pl.num_programs(0) - 1)
    def _():
        mesh_out_ref[...] = (mesh_ref[...].astype(F32) + total[...] * scale).astype(BF)


def sent_back(count, columns, lines, cots, receiver, own_query, total):
    rows = own_query.shape[0]
    lanes = lax.broadcasted_iota(jnp.int32, columns.shape, 1)

    def one(j, carry):
        column = jnp.sum(jnp.where(lanes == j, columns[...], 0), axis=1, keepdims=True)
        value = dot(selection(column, rows), own_query) + receiver[...]
        _, slopes = silu_and_slope(value)
        slopes = (cots[...] * slopes).astype(BF)
        total[...] += dot(selection_t(lines[pl.ds(j, 1), :], rows), slopes)
        return carry

    lax.fori_loop(0, count, one, 0)


def senders(tail, wanted, rows):
    whole_tail = tail.astype(F32).astype(jnp.int32)
    turn = whole_tail.shape[1] // 2
    return (whole_tail[:, :turn] - wanted) * rows + whole_tail[:, turn:]


def near_kernel(
    mesh_scale, count,
    sub_ref, band_ref, proc_ref, recv_ref,
    query_ref, receiver_ref, grad_ref,
    cots, receiver, columns, lines,
):
    rows, latent = grad_ref.shape
    hidden = band_ref[:, :latent]
    query_ref[...] = dot(hidden, proc_ref[...]).astype(BF)
    receiver[...] = dot(hidden, recv_ref[...])
    receiver_ref[...] = receiver[:rows, :]
    columns[...] = senders(band_ref[:, 2 * latent :], sub_ref[0] + 1, rows)
    lines[...] = columns[...].T
    cots[...] = band_ref[:, latent : 2 * latent].astype(F32) * mesh_scale
    grad_ref[...] = jnp.zeros_like(grad_ref)
    sent_back(count, columns, lines, cots, receiver, query_ref[:rows, :], grad_ref)


def mesh_kernel(
    mesh_scale, scale, count,
    sub_ref, own_ref, far_ref, side_ref, query_ref, receiver_ref, near_ref, proc_ref, recv_ref, edge_ref,
    active_ref, normed_ref, inverse_ref, bslope_ref, hidden_ref,
    out_ref, bgrad_ref, wgrad_ref,
    far_receiver, cots, columns, lines, query_grad, upper_ref, edge_total, src_total,
):
    step = pl.program_id(0)
    rows, latent = side_ref.shape
    wide = far_ref.shape[0]

    @pl.when(step == 0)
    def _():
        sub = sub_ref[0]
        lower = sub < SUBS // 2
        proc = proc_ref[...]
        recv = recv_ref[...]
        own = own_ref[:, :latent]
        beyond = jnp.concatenate([far_ref[:, :latent], side_ref[...]], axis=0)
        query = jnp.concatenate([query_ref[...], dot(beyond, proc).astype(BF)], axis=0)
        receiver = receiver_ref[...]

        tail = own_ref[:, 2 * latent :].astype(F32).astype(jnp.int32)
        turn = tail.shape[1] // 2
        block, line = tail[:, :turn], tail[:, turn:]
        inside = lax.rem(sub + SUBS + 1 - block, SUBS) * rows
        below = jnp.where(lower, wide + lax.rem(sub + 1, SUBS) * rows, 2 * wide)
        above = jnp.where(lower, 2 * wide, wide + sub * rows)
        place = jnp.where(block == 0, below, jnp.where(block == SUBS + 1, above, inside)) + line
        summed = jnp.zeros((rows, latent), F32)
        slopes = jnp.zeros((rows, latent), F32)
        for j in range(count):
            sent = dot(selection(place[:, j : j + 1], query.shape[0]), query)
            active, slope = silu_and_slope(sent + receiver)
            summed += active
            slopes += slope
        out_ref[...] = (own.astype(F32) + summed * mesh_scale).astype(BF)
        upstream = own_ref[:, latent : 2 * latent].astype(F32)
        receiver_grad = upstream * mesh_scale * slopes

        wanted = jnp.where(lower, SUBS + 1 + sub, sub - SUBS + 1)
        columns[...] = senders(far_ref[:, 2 * latent :], wanted, rows)
        lines[...] = columns[...].T
        cots[...] = far_ref[:, latent : 2 * latent].astype(F32) * mesh_scale
        far_receiver[...] = dot(far_ref[:, :latent], recv)
        query_grad[...] = near_ref[...]
        sent_back(count, columns, lines, cots, far_receiver, query_ref[:rows, :], query_grad)
        mesh_grad = upstream + dot_t(query_grad[...].astype(BF), proc)
        mesh_grad = mesh_grad + dot_t(receiver_grad.astype(BF), recv)
        upper_ref[...] = mesh_grad * scale
        edge_total[...] = jnp.zeros_like(edge_total)
        src_total[...] = jnp.zeros_like(src_total)

    upper = upper_ref[...]
    centred = upper - jnp.mean(upper, axis=-1, keepdims=True)
    normed = normed_ref[...].astype(F32).reshape(-1, rows, latent)
    inverse = inverse_ref[...].reshape(-1, rows, 1)
    along = jnp.mean(upper[None] * normed, axis=-1, keepdims=True)
    ngrad = ((centred[None] - normed * along) * inverse).reshape(-1, latent).astype(BF)
    edge_total[...] += t_dot(active_ref[...], ngrad)
    bgrad = (dot_t(ngrad, edge_ref[...]) * bslope_ref[...].astype(F32)).astype(BF)
    bgrad_ref[...] = bgrad
    src_total[...] += t_dot(hidden_ref[...], bgrad)

    @pl.when(step == pl.num_programs(0) - 1)
    def _():
        wgrad_ref[:latent, :] = edge_total[...].astype(BF)
        wgrad_ref[latent:, :] = src_total[...].astype(BF)


def grid_kernel(
    sub_ref, index_ref, src_ref, embed_ref, bgrad_ref, hslope_ref,
    own_ref, one_ref, two_ref, three_ref, low_ref, high_ref,
    pad, total,
):
    step = pl.program_id(0)
    channels, nodes = low_ref.shape
    targets = (own_ref, one_ref, two_ref, three_ref, low_ref, high_ref)
    sub = sub_ref[0]
    bases = [(lax.rem(sub + k, SUBS) + 1) * nodes for k in range(SUBS)]
    bases += [0, (SUBS + 1) * nodes]

    @pl.when(step == 0)
    def _():
        padded_rows(embed_ref, pad)
        total[...] = jnp.zeros_like(total)

    hgrad = (dot_t(bgrad_ref[...], src_ref[...]) * hslope_ref[...].astype(F32)).astype(BF)
    ggrad = dot_t(pad[...], hgrad).astype(BF)
    column = index_ref[...]
    for block, base in enumerate(bases):
        total[block] += dot(ggrad, selection(column - base, nodes))

    @pl.when(step == pl.num_programs(0) - 1)
    def _():
        for block, target in enumerate(targets):
            target[...] = total[block][:channels].astype(BF)


def whole(shape):
    return pl.BlockSpec(shape, lambda i, n=len(shape): (0,) * n)


def tiled(edges, width):
    return pl.BlockSpec((edges, width), lambda i: (i, 0))


def scalar():
    return pl.BlockSpec(memory_space=pltpu.SMEM)


def params():
    return pltpu.CompilerParams(dimension_semantics=("arbitrary",), vmem_limit_bytes=VMEM)


def from_everyone(shard, axis):
    devices = lax.axis_size(axis)
    return lax.all_to_all(
        jnp.broadcast_to(shard[None], (devices, *shard.shape)), axis, 0, 0, tiled=True
    )


def bands_up(value):
    count = lax.axis_size(BAND)
    return lax.ppermute(value, BAND, [(i, i + 1) for i in range(count - 1)])


def bands_down(value):
    count = lax.axis_size(BAND)
    return lax.ppermute(value, BAND, [(i + 1, i) for i in range(count - 1)])


def outwards(value, near):
    bands, subs = lax.axis_size(BAND), lax.axis_size("sub")
    pairs = []
    for band in range(bands):
        for sub in range(subs):
            up = (sub < subs // 2) == near
            to = band + 1 if up else band - 1
            if 0 <= to < bands:
                pairs.append((band * subs + sub, to * subs + sub))
    return lax.ppermute(value, ALL, pairs)


def along_sub(value, steps):
    count = lax.axis_size("sub")
    return lax.ppermute(value, "sub", [(i, (i + steps) % count) for i in range(count)])


def summed(parts):
    return jnp.sum(parts.astype(F32), axis=0).astype(BF)


def body(
    grid_x, mesh_in, w_embed, w_src, w_dst, w_edge, w_proc, w_recv, g2m_src, mesh_src, cotangent
):
    channels, nodes = grid_x.shape
    latent = w_src.shape[0]
    rows, enc_count = g2m_src.shape
    mesh_count = mesh_src.shape[1]
    band = lax.axis_index(BAND)
    sub = lax.axis_index("sub")
    sub_scalar = sub.astype(jnp.int32).reshape(1)
    wide = -(-channels // 128) * 128
    edges = rows * enc_count
    steps = 4
    tile = edges // steps
    width = SUBS * rows
    scale = 1.0 / math.sqrt(enc_count)
    mesh_scale = 1.0 / math.sqrt(mesh_count)

    grid = [grid_x] + [along_sub(grid_x, k) for k in range(1, SUBS)]
    grid_local = (g2m_src - (band * (nodes * SUBS) - nodes)).T.reshape(edges, 1)

    place = mesh_src - (band * width - rows)
    half = 64
    spare = jnp.zeros((rows, half - mesh_count), BF)
    pay = jnp.concatenate(
        [cotangent, (place // rows).astype(BF), spare, (place % rows).astype(BF), spare], axis=1
    )
    pays = [pay] + [along_sub(pay, k) for k in range(1, SUBS)]

    nearest = (0, 1, 3)
    picked = pl.pallas_call(
        functools.partial(gather_kernel, nearest),
        grid=(2,),
        in_specs=[scalar(), tiled(edges // 2, 1)] + [whole((channels, nodes))] * len(nearest),
        out_specs=tiled(edges // 2, wide),
        out_shape=jax.ShapeDtypeStruct((edges, wide), BF),
        scratch_shapes=[
            pltpu.VMEM((len(nearest) * nodes, wide), BF),
            pltpu.VMEM((wide, nodes), BF),
        ],
        compiler_params=params(),
        cost_estimate=pl.CostEstimate(
            flops=2 * edges * wide * nodes * len(nearest),
            bytes_accessed=2 * edges * wide,
            transcendentals=0,
        ),
        name="gather",
    )(sub_scalar, grid_local, *[grid[k] for k in nearest])

    grid[2], picked, *pays = lax.optimization_barrier((grid[2], picked, *pays))
    last = lax.select_n(lax.rem(sub + 1, SUBS), *grid)
    first = lax.select_n(sub, *grid)
    grid_low = bands_up(last)
    grid_high = bands_down(first)

    hidden, hslope, active, bslope, normed, inverse, hidden_mesh = pl.pallas_call(
        functools.partial(forward_kernel, scale),
        grid=(steps,),
        in_specs=[scalar(), tiled(tile, 1), tiled(tile, wide)]
        + [whole((channels, nodes))] * 3
        + [
            whole((rows, latent)),
            whole((channels, latent)),
            whole((latent, latent)),
            whole((latent, latent)),
            whole((latent, latent)),
        ],
        out_specs=[tiled(tile, latent)] * 5 + [tiled(tile, 1), whole((rows, latent))],
        out_shape=[jax.ShapeDtypeStruct((edges, latent), BF)] * 5
        + [jax.ShapeDtypeStruct((edges, 1), F32), jax.ShapeDtypeStruct((rows, latent), BF)],
        scratch_shapes=[
            pltpu.VMEM((3 * nodes, wide), BF),
            pltpu.VMEM((wide, nodes), BF),
            pltpu.VMEM((wide, latent), BF),
            pltpu.VMEM((rows, latent), F32),
            pltpu.VMEM((rows, latent), F32),
        ],
        compiler_params=params(),
        name="encode",
    )(sub_scalar, grid_local, picked, grid[2], grid_low, grid_high, mesh_in, w_embed, w_src, w_dst, w_edge)

    mesh_band = jnp.concatenate([hidden_mesh] + [along_sub(hidden_mesh, k) for k in range(1, SUBS)])
    mesh_band = jnp.concatenate([mesh_band, jnp.concatenate(pays)], axis=1)
    mesh_far = outwards(mesh_band, True)
    at = jnp.where(sub < SUBS // 2, sub, lax.rem(sub + 1, SUBS)) * rows
    mesh_side = outwards(lax.dynamic_slice(mesh_band, (at, 0), (rows, latent)), False)

    band_then = mesh_band
    query_band, receiver, near_grad = pl.pallas_call(
        functools.partial(near_kernel, mesh_scale, mesh_count),
        grid=(1,),
        in_specs=[
            scalar(),
            whole((width, 2 * latent + 2 * half)),
            whole((latent, latent)),
            whole((latent, latent)),
        ],
        out_specs=[whole((width, latent)), whole((rows, latent)), whole((rows, latent))],
        out_shape=[
            jax.ShapeDtypeStruct((width, latent), BF),
            jax.ShapeDtypeStruct((rows, latent), F32),
            jax.ShapeDtypeStruct((rows, latent), F32),
        ],
        scratch_shapes=[
            pltpu.VMEM((width, latent), F32),
            pltpu.VMEM((width, latent), F32),
            pltpu.VMEM((width, half), jnp.int32),
            pltpu.VMEM((half, width), jnp.int32),
        ],
        compiler_params=params(),
        cost_estimate=pl.CostEstimate(
            flops=8 * width * latent * latent, bytes_accessed=4 * width * latent, transcendentals=0
        ),
        name="near",
    )(sub_scalar, band_then, w_proc, w_recv)

    mesh_out, bgrad, part = pl.pallas_call(
        functools.partial(mesh_kernel, mesh_scale, scale, mesh_count),
        grid=(steps,),
        in_specs=[
            scalar(),
            whole((rows, 2 * latent + 2 * half)),
            whole((width, 2 * latent + 2 * half)),
            whole((rows, latent)),
            whole((width, latent)),
            whole((rows, latent)),
            whole((rows, latent)),
            whole((latent, latent)),
            whole((latent, latent)),
            whole((latent, latent)),
            tiled(tile, latent),
            tiled(tile, latent),
            tiled(tile, 1),
            tiled(tile, latent),
            tiled(tile, latent),
        ],
        out_specs=[whole((rows, latent)), tiled(tile, latent), whole((2 * latent, latent))],
        out_shape=[
            jax.ShapeDtypeStruct((rows, latent), BF),
            jax.ShapeDtypeStruct((edges, latent), BF),
            jax.ShapeDtypeStruct((2 * latent, latent), BF),
        ],
        scratch_shapes=[
            pltpu.VMEM((width, latent), F32),
            pltpu.VMEM((width, latent), F32),
            pltpu.VMEM((width, half), jnp.int32),
            pltpu.VMEM((half, width), jnp.int32),
            pltpu.VMEM((rows, latent), F32),
            pltpu.VMEM((rows, latent), F32),
            pltpu.VMEM((latent, latent), F32),
            pltpu.VMEM((latent, latent), F32),
        ],
        compiler_params=params(),
        name="process",
    )(
        sub_scalar, mesh_band, mesh_far, mesh_side, query_band, receiver, near_grad,
        w_proc, w_recv, w_edge, active, normed, inverse, bslope, hidden,
    )

    *parts, part_low, part_high = pl.pallas_call(
        grid_kernel,
        grid=(steps,),
        in_specs=[
            scalar(),
            tiled(tile, 1),
            whole((latent, latent)),
            whole((channels, latent)),
            tiled(tile, latent),
            tiled(tile, latent),
        ],
        out_specs=[whole((channels, nodes))] * (SUBS + 2),
        out_shape=[jax.ShapeDtypeStruct((channels, nodes), BF)] * (SUBS + 2),
        scratch_shapes=[pltpu.VMEM((wide, latent), BF), pltpu.VMEM((SUBS + 2, wide, nodes), F32)],
        compiler_params=params(),
        name="channels",
    )(sub_scalar, grid_local, w_src, w_embed, bgrad, hslope)

    near = lax.axis_size(NEAR)
    pieces = lax.all_to_all(part.reshape(near, -1, latent), NEAR, 0, 0, tiled=True)
    from_above = bands_down(part_low)
    from_below = bands_up(part_high)
    values = []
    for k in range(SUBS):
        block = lax.rem(sub + k, SUBS)
        value = parts[k].astype(F32)
        value += jnp.where(block == 0, from_below, jnp.zeros_like(from_below)).astype(F32)
        value += jnp.where(block == SUBS - 1, from_above, jnp.zeros_like(from_above)).astype(F32)
        values.append(value.astype(BF) if k else value)
    arrived = values[:1] + [along_sub(values[k], k) for k in range(1, SUBS)]
    pieces = from_everyone(summed(pieces), FAR)
    pieces, arrived[1], arrived[3] = lax.optimization_barrier((pieces, arrived[1], arrived[3]))
    weights = from_everyone(summed(pieces), NEAR).reshape(2 * latent, latent)
    grid_grad = functools.reduce(jnp.add, [value.astype(F32) for value in arrived])
    src_grad, edge_grad = weights[latent:].astype(F32), weights[:latent].astype(F32)
    return (mesh_out, grid_grad, src_grad, edge_grad)


def solution(mesh):
    torus = Mesh(mesh.devices.reshape(8, 4, 2, mesh.shape["sub"]), ALL)
    return jax.shard_map(
        body,
        mesh=torus,
        in_specs=(
            P(None, ALL),
            P(ALL, None),
            P(),
            P(),
            P(),
            P(),
            P(),
            P(),
            P(ALL, None),
            P(ALL, None),
            P(ALL, None),
        ),
        out_specs=(P(ALL, None), P(None, ALL), P(), P()),
        check_vma=False,
    )
```

```python
import functools
import math

import jax
import jax.numpy as jnp
from jax import lax
from jax.experimental import pallas as pl
from jax.experimental.pallas import tpu as pltpu
from jax.sharding import Mesh
from jax.sharding import PartitionSpec as P

BAND = ("band_0", "band_1", "band_2")
ALL = ("band_0", "band_1", "band_2", "sub")
NEAR = ("band_1", "band_2", "sub")
FAR = "band_0"
SUBS = 4

EPSILON = 1e-05
BF = jnp.bfloat16
F32 = jnp.float32
VMEM = 60 * 1024 * 1024


def sigmoid(value):
    return 0.5 * jnp.tanh(0.5 * value) + 0.5


def silu_and_slope(value):
    sigma = sigmoid(value)
    active = value * sigma
    return active, sigma + active * (1.0 - sigma)


def dot(left, right):
    return jnp.dot(left, right, preferred_element_type=F32)


def dot_t(left, right):
    return lax.dot_general(left, right, (((1,), (1,)), ((), ())), preferred_element_type=F32)


def t_dot(left, right):
    return lax.dot_general(left, right, (((0,), (0,)), ((), ())), preferred_element_type=F32)


def selection(column, width):
    lanes = lax.broadcasted_iota(jnp.int32, (column.shape[0], width), 1)
    return jnp.where(column == lanes, 1.0, 0.0).astype(BF)


def selection_t(row, height):
    lines = lax.broadcasted_iota(jnp.int32, (height, row.shape[1]), 0)
    return jnp.where(row == lines, 1.0, 0.0).astype(BF)


def padded_rows(ref, scratch):
    rows = ref.shape[0]
    scratch[...] = jnp.zeros_like(scratch)
    scratch[:rows, :] = ref[...]
    return scratch[...]


def gather_kernel(blocks, sub_ref, index_ref, *refs):
    *sources, picked_ref, table, pad = refs
    nodes = sources[0].shape[1]
    sub = sub_ref[0]

    @pl.when(pl.program_id(0) == 0)
    def _():
        for place, source in enumerate(sources):
            table[place * nodes : (place + 1) * nodes, :] = padded_rows(source, pad).T

    column = index_ref[...]
    chosen = [
        selection(column - (lax.rem(sub + SUBS - k, SUBS) + 1) * nodes, nodes) for k in blocks
    ]
    picked_ref[...] = dot(jnp.concatenate(chosen, axis=1), table[...]).astype(BF)


def forward_kernel(
    scale,
    sub_ref, index_ref, picked_ref, two_ref, low_ref, high_ref,
    mesh_ref, embed_ref, src_ref, dst_ref, edge_ref,
    hidden_ref, hslope_ref, active_ref, bslope_ref, normed_ref, inverse_ref, mesh_out_ref,
    table, pad, embed, dest, total,
):
    step = pl.program_id(0)
    sources = (two_ref, low_ref, high_ref)
    nodes = low_ref.shape[1]
    rows = mesh_ref.shape[0]
    sub = sub_ref[0]
    bases = [(lax.rem(sub + SUBS - 2, SUBS) + 1) * nodes, 0, (SUBS + 1) * nodes]

    @pl.when(step == 0)
    def _():
        for block, source in enumerate(sources):
            table[block * nodes : (block + 1) * nodes, :] = padded_rows(source, pad).T
        embed[...] = padded_rows(embed_ref, pad)
        dest[...] = dot(mesh_ref[...], dst_ref[...])
        total[...] = jnp.zeros_like(total)

    column = index_ref[...]
    chosen = [selection(column - base, nodes) for base in bases]
    picked = dot(jnp.concatenate(chosen, axis=1), table[...]).astype(BF) + picked_ref[...]
    hidden, hslope = silu_and_slope(dot(picked, embed[...]))
    hidden = hidden.astype(BF)
    hidden_ref[...] = hidden
    hslope_ref[...] = hslope.astype(BF)
    projected = dot(hidden, src_ref[...]).astype(BF).astype(F32)
    before = (projected.reshape(-1, rows, projected.shape[1]) + dest[...][None]).reshape(projected.shape)
    active, bslope = silu_and_slope(before)
    active = active.astype(BF)
    active_ref[...] = active
    bslope_ref[...] = bslope.astype(BF)
    out = dot(active, edge_ref[...])
    centred = out - jnp.mean(out, axis=-1, keepdims=True)
    inverse = lax.rsqrt(jnp.mean(centred * centred, axis=-1, keepdims=True) + EPSILON)
    normed = centred * inverse
    normed_ref[...] = normed.astype(BF)
    inverse_ref[...] = inverse
    total[...] += jnp.sum(normed.reshape(-1, rows, normed.shape[1]), axis=0)

    @pl.when(step == pl.num_programs(0) - 1)
    def _():
        mesh_out_ref[...] = (mesh_ref[...].astype(F32) + total[...] * scale).astype(BF)


def mesh_kernel(
    mesh_scale, scale, count,
    sub_ref, band_ref, far_ref, side_ref, pay_ref, far_pay_ref, proc_ref, recv_ref, edge_ref,
    active_ref, normed_ref, inverse_ref, bslope_ref, hidden_ref,
    out_ref, bgrad_ref, wgrad_ref,
    receiver_all, cots, columns, lines, query_grad, upper_ref, edge_total, src_total,
):
    step = pl.program_id(0)
    rows, latent = side_ref.shape
    wide = band_ref.shape[0]

    @pl.when(step == 0)
    def _():
        sub = sub_ref[0]
        lower = sub < SUBS // 2
        proc = proc_ref[...]
        recv = recv_ref[...]
        own = band_ref[:rows, :]
        window = jnp.concatenate([band_ref[...], far_ref[...], side_ref[...]], axis=0)
        query = dot(window, proc).astype(BF)
        receiver_all[:wide, :] = dot(band_ref[...], recv)
        receiver_all[wide:, :] = dot(far_ref[...], recv)
        receiver = receiver_all[:rows, :]

        tail = pay_ref[:, latent:].astype(F32).astype(jnp.int32)
        far_tail = far_pay_ref[:, latent:].astype(F32).astype(jnp.int32)
        turn = tail.shape[1] // 2
        block, line = tail[:, :turn], tail[:, turn:]
        far_block, far_line = far_tail[:, :turn], far_tail[:, turn:]
        far_wanted = jnp.where(lower, SUBS + 1 + sub, sub - SUBS + 1)
        columns[:wide, :turn] = (block - (sub + 1)) * rows + line
        columns[wide:, :turn] = (far_block - far_wanted) * rows + far_line
        own_block, own_line = block[:rows], line[:rows]
        inside = lax.rem(sub + SUBS + 1 - own_block, SUBS) * rows
        below = jnp.where(lower, wide + lax.rem(sub + 1, SUBS) * rows, 2 * wide)
        above = jnp.where(lower, 2 * wide, wide + sub * rows)
        place = jnp.where(own_block == 0, below, jnp.where(own_block == SUBS + 1, above, inside))
        place = place + own_line
        columns[:, turn:] = jnp.zeros_like(columns[:, turn:])
        lines[...] = columns[...].T
        cots[:wide, :] = pay_ref[:, :latent].astype(F32) * mesh_scale
        cots[wide:, :] = far_pay_ref[:, :latent].astype(F32) * mesh_scale

        summed = jnp.zeros((rows, latent), F32)
        slopes = jnp.zeros((rows, latent), F32)
        for j in range(count):
            sent = dot(selection(place[:, j : j + 1], window.shape[0]), query)
            active, slope = silu_and_slope(sent + receiver)
            summed += active
            slopes += slope
        out_ref[...] = (own.astype(F32) + summed * mesh_scale).astype(BF)
        receiver_grad = cots[:rows, :] * slopes

        own_query = query[:rows]
        query_grad[...] = jnp.zeros_like(query_grad)
        lanes = lax.broadcasted_iota(jnp.int32, columns.shape, 1)

        def one(j, carry):
            column = jnp.sum(jnp.where(lanes == j, columns[...], 0), axis=1, keepdims=True)
            value = dot(selection(column, rows), own_query) + receiver_all[...]
            _, slopes = silu_and_slope(value)
            slopes = (cots[...] * slopes).astype(BF)
            query_grad[...] += dot(selection_t(lines[pl.ds(j, 1), :], rows), slopes)
            return carry

        lax.fori_loop(0, count, one, 0)
        mesh_grad = pay_ref[:rows, :latent].astype(F32) + dot_t(query_grad[...].astype(BF), proc)
        mesh_grad = mesh_grad + dot_t(receiver_grad.astype(BF), recv)
        upper_ref[...] = mesh_grad * scale
        edge_total[...] = jnp.zeros_like(edge_total)
        src_total[...] = jnp.zeros_like(src_total)

    upper = upper_ref[...]
    centred = upper - jnp.mean(upper, axis=-1, keepdims=True)
    normed = normed_ref[...].astype(F32).reshape(-1, rows, latent)
    inverse = inverse_ref[...].reshape(-1, rows, 1)
    along = jnp.mean(upper[None] * normed, axis=-1, keepdims=True)
    ngrad = ((centred[None] - normed * along) * inverse).reshape(-1, latent).astype(BF)
    edge_total[...] += t_dot(active_ref[...], ngrad)
    bgrad = (dot_t(ngrad, edge_ref[...]) * bslope_ref[...].astype(F32)).astype(BF)
    bgrad_ref[...] = bgrad
    src_total[...] += t_dot(hidden_ref[...], bgrad)

    @pl.when(step == pl.num_programs(0) - 1)
    def _():
        wgrad_ref[:latent, :] = edge_total[...].astype(BF)
        wgrad_ref[latent:, :] = src_total[...].astype(BF)


def grid_kernel(
    sub_ref, index_ref, src_ref, embed_ref, bgrad_ref, hslope_ref,
    own_ref, one_ref, two_ref, three_ref, low_ref, high_ref,
    pad, total,
):
    step = pl.program_id(0)
    channels, nodes = low_ref.shape
    targets = (own_ref, one_ref, two_ref, three_ref, low_ref, high_ref)
    sub = sub_ref[0]
    bases = [(lax.rem(sub + k, SUBS) + 1) * nodes for k in range(SUBS)]
    bases += [0, (SUBS + 1) * nodes]

    @pl.when(step == 0)
    def _():
        padded_rows(embed_ref, pad)
        total[...] = jnp.zeros_like(total)

    hgrad = (dot_t(bgrad_ref[...], src_ref[...]) * hslope_ref[...].astype(F32)).astype(BF)
    ggrad = dot_t(pad[...], hgrad).astype(BF)
    column = index_ref[...]
    for block, base in enumerate(bases):
        total[block] += dot(ggrad, selection(column - base, nodes))

    @pl.when(step == pl.num_programs(0) - 1)
    def _():
        for block, target in enumerate(targets):
            target[...] = total[block][:channels].astype(BF)


def whole(shape):
    return pl.BlockSpec(shape, lambda i, n=len(shape): (0,) * n)


def tiled(edges, width):
    return pl.BlockSpec((edges, width), lambda i: (i, 0))


def scalar():
    return pl.BlockSpec(memory_space=pltpu.SMEM)


def params():
    return pltpu.CompilerParams(dimension_semantics=("arbitrary",), vmem_limit_bytes=VMEM)


def from_everyone(shard, axis):
    devices = lax.axis_size(axis)
    return lax.all_to_all(
        jnp.broadcast_to(shard[None], (devices, *shard.shape)), axis, 0, 0, tiled=True
    )


def bands_up(value):
    count = lax.axis_size(BAND)
    return lax.ppermute(value, BAND, [(i, i + 1) for i in range(count - 1)])


def bands_down(value):
    count = lax.axis_size(BAND)
    return lax.ppermute(value, BAND, [(i + 1, i) for i in range(count - 1)])


def outwards(value, near):
    bands, subs = lax.axis_size(BAND), lax.axis_size("sub")
    pairs = []
    for band in range(bands):
        for sub in range(subs):
            up = (sub < subs // 2) == near
            to = band + 1 if up else band - 1
            if 0 <= to < bands:
                pairs.append((band * subs + sub, to * subs + sub))
    return lax.ppermute(value, ALL, pairs)


def along_sub(value, steps):
    count = lax.axis_size("sub")
    return lax.ppermute(value, "sub", [(i, (i + steps) % count) for i in range(count)])


def summed(parts):
    return jnp.sum(parts.astype(F32), axis=0).astype(BF)


def body(
    grid_x, mesh_in, w_embed, w_src, w_dst, w_edge, w_proc, w_recv, g2m_src, mesh_src, cotangent
):
    channels, nodes = grid_x.shape
    latent = w_src.shape[0]
    rows, enc_count = g2m_src.shape
    mesh_count = mesh_src.shape[1]
    band = lax.axis_index(BAND)
    sub = lax.axis_index("sub")
    sub_scalar = sub.astype(jnp.int32).reshape(1)
    wide = -(-channels // 128) * 128
    edges = rows * enc_count
    steps = 4
    tile = edges // steps
    width = SUBS * rows
    scale = 1.0 / math.sqrt(enc_count)
    mesh_scale = 1.0 / math.sqrt(mesh_count)

    grid = [grid_x] + [along_sub(grid_x, k) for k in range(1, SUBS)]
    grid_local = (g2m_src - (band * (nodes * SUBS) - nodes)).T.reshape(edges, 1)

    place = mesh_src - (band * width - rows)
    half = 64
    spare = jnp.zeros((rows, half - mesh_count), BF)
    pay = jnp.concatenate(
        [cotangent, (place // rows).astype(BF), spare, (place % rows).astype(BF), spare], axis=1
    )
    pays = [pay] + [along_sub(pay, k) for k in range(1, SUBS)]

    nearest = (0, 1, 3)
    picked = pl.pallas_call(
        functools.partial(gather_kernel, nearest),
        grid=(2,),
        in_specs=[scalar(), tiled(edges // 2, 1)] + [whole((channels, nodes))] * len(nearest),
        out_specs=tiled(edges // 2, wide),
        out_shape=jax.ShapeDtypeStruct((edges, wide), BF),
        scratch_shapes=[
            pltpu.VMEM((len(nearest) * nodes, wide), BF),
            pltpu.VMEM((wide, nodes), BF),
        ],
        compiler_params=params(),
        cost_estimate=pl.CostEstimate(
            flops=2 * edges * wide * nodes * len(nearest),
            bytes_accessed=2 * edges * wide,
            transcendentals=0,
        ),
        name="gather",
    )(sub_scalar, grid_local, *[grid[k] for k in nearest])

    grid[2], picked, *pays = lax.optimization_barrier((grid[2], picked, *pays))
    last = lax.select_n(lax.rem(sub + 1, SUBS), *grid)
    first = lax.select_n(sub, *grid)
    grid_low = bands_up(last)
    grid_high = bands_down(first)
    pay = jnp.concatenate(pays)
    far_pay = outwards(pay, True)

    hidden, hslope, active, bslope, normed, inverse, hidden_mesh = pl.pallas_call(
        functools.partial(forward_kernel, scale),
        grid=(steps,),
        in_specs=[scalar(), tiled(tile, 1), tiled(tile, wide)]
        + [whole((channels, nodes))] * 3
        + [
            whole((rows, latent)),
            whole((channels, latent)),
            whole((latent, latent)),
            whole((latent, latent)),
            whole((latent, latent)),
        ],
        out_specs=[tiled(tile, latent)] * 5 + [tiled(tile, 1), whole((rows, latent))],
        out_shape=[jax.ShapeDtypeStruct((edges, latent), BF)] * 5
        + [jax.ShapeDtypeStruct((edges, 1), F32), jax.ShapeDtypeStruct((rows, latent), BF)],
        scratch_shapes=[
            pltpu.VMEM((3 * nodes, wide), BF),
            pltpu.VMEM((wide, nodes), BF),
            pltpu.VMEM((wide, latent), BF),
            pltpu.VMEM((rows, latent), F32),
            pltpu.VMEM((rows, latent), F32),
        ],
        compiler_params=params(),
        name="encode",
    )(sub_scalar, grid_local, picked, grid[2], grid_low, grid_high, mesh_in, w_embed, w_src, w_dst, w_edge)

    mesh_band = jnp.concatenate([hidden_mesh] + [along_sub(hidden_mesh, k) for k in range(1, SUBS)])
    mesh_far = outwards(mesh_band, True)
    at = jnp.where(sub < SUBS // 2, sub, lax.rem(sub + 1, SUBS)) * rows
    mesh_side = outwards(lax.dynamic_slice_in_dim(mesh_band, at, rows), False)

    mesh_out, bgrad, part = pl.pallas_call(
        functools.partial(mesh_kernel, mesh_scale, scale, mesh_count),
        grid=(steps,),
        in_specs=[
            scalar(),
            whole((width, latent)),
            whole((width, latent)),
            whole((rows, latent)),
            whole((width, latent + 2 * half)),
            whole((width, latent + 2 * half)),
            whole((latent, latent)),
            whole((latent, latent)),
            whole((latent, latent)),
            tiled(tile, latent),
            tiled(tile, latent),
            tiled(tile, 1),
            tiled(tile, latent),
            tiled(tile, latent),
        ],
        out_specs=[whole((rows, latent)), tiled(tile, latent), whole((2 * latent, latent))],
        out_shape=[
            jax.ShapeDtypeStruct((rows, latent), BF),
            jax.ShapeDtypeStruct((edges, latent), BF),
            jax.ShapeDtypeStruct((2 * latent, latent), BF),
        ],
        scratch_shapes=[
            pltpu.VMEM((2 * width, latent), F32),
            pltpu.VMEM((2 * width, latent), F32),
            pltpu.VMEM((2 * width, 2 * half), jnp.int32),
            pltpu.VMEM((2 * half, 2 * width), jnp.int32),
            pltpu.VMEM((rows, latent), F32),
            pltpu.VMEM((rows, latent), F32),
            pltpu.VMEM((latent, latent), F32),
            pltpu.VMEM((latent, latent), F32),
        ],
        compiler_params=params(),
        name="process",
    )(
        sub_scalar, mesh_band, mesh_far, mesh_side, pay, far_pay, w_proc, w_recv, w_edge,
        active, normed, inverse, bslope, hidden,
    )

    *parts, part_low, part_high = pl.pallas_call(
        grid_kernel,
        grid=(steps,),
        in_specs=[
            scalar(),
            tiled(tile, 1),
            whole((latent, latent)),
            whole((channels, latent)),
            tiled(tile, latent),
            tiled(tile, latent),
        ],
        out_specs=[whole((channels, nodes))] * (SUBS + 2),
        out_shape=[jax.ShapeDtypeStruct((channels, nodes), BF)] * (SUBS + 2),
        scratch_shapes=[pltpu.VMEM((wide, latent), BF), pltpu.VMEM((SUBS + 2, wide, nodes), F32)],
        compiler_params=params(),
        name="channels",
    )(sub_scalar, grid_local, w_src, w_embed, bgrad, hslope)

    near = lax.axis_size(NEAR)
    pieces = lax.all_to_all(part.reshape(near, -1, latent), NEAR, 0, 0, tiled=True)
    from_above = bands_down(part_low)
    from_below = bands_up(part_high)
    values = []
    for k in range(SUBS):
        block = lax.rem(sub + k, SUBS)
        value = parts[k].astype(F32)
        value += jnp.where(block == 0, from_below, jnp.zeros_like(from_below)).astype(F32)
        value += jnp.where(block == SUBS - 1, from_above, jnp.zeros_like(from_above)).astype(F32)
        values.append(value.astype(BF) if k else value)
    arrived = values[:1] + [along_sub(values[k], k) for k in range(1, SUBS)]
    pieces = from_everyone(summed(pieces), FAR)
    pieces, arrived[1], arrived[3] = lax.optimization_barrier((pieces, arrived[1], arrived[3]))
    weights = from_everyone(summed(pieces), NEAR).reshape(2 * latent, latent)
    grid_grad = functools.reduce(jnp.add, [value.astype(F32) for value in arrived])
    src_grad, edge_grad = weights[latent:].astype(F32), weights[:latent].astype(F32)
    return (mesh_out, grid_grad, src_grad, edge_grad)


def solution(mesh):
    torus = Mesh(mesh.devices.reshape(8, 4, 2, mesh.shape["sub"]), ALL)
    return jax.shard_map(
        body,
        mesh=torus,
        in_specs=(
            P(None, ALL),
            P(ALL, None),
            P(),
            P(),
            P(),
            P(),
            P(),
            P(),
            P(ALL, None),
            P(ALL, None),
            P(ALL, None),
        ),
        out_specs=(P(ALL, None), P(None, ALL), P(), P()),
        check_vma=False,
    )
```

```python
import functools
import math

import jax
import jax.numpy as jnp
from jax import lax
from jax.experimental import pallas as pl
from jax.experimental.pallas import tpu as pltpu
from jax.sharding import Mesh
from jax.sharding import PartitionSpec as P

BAND = ("band_0", "band_1", "band_2")
ALL = ("band_0", "band_1", "band_2", "sub")
NEAR = ("band_1", "band_2", "sub")
FAR = "band_0"
SUBS = 4

EPSILON = 1e-05
BF = jnp.bfloat16
F32 = jnp.float32
VMEM = 60 * 1024 * 1024


def sigmoid(value):
    return 0.5 * jnp.tanh(0.5 * value) + 0.5


def silu_and_slope(value):
    sigma = sigmoid(value)
    active = value * sigma
    return active, sigma + active * (1.0 - sigma)


def dot(left, right):
    return jnp.dot(left, right, preferred_element_type=F32)


def dot_t(left, right):
    return lax.dot_general(left, right, (((1,), (1,)), ((), ())), preferred_element_type=F32)


def t_dot(left, right):
    return lax.dot_general(left, right, (((0,), (0,)), ((), ())), preferred_element_type=F32)


def selection(column, width):
    lanes = lax.broadcasted_iota(jnp.int32, (column.shape[0], width), 1)
    return jnp.where(column == lanes, 1.0, 0.0).astype(BF)


def selection_t(row, height):
    lines = lax.broadcasted_iota(jnp.int32, (height, row.shape[1]), 0)
    return jnp.where(row == lines, 1.0, 0.0).astype(BF)


def padded_rows(ref, scratch):
    rows = ref.shape[0]
    scratch[...] = jnp.zeros_like(scratch)
    scratch[:rows, :] = ref[...]
    return scratch[...]


def gather_kernel(blocks, sub_ref, index_ref, *refs):
    *sources, picked_ref, table, pad = refs
    nodes = sources[0].shape[1]
    sub = sub_ref[0]

    @pl.when(pl.program_id(0) == 0)
    def _():
        for place, source in enumerate(sources):
            table[place * nodes : (place + 1) * nodes, :] = padded_rows(source, pad).T

    column = index_ref[...]
    chosen = [
        selection(column - (lax.rem(sub + SUBS - k, SUBS) + 1) * nodes, nodes) for k in blocks
    ]
    picked_ref[...] = dot(jnp.concatenate(chosen, axis=1), table[...]).astype(BF)


def forward_kernel(
    scale,
    sub_ref, index_ref, picked_ref, two_ref, low_ref, high_ref,
    mesh_ref, embed_ref, src_ref, dst_ref, edge_ref,
    hidden_ref, hslope_ref, active_ref, bslope_ref, normed_ref, inverse_ref, mesh_out_ref,
    table, pad, embed, dest, total,
):
    step = pl.program_id(0)
    sources = (two_ref, low_ref, high_ref)
    nodes = low_ref.shape[1]
    rows = mesh_ref.shape[0]
    sub = sub_ref[0]
    bases = [(lax.rem(sub + SUBS - 2, SUBS) + 1) * nodes, 0, (SUBS + 1) * nodes]

    @pl.when(step == 0)
    def _():
        for block, source in enumerate(sources):
            table[block * nodes : (block + 1) * nodes, :] = padded_rows(source, pad).T
        embed[...] = padded_rows(embed_ref, pad)
        dest[...] = dot(mesh_ref[...], dst_ref[...])
        total[...] = jnp.zeros_like(total)

    column = index_ref[...]
    chosen = [selection(column - base, nodes) for base in bases]
    picked = dot(jnp.concatenate(chosen, axis=1), table[...]).astype(BF) + picked_ref[...]
    hidden, hslope = silu_and_slope(dot(picked, embed[...]))
    hidden = hidden.astype(BF)
    hidden_ref[...] = hidden
    hslope_ref[...] = hslope.astype(BF)
    projected = dot(hidden, src_ref[...]).astype(BF).astype(F32)
    before = (projected.reshape(-1, rows, projected.shape[1]) + dest[...][None]).reshape(projected.shape)
    active, bslope = silu_and_slope(before)
    active = active.astype(BF)
    active_ref[...] = active
    bslope_ref[...] = bslope.astype(BF)
    out = dot(active, edge_ref[...])
    centred = out - jnp.mean(out, axis=-1, keepdims=True)
    inverse = lax.rsqrt(jnp.mean(centred * centred, axis=-1, keepdims=True) + EPSILON)
    normed = centred * inverse
    normed_ref[...] = normed.astype(BF)
    inverse_ref[...] = inverse
    total[...] += jnp.sum(normed.reshape(-1, rows, normed.shape[1]), axis=0)

    @pl.when(step == pl.num_programs(0) - 1)
    def _():
        mesh_out_ref[...] = (mesh_ref[...].astype(F32) + total[...] * scale).astype(BF)


def mesh_kernel(
    mesh_scale, scale, count,
    sub_ref, band_ref, far_ref, side_ref, pay_ref, far_pay_ref, proc_ref, recv_ref, edge_ref,
    active_ref, normed_ref, inverse_ref, bslope_ref, hidden_ref,
    out_ref, bgrad_ref, wgrad_ref,
    receiver_all, cots, columns, lines, query_grad, upper_ref, edge_total, src_total,
):
    step = pl.program_id(0)
    rows, latent = side_ref.shape
    wide = band_ref.shape[0]

    @pl.when(step == 0)
    def _():
        sub = sub_ref[0]
        lower = sub < SUBS // 2
        proc = proc_ref[...]
        recv = recv_ref[...]
        own = band_ref[:rows, :]
        window = jnp.concatenate([band_ref[...], far_ref[...], side_ref[...]], axis=0)
        query = dot(window, proc).astype(BF)
        receiver_all[:wide, :] = dot(band_ref[...], recv)
        receiver_all[wide:, :] = dot(far_ref[...], recv)
        receiver = receiver_all[:rows, :]

        tail = pay_ref[:, latent:].astype(F32).astype(jnp.int32)
        far_tail = far_pay_ref[:, latent:].astype(F32).astype(jnp.int32)
        turn = tail.shape[1] // 2
        block, line = tail[:, :turn], tail[:, turn:]
        far_block, far_line = far_tail[:, :turn], far_tail[:, turn:]
        far_wanted = jnp.where(lower, SUBS + 1 + sub, sub - SUBS + 1)
        columns[:wide, :turn] = (block - (sub + 1)) * rows + line
        columns[wide:, :turn] = (far_block - far_wanted) * rows + far_line
        own_block, own_line = block[:rows], line[:rows]
        inside = lax.rem(sub + SUBS + 1 - own_block, SUBS) * rows
        below = jnp.where(lower, wide + lax.rem(sub + 1, SUBS) * rows, 2 * wide)
        above = jnp.where(lower, 2 * wide, wide + sub * rows)
        place = jnp.where(own_block == 0, below, jnp.where(own_block == SUBS + 1, above, inside))
        place = place + own_line
        columns[:, turn:] = jnp.zeros_like(columns[:, turn:])
        lines[...] = columns[...].T
        cots[:wide, :] = pay_ref[:, :latent].astype(F32) * mesh_scale
        cots[wide:, :] = far_pay_ref[:, :latent].astype(F32) * mesh_scale

        summed = jnp.zeros((rows, latent), F32)
        slopes = jnp.zeros((rows, latent), F32)
        for j in range(count):
            sent = dot(selection(place[:, j : j + 1], window.shape[0]), query)
            active, slope = silu_and_slope(sent + receiver)
            summed += active
            slopes += slope
        out_ref[...] = (own.astype(F32) + summed * mesh_scale).astype(BF)
        receiver_grad = cots[:rows, :] * slopes

        own_query = query[:rows]
        query_grad[...] = jnp.zeros_like(query_grad)
        lanes = lax.broadcasted_iota(jnp.int32, columns.shape, 1)

        def one(j, carry):
            column = jnp.sum(jnp.where(lanes == j, columns[...], 0), axis=1, keepdims=True)
            value = dot(selection(column, rows), own_query) + receiver_all[...]
            _, slopes = silu_and_slope(value)
            slopes = (cots[...] * slopes).astype(BF)
            query_grad[...] += dot(selection_t(lines[pl.ds(j, 1), :], rows), slopes)
            return carry

        lax.fori_loop(0, count, one, 0)
        mesh_grad = pay_ref[:rows, :latent].astype(F32) + dot_t(query_grad[...].astype(BF), proc)
        mesh_grad = mesh_grad + dot_t(receiver_grad.astype(BF), recv)
        upper_ref[...] = mesh_grad * scale
        edge_total[...] = jnp.zeros_like(edge_total)
        src_total[...] = jnp.zeros_like(src_total)

    upper = upper_ref[...]
    centred = upper - jnp.mean(upper, axis=-1, keepdims=True)
    normed = normed_ref[...].astype(F32).reshape(-1, rows, latent)
    inverse = inverse_ref[...].reshape(-1, rows, 1)
    along = jnp.mean(upper[None] * normed, axis=-1, keepdims=True)
    ngrad = ((centred[None] - normed * along) * inverse).reshape(-1, latent).astype(BF)
    edge_total[...] += t_dot(active_ref[...], ngrad)
    bgrad = (dot_t(ngrad, edge_ref[...]) * bslope_ref[...].astype(F32)).astype(BF)
    bgrad_ref[...] = bgrad
    src_total[...] += t_dot(hidden_ref[...], bgrad)

    @pl.when(step == pl.num_programs(0) - 1)
    def _():
        wgrad_ref[:latent, :] = edge_total[...].astype(BF)
        wgrad_ref[latent:, :] = src_total[...].astype(BF)


def grid_kernel(
    sub_ref, index_ref, src_ref, embed_ref, bgrad_ref, hslope_ref,
    own_ref, one_ref, two_ref, three_ref, low_ref, high_ref,
    pad, total,
):
    step = pl.program_id(0)
    channels, nodes = low_ref.shape
    targets = (own_ref, one_ref, two_ref, three_ref, low_ref, high_ref)
    sub = sub_ref[0]
    bases = [(lax.rem(sub + k, SUBS) + 1) * nodes for k in range(SUBS)]
    bases += [0, (SUBS + 1) * nodes]

    @pl.when(step == 0)
    def _():
        padded_rows(embed_ref, pad)
        total[...] = jnp.zeros_like(total)

    hgrad = (dot_t(bgrad_ref[...], src_ref[...]) * hslope_ref[...].astype(F32)).astype(BF)
    ggrad = dot_t(pad[...], hgrad).astype(BF)
    column = index_ref[...]
    for block, base in enumerate(bases):
        total[block] += dot(ggrad, selection(column - base, nodes))

    @pl.when(step == pl.num_programs(0) - 1)
    def _():
        for block, target in enumerate(targets):
            target[...] = total[block][:channels].astype(BF)


def whole(shape):
    return pl.BlockSpec(shape, lambda i, n=len(shape): (0,) * n)


def tiled(edges, width):
    return pl.BlockSpec((edges, width), lambda i: (i, 0))


def scalar():
    return pl.BlockSpec(memory_space=pltpu.SMEM)


def params():
    return pltpu.CompilerParams(dimension_semantics=("arbitrary",), vmem_limit_bytes=VMEM)


def from_everyone(shard, axis):
    devices = lax.axis_size(axis)
    return lax.all_to_all(
        jnp.broadcast_to(shard[None], (devices, *shard.shape)), axis, 0, 0, tiled=True
    )


def bands_up(value):
    count = lax.axis_size(BAND)
    return lax.ppermute(value, BAND, [(i, i + 1) for i in range(count - 1)])


def bands_down(value):
    count = lax.axis_size(BAND)
    return lax.ppermute(value, BAND, [(i + 1, i) for i in range(count - 1)])


def outwards(value, near):
    bands, subs = lax.axis_size(BAND), lax.axis_size("sub")
    pairs = []
    for band in range(bands):
        for sub in range(subs):
            up = (sub < subs // 2) == near
            to = band + 1 if up else band - 1
            if 0 <= to < bands:
                pairs.append((band * subs + sub, to * subs + sub))
    return lax.ppermute(value, ALL, pairs)


def along_sub(value, steps):
    count = lax.axis_size("sub")
    return lax.ppermute(value, "sub", [(i, (i + steps) % count) for i in range(count)])


def summed(parts):
    return jnp.sum(parts.astype(F32), axis=0).astype(BF)


def body(
    grid_x, mesh_in, w_embed, w_src, w_dst, w_edge, w_proc, w_recv, g2m_src, mesh_src, cotangent
):
    channels, nodes = grid_x.shape
    latent = w_src.shape[0]
    rows, enc_count = g2m_src.shape
    mesh_count = mesh_src.shape[1]
    band = lax.axis_index(BAND)
    sub = lax.axis_index("sub")
    sub_scalar = sub.astype(jnp.int32).reshape(1)
    wide = -(-channels // 128) * 128
    edges = rows * enc_count
    steps = 4
    tile = edges // steps
    width = SUBS * rows
    scale = 1.0 / math.sqrt(enc_count)
    mesh_scale = 1.0 / math.sqrt(mesh_count)

    grid = [grid_x] + [along_sub(grid_x, k) for k in range(1, SUBS)]
    grid_local = (g2m_src - (band * (nodes * SUBS) - nodes)).T.reshape(edges, 1)

    place = mesh_src - (band * width - rows)
    half = 64
    spare = jnp.zeros((rows, half - mesh_count), BF)
    pay = jnp.concatenate(
        [cotangent, (place // rows).astype(BF), spare, (place % rows).astype(BF), spare], axis=1
    )
    pays = [pay] + [along_sub(pay, k) for k in range(1, SUBS)]

    nearest = (0, 1, 3)
    picked = pl.pallas_call(
        functools.partial(gather_kernel, nearest),
        grid=(2,),
        in_specs=[scalar(), tiled(edges // 2, 1)] + [whole((channels, nodes))] * len(nearest),
        out_specs=tiled(edges // 2, wide),
        out_shape=jax.ShapeDtypeStruct((edges, wide), BF),
        scratch_shapes=[
            pltpu.VMEM((len(nearest) * nodes, wide), BF),
            pltpu.VMEM((wide, nodes), BF),
        ],
        compiler_params=params(),
        cost_estimate=pl.CostEstimate(
            flops=2 * edges * wide * nodes * len(nearest),
            bytes_accessed=2 * edges * wide,
            transcendentals=0,
        ),
        name="gather",
    )(sub_scalar, grid_local, *[grid[k] for k in nearest])

    grid[2], picked, *pays = lax.optimization_barrier((grid[2], picked, *pays))
    last = lax.select_n(lax.rem(sub + 1, SUBS), *grid)
    first = lax.select_n(sub, *grid)
    grid_low = bands_up(last)
    grid_high = bands_down(first)
    pay = jnp.concatenate(pays)
    far_pay = outwards(pay, True)

    hidden, hslope, active, bslope, normed, inverse, hidden_mesh = pl.pallas_call(
        functools.partial(forward_kernel, scale),
        grid=(steps,),
        in_specs=[scalar(), tiled(tile, 1), tiled(tile, wide)]
        + [whole((channels, nodes))] * 3
        + [
            whole((rows, latent)),
            whole((channels, latent)),
            whole((latent, latent)),
            whole((latent, latent)),
            whole((latent, latent)),
        ],
        out_specs=[tiled(tile, latent)] * 5 + [tiled(tile, 1), whole((rows, latent))],
        out_shape=[jax.ShapeDtypeStruct((edges, latent), BF)] * 5
        + [jax.ShapeDtypeStruct((edges, 1), F32), jax.ShapeDtypeStruct((rows, latent), BF)],
        scratch_shapes=[
            pltpu.VMEM((3 * nodes, wide), BF),
            pltpu.VMEM((wide, nodes), BF),
            pltpu.VMEM((wide, latent), BF),
            pltpu.VMEM((rows, latent), F32),
            pltpu.VMEM((rows, latent), F32),
        ],
        compiler_params=params(),
        name="encode",
    )(sub_scalar, grid_local, picked, grid[2], grid_low, grid_high, mesh_in, w_embed, w_src, w_dst, w_edge)

    mesh_band = jnp.concatenate([hidden_mesh] + [along_sub(hidden_mesh, k) for k in range(1, SUBS)])
    mesh_far = outwards(mesh_band, True)
    at = jnp.where(sub < SUBS // 2, sub, lax.rem(sub + 1, SUBS)) * rows
    mesh_side = outwards(lax.dynamic_slice_in_dim(mesh_band, at, rows), False)

    mesh_out, bgrad, part = pl.pallas_call(
        functools.partial(mesh_kernel, mesh_scale, scale, mesh_count),
        grid=(steps,),
        in_specs=[
            scalar(),
            whole((width, latent)),
            whole((width, latent)),
            whole((rows, latent)),
            whole((width, latent + 2 * half)),
            whole((width, latent + 2 * half)),
            whole((latent, latent)),
            whole((latent, latent)),
            whole((latent, latent)),
            tiled(tile, latent),
            tiled(tile, latent),
            tiled(tile, 1),
            tiled(tile, latent),
            tiled(tile, latent),
        ],
        out_specs=[whole((rows, latent)), tiled(tile, latent), whole((2 * latent, latent))],
        out_shape=[
            jax.ShapeDtypeStruct((rows, latent), BF),
            jax.ShapeDtypeStruct((edges, latent), BF),
            jax.ShapeDtypeStruct((2 * latent, latent), BF),
        ],
        scratch_shapes=[
            pltpu.VMEM((2 * width, latent), F32),
            pltpu.VMEM((2 * width, latent), F32),
            pltpu.VMEM((2 * width, 2 * half), jnp.int32),
            pltpu.VMEM((2 * half, 2 * width), jnp.int32),
            pltpu.VMEM((rows, latent), F32),
            pltpu.VMEM((rows, latent), F32),
            pltpu.VMEM((latent, latent), F32),
            pltpu.VMEM((latent, latent), F32),
        ],
        compiler_params=params(),
        name="process",
    )(
        sub_scalar, mesh_band, mesh_far, mesh_side, pay, far_pay, w_proc, w_recv, w_edge,
        active, normed, inverse, bslope, hidden,
    )

    *parts, part_low, part_high = pl.pallas_call(
        grid_kernel,
        grid=(steps // 2,),
        in_specs=[
            scalar(),
            tiled(2 * tile, 1),
            whole((latent, latent)),
            whole((channels, latent)),
            tiled(2 * tile, latent),
            tiled(2 * tile, latent),
        ],
        out_specs=[whole((channels, nodes))] * (SUBS + 2),
        out_shape=[jax.ShapeDtypeStruct((channels, nodes), BF)] * (SUBS + 2),
        scratch_shapes=[pltpu.VMEM((wide, latent), BF), pltpu.VMEM((SUBS + 2, wide, nodes), F32)],
        compiler_params=params(),
        name="channels",
    )(sub_scalar, grid_local, w_src, w_embed, bgrad, hslope)

    near = lax.axis_size(NEAR)
    pieces = lax.all_to_all(part.reshape(near, -1, latent), NEAR, 0, 0, tiled=True)
    from_above = bands_down(part_low)
    from_below = bands_up(part_high)
    values = []
    for k in range(SUBS):
        block = lax.rem(sub + k, SUBS)
        value = parts[k].astype(F32)
        value += jnp.where(block == 0, from_below, jnp.zeros_like(from_below)).astype(F32)
        value += jnp.where(block == SUBS - 1, from_above, jnp.zeros_like(from_above)).astype(F32)
        values.append(value.astype(BF) if k else value)
    arrived = values[:1] + [along_sub(values[k], k) for k in range(1, SUBS)]
    pieces = from_everyone(summed(pieces), FAR)
    pieces, arrived[1], arrived[3] = lax.optimization_barrier((pieces, arrived[1], arrived[3]))
    weights = from_everyone(summed(pieces), NEAR).reshape(2 * latent, latent)
    src_grad, edge_grad = weights[latent:].astype(F32), weights[:latent].astype(F32)
    src_grad, edge_grad, arrived[2] = lax.optimization_barrier((src_grad, edge_grad, arrived[2]))
    grid_grad = functools.reduce(jnp.add, [value.astype(F32) for value in arrived])
    return (mesh_out, grid_grad, src_grad, edge_grad)


def solution(mesh):
    torus = Mesh(mesh.devices.reshape(8, 4, 2, mesh.shape["sub"]), ALL)
    return jax.shard_map(
        body,
        mesh=torus,
        in_specs=(
            P(None, ALL),
            P(ALL, None),
            P(),
            P(),
            P(),
            P(),
            P(),
            P(),
            P(ALL, None),
            P(ALL, None),
            P(ALL, None),
        ),
        out_specs=(P(ALL, None), P(None, ALL), P(), P()),
        check_vma=False,
    )
```

```python
import functools
import math

import jax
import jax.numpy as jnp
from jax import lax
from jax.experimental import pallas as pl
from jax.experimental.pallas import tpu as pltpu
from jax.sharding import Mesh
from jax.sharding import PartitionSpec as P

BAND = ("band_0", "band_1", "band_2")
ALL = ("band_0", "band_1", "band_2", "sub")
NEAR = ("band_1", "band_2", "sub")
FAR = "band_0"
SUBS = 4

EPSILON = 1e-05
BF = jnp.bfloat16
F32 = jnp.float32
VMEM = 60 * 1024 * 1024


def sigmoid(value):
    return 0.5 * jnp.tanh(0.5 * value) + 0.5


def silu_and_slope(value):
    sigma = sigmoid(value)
    active = value * sigma
    return active, sigma + active * (1.0 - sigma)


def dot(left, right):
    return jnp.dot(left, right, preferred_element_type=F32)


def dot_t(left, right):
    return lax.dot_general(left, right, (((1,), (1,)), ((), ())), preferred_element_type=F32)


def t_dot(left, right):
    return lax.dot_general(left, right, (((0,), (0,)), ((), ())), preferred_element_type=F32)


def selection(column, width):
    lanes = lax.broadcasted_iota(jnp.int32, (column.shape[0], width), 1)
    return jnp.where(column == lanes, 1.0, 0.0).astype(BF)


def selection_t(row, height):
    lines = lax.broadcasted_iota(jnp.int32, (height, row.shape[1]), 0)
    return jnp.where(row == lines, 1.0, 0.0).astype(BF)


def padded_rows(ref, scratch):
    rows = ref.shape[0]
    scratch[...] = jnp.zeros_like(scratch)
    scratch[:rows, :] = ref[...]
    return scratch[...]


def gather_kernel(blocks, sub_ref, base_ref, edges_ref, *refs):
    *sources, picked_ref, index_ref, table, pad = refs
    nodes = sources[0].shape[1]
    sub = sub_ref[0]
    step = pl.program_id(0)

    @pl.when(step == 0)
    def _():
        local = edges_ref[...] - base_ref[0]
        columns = [local[:, k : k + 1] for k in range(local.shape[1])]
        index_ref[...] = jnp.concatenate(columns, axis=0)
        for place, source in enumerate(sources):
            table[place * nodes : (place + 1) * nodes, :] = padded_rows(source, pad).T

    edges = picked_ref.shape[0]
    column = index_ref[pl.ds(pl.multiple_of(step * edges, edges), edges), :]
    chosen = [
        selection(column - (lax.rem(sub + SUBS - k, SUBS) + 1) * nodes, nodes) for k in blocks
    ]
    picked_ref[...] = dot(jnp.concatenate(chosen, axis=1), table[...]).astype(BF)


def forward_kernel(
    scale,
    sub_ref, index_ref, picked_ref, two_ref, low_ref, high_ref,
    mesh_ref, embed_ref, src_ref, dst_ref, edge_ref,
    hidden_ref, hslope_ref, active_ref, bslope_ref, normed_ref, inverse_ref, mesh_out_ref,
    table, pad, embed, dest, total,
):
    step = pl.program_id(0)
    sources = (two_ref, low_ref, high_ref)
    nodes = low_ref.shape[1]
    rows = mesh_ref.shape[0]
    sub = sub_ref[0]
    bases = [(lax.rem(sub + SUBS - 2, SUBS) + 1) * nodes, 0, (SUBS + 1) * nodes]

    @pl.when(step == 0)
    def _():
        for block, source in enumerate(sources):
            table[block * nodes : (block + 1) * nodes, :] = padded_rows(source, pad).T
        embed[...] = padded_rows(embed_ref, pad)
        dest[...] = dot(mesh_ref[...], dst_ref[...])
        total[...] = jnp.zeros_like(total)

    column = index_ref[...]
    chosen = [selection(column - base, nodes) for base in bases]
    picked = dot(jnp.concatenate(chosen, axis=1), table[...]).astype(BF) + picked_ref[...]
    hidden, hslope = silu_and_slope(dot(picked, embed[...]))
    hidden = hidden.astype(BF)
    hidden_ref[...] = hidden
    hslope_ref[...] = hslope.astype(BF)
    projected = dot(hidden, src_ref[...]).astype(BF).astype(F32)
    before = (projected.reshape(-1, rows, projected.shape[1]) + dest[...][None]).reshape(projected.shape)
    active, bslope = silu_and_slope(before)
    active = active.astype(BF)
    active_ref[...] = active
    bslope_ref[...] = bslope.astype(BF)
    out = dot(active, edge_ref[...])
    centred = out - jnp.mean(out, axis=-1, keepdims=True)
    inverse = lax.rsqrt(jnp.mean(centred * centred, axis=-1, keepdims=True) + EPSILON)
    normed = centred * inverse
    normed_ref[...] = normed.astype(BF)
    inverse_ref[...] = inverse
    total[...] += jnp.sum(normed.reshape(-1, rows, normed.shape[1]), axis=0)

    @pl.when(step == pl.num_programs(0) - 1)
    def _():
        mesh_out_ref[...] = (mesh_ref[...].astype(F32) + total[...] * scale).astype(BF)


def mesh_kernel(
    mesh_scale, scale, count,
    sub_ref, band_ref, far_ref, side_ref, pay_ref, far_pay_ref, proc_ref, recv_ref, edge_ref,
    active_ref, normed_ref, inverse_ref, bslope_ref, hidden_ref,
    out_ref, bgrad_ref, wgrad_ref,
    receiver_all, cots, columns, lines, query_grad, upper_ref, edge_total, src_total,
):
    step = pl.program_id(0)
    rows, latent = side_ref.shape
    wide = band_ref.shape[0]

    @pl.when(step == 0)
    def _():
        sub = sub_ref[0]
        lower = sub < SUBS // 2
        proc = proc_ref[...]
        recv = recv_ref[...]
        own = band_ref[:rows, :]
        window = jnp.concatenate([band_ref[...], far_ref[...], side_ref[...]], axis=0)
        query = dot(window, proc).astype(BF)
        receiver_all[:wide, :] = dot(band_ref[...], recv)
        receiver_all[wide:, :] = dot(far_ref[...], recv)
        receiver = receiver_all[:rows, :]

        tail = pay_ref[:, latent:].astype(F32).astype(jnp.int32)
        far_tail = far_pay_ref[:, latent:].astype(F32).astype(jnp.int32)
        turn = tail.shape[1] // 2
        block, line = tail[:, :turn], tail[:, turn:]
        far_block, far_line = far_tail[:, :turn], far_tail[:, turn:]
        far_wanted = jnp.where(lower, SUBS + 1 + sub, sub - SUBS + 1)
        columns[:wide, :turn] = (block - (sub + 1)) * rows + line
        columns[wide:, :turn] = (far_block - far_wanted) * rows + far_line
        own_block, own_line = block[:rows], line[:rows]
        inside = lax.rem(sub + SUBS + 1 - own_block, SUBS) * rows
        below = jnp.where(lower, wide + lax.rem(sub + 1, SUBS) * rows, 2 * wide)
        above = jnp.where(lower, 2 * wide, wide + sub * rows)
        place = jnp.where(own_block == 0, below, jnp.where(own_block == SUBS + 1, above, inside))
        place = place + own_line
        columns[:, turn:] = jnp.zeros_like(columns[:, turn:])
        lines[...] = columns[...].T
        cots[:wide, :] = pay_ref[:, :latent].astype(F32) * mesh_scale
        cots[wide:, :] = far_pay_ref[:, :latent].astype(F32) * mesh_scale

        summed = jnp.zeros((rows, latent), F32)
        slopes = jnp.zeros((rows, latent), F32)
        for j in range(count):
            sent = dot(selection(place[:, j : j + 1], window.shape[0]), query)
            active, slope = silu_and_slope(sent + receiver)
            summed += active
            slopes += slope
        out_ref[...] = (own.astype(F32) + summed * mesh_scale).astype(BF)
        receiver_grad = cots[:rows, :] * slopes

        own_query = query[:rows]
        query_grad[...] = jnp.zeros_like(query_grad)
        lanes = lax.broadcasted_iota(jnp.int32, columns.shape, 1)

        def one(j, carry):
            column = jnp.sum(jnp.where(lanes == j, columns[...], 0), axis=1, keepdims=True)
            value = dot(selection(column, rows), own_query) + receiver_all[...]
            _, slopes = silu_and_slope(value)
            slopes = (cots[...] * slopes).astype(BF)
            query_grad[...] += dot(selection_t(lines[pl.ds(j, 1), :], rows), slopes)
            return carry

        lax.fori_loop(0, count, one, 0)
        mesh_grad = pay_ref[:rows, :latent].astype(F32) + dot_t(query_grad[...].astype(BF), proc)
        mesh_grad = mesh_grad + dot_t(receiver_grad.astype(BF), recv)
        upper_ref[...] = mesh_grad * scale
        edge_total[...] = jnp.zeros_like(edge_total)
        src_total[...] = jnp.zeros_like(src_total)

    upper = upper_ref[...]
    centred = upper - jnp.mean(upper, axis=-1, keepdims=True)
    normed = normed_ref[...].astype(F32).reshape(-1, rows, latent)
    inverse = inverse_ref[...].reshape(-1, rows, 1)
    along = jnp.mean(upper[None] * normed, axis=-1, keepdims=True)
    ngrad = ((centred[None] - normed * along) * inverse).reshape(-1, latent).astype(BF)
    edge_total[...] += t_dot(active_ref[...], ngrad)
    bgrad = (dot_t(ngrad, edge_ref[...]) * bslope_ref[...].astype(F32)).astype(BF)
    bgrad_ref[...] = bgrad
    src_total[...] += t_dot(hidden_ref[...], bgrad)

    @pl.when(step == pl.num_programs(0) - 1)
    def _():
        wgrad_ref[:latent, :] = edge_total[...].astype(BF)
        wgrad_ref[latent:, :] = src_total[...].astype(BF)


def grid_kernel(
    sub_ref, index_ref, src_ref, embed_ref, bgrad_ref, hslope_ref,
    own_ref, one_ref, two_ref, three_ref, low_ref, high_ref,
    pad, total,
):
    step = pl.program_id(0)
    channels, nodes = low_ref.shape
    targets = (own_ref, one_ref, two_ref, three_ref, low_ref, high_ref)
    sub = sub_ref[0]
    bases = [(lax.rem(sub + k, SUBS) + 1) * nodes for k in range(SUBS)]
    bases += [0, (SUBS + 1) * nodes]

    @pl.when(step == 0)
    def _():
        padded_rows(embed_ref, pad)
        total[...] = jnp.zeros_like(total)

    hgrad = (dot_t(bgrad_ref[...], src_ref[...]) * hslope_ref[...].astype(F32)).astype(BF)
    ggrad = dot_t(pad[...], hgrad).astype(BF)
    column = index_ref[...]
    for block, base in enumerate(bases):
        total[block] += dot(ggrad, selection(column - base, nodes))

    @pl.when(step == pl.num_programs(0) - 1)
    def _():
        for block, target in enumerate(targets):
            target[...] = total[block][:channels].astype(BF)


def whole(shape):
    return pl.BlockSpec(shape, lambda i, n=len(shape): (0,) * n)


def tiled(edges, width):
    return pl.BlockSpec((edges, width), lambda i: (i, 0))


def scalar():
    return pl.BlockSpec(memory_space=pltpu.SMEM)


def params():
    return pltpu.CompilerParams(dimension_semantics=("arbitrary",), vmem_limit_bytes=VMEM)


def from_everyone(shard, axis):
    devices = lax.axis_size(axis)
    return lax.all_to_all(
        jnp.broadcast_to(shard[None], (devices, *shard.shape)), axis, 0, 0, tiled=True
    )


def bands_up(value):
    count = lax.axis_size(BAND)
    return lax.ppermute(value, BAND, [(i, i + 1) for i in range(count - 1)])


def bands_down(value):
    count = lax.axis_size(BAND)
    return lax.ppermute(value, BAND, [(i + 1, i) for i in range(count - 1)])


def outwards(value, near):
    bands, subs = lax.axis_size(BAND), lax.axis_size("sub")
    pairs = []
    for band in range(bands):
        for sub in range(subs):
            up = (sub < subs // 2) == near
            to = band + 1 if up else band - 1
            if 0 <= to < bands:
                pairs.append((band * subs + sub, to * subs + sub))
    return lax.ppermute(value, ALL, pairs)


def along_sub(value, steps):
    count = lax.axis_size("sub")
    return lax.ppermute(value, "sub", [(i, (i + steps) % count) for i in range(count)])


def summed(parts):
    return jnp.sum(parts.astype(F32), axis=0).astype(BF)


def body(
    grid_x, mesh_in, w_embed, w_src, w_dst, w_edge, w_proc, w_recv, g2m_src, mesh_src, cotangent
):
    channels, nodes = grid_x.shape
    latent = w_src.shape[0]
    rows, enc_count = g2m_src.shape
    mesh_count = mesh_src.shape[1]
    band = lax.axis_index(BAND)
    sub = lax.axis_index("sub")
    sub_scalar = sub.astype(jnp.int32).reshape(1)
    wide = -(-channels // 128) * 128
    edges = rows * enc_count
    steps = 4
    tile = edges // steps
    width = SUBS * rows
    scale = 1.0 / math.sqrt(enc_count)
    mesh_scale = 1.0 / math.sqrt(mesh_count)

    grid = [grid_x] + [along_sub(grid_x, k) for k in range(1, SUBS)]
    grid_base = (band * (nodes * SUBS) - nodes).astype(jnp.int32).reshape(1)

    place = mesh_src - (band * width - rows)
    half = 64
    spare = jnp.zeros((rows, half - mesh_count), BF)
    pay = jnp.concatenate(
        [cotangent, (place // rows).astype(BF), spare, (place % rows).astype(BF), spare], axis=1
    )
    pays = [pay] + [along_sub(pay, k) for k in range(1, SUBS)]

    nearest = (0, 1, 3)
    picked, grid_local = pl.pallas_call(
        functools.partial(gather_kernel, nearest),
        grid=(2,),
        in_specs=[scalar(), scalar(), whole((rows, enc_count))]
        + [whole((channels, nodes))] * len(nearest),
        out_specs=[tiled(edges // 2, wide), whole((edges, 1))],
        out_shape=[
            jax.ShapeDtypeStruct((edges, wide), BF),
            jax.ShapeDtypeStruct((edges, 1), jnp.int32),
        ],
        scratch_shapes=[
            pltpu.VMEM((len(nearest) * nodes, wide), BF),
            pltpu.VMEM((wide, nodes), BF),
        ],
        compiler_params=params(),
        cost_estimate=pl.CostEstimate(
            flops=2 * edges * wide * nodes * len(nearest),
            bytes_accessed=2 * edges * wide,
            transcendentals=0,
        ),
        name="gather",
    )(sub_scalar, grid_base, g2m_src, *[grid[k] for k in nearest])

    grid[2], picked, *pays = lax.optimization_barrier((grid[2], picked, *pays))
    last = lax.select_n(lax.rem(sub + 1, SUBS), *grid)
    first = lax.select_n(sub, *grid)
    grid_low = bands_up(last)
    grid_high = bands_down(first)
    pay = jnp.concatenate(pays)
    far_pay = outwards(pay, True)

    hidden, hslope, active, bslope, normed, inverse, hidden_mesh = pl.pallas_call(
        functools.partial(forward_kernel, scale),
        grid=(steps,),
        in_specs=[scalar(), tiled(tile, 1), tiled(tile, wide)]
        + [whole((channels, nodes))] * 3
        + [
            whole((rows, latent)),
            whole((channels, latent)),
            whole((latent, latent)),
            whole((latent, latent)),
            whole((latent, latent)),
        ],
        out_specs=[tiled(tile, latent)] * 5 + [tiled(tile, 1), whole((rows, latent))],
        out_shape=[jax.ShapeDtypeStruct((edges, latent), BF)] * 5
        + [jax.ShapeDtypeStruct((edges, 1), F32), jax.ShapeDtypeStruct((rows, latent), BF)],
        scratch_shapes=[
            pltpu.VMEM((3 * nodes, wide), BF),
            pltpu.VMEM((wide, nodes), BF),
            pltpu.VMEM((wide, latent), BF),
            pltpu.VMEM((rows, latent), F32),
            pltpu.VMEM((rows, latent), F32),
        ],
        compiler_params=params(),
        name="encode",
    )(sub_scalar, grid_local, picked, grid[2], grid_low, grid_high, mesh_in, w_embed, w_src, w_dst, w_edge)

    mesh_band = jnp.concatenate([hidden_mesh] + [along_sub(hidden_mesh, k) for k in range(1, SUBS)])
    mesh_far = outwards(mesh_band, True)
    at = jnp.where(sub < SUBS // 2, sub, lax.rem(sub + 1, SUBS)) * rows
    mesh_side = outwards(lax.dynamic_slice_in_dim(mesh_band, at, rows), False)

    mesh_out, bgrad, part = pl.pallas_call(
        functools.partial(mesh_kernel, mesh_scale, scale, mesh_count),
        grid=(steps,),
        in_specs=[
            scalar(),
            whole((width, latent)),
            whole((width, latent)),
            whole((rows, latent)),
            whole((width, latent + 2 * half)),
            whole((width, latent + 2 * half)),
            whole((latent, latent)),
            whole((latent, latent)),
            whole((latent, latent)),
            tiled(tile, latent),
            tiled(tile, latent),
            tiled(tile, 1),
            tiled(tile, latent),
            tiled(tile, latent),
        ],
        out_specs=[whole((rows, latent)), tiled(tile, latent), whole((2 * latent, latent))],
        out_shape=[
            jax.ShapeDtypeStruct((rows, latent), BF),
            jax.ShapeDtypeStruct((edges, latent), BF),
            jax.ShapeDtypeStruct((2 * latent, latent), BF),
        ],
        scratch_shapes=[
            pltpu.VMEM((2 * width, latent), F32),
            pltpu.VMEM((2 * width, latent), F32),
            pltpu.VMEM((2 * width, 2 * half), jnp.int32),
            pltpu.VMEM((2 * half, 2 * width), jnp.int32),
            pltpu.VMEM((rows, latent), F32),
            pltpu.VMEM((rows, latent), F32),
            pltpu.VMEM((latent, latent), F32),
            pltpu.VMEM((latent, latent), F32),
        ],
        compiler_params=params(),
        name="process",
    )(
        sub_scalar, mesh_band, mesh_far, mesh_side, pay, far_pay, w_proc, w_recv, w_edge,
        active, normed, inverse, bslope, hidden,
    )

    *parts, part_low, part_high = pl.pallas_call(
        grid_kernel,
        grid=(steps // 2,),
        in_specs=[
            scalar(),
            tiled(2 * tile, 1),
            whole((latent, latent)),
            whole((channels, latent)),
            tiled(2 * tile, latent),
            tiled(2 * tile, latent),
        ],
        out_specs=[whole((channels, nodes))] * (SUBS + 2),
        out_shape=[jax.ShapeDtypeStruct((channels, nodes), BF)] * (SUBS + 2),
        scratch_shapes=[pltpu.VMEM((wide, latent), BF), pltpu.VMEM((SUBS + 2, wide, nodes), F32)],
        compiler_params=params(),
        name="channels",
    )(sub_scalar, grid_local, w_src, w_embed, bgrad, hslope)

    near = lax.axis_size(NEAR)
    pieces = lax.all_to_all(part.reshape(near, -1, latent), NEAR, 0, 0, tiled=True)
    from_above = bands_down(part_low)
    from_below = bands_up(part_high)
    values = []
    for k in range(SUBS):
        block = lax.rem(sub + k, SUBS)
        value = parts[k].astype(F32)
        value += jnp.where(block == 0, from_below, jnp.zeros_like(from_below)).astype(F32)
        value += jnp.where(block == SUBS - 1, from_above, jnp.zeros_like(from_above)).astype(F32)
        values.append(value.astype(BF) if k else value)
    arrived = values[:1] + [along_sub(values[k], k) for k in range(1, SUBS)]
    pieces = from_everyone(summed(pieces), FAR)
    pieces, arrived[1], arrived[3] = lax.optimization_barrier((pieces, arrived[1], arrived[3]))
    weights = from_everyone(summed(pieces), NEAR).reshape(2 * latent, latent)
    src_grad, edge_grad = weights[latent:].astype(F32), weights[:latent].astype(F32)
    src_grad, edge_grad, arrived[2] = lax.optimization_barrier((src_grad, edge_grad, arrived[2]))
    grid_grad = functools.reduce(jnp.add, [value.astype(F32) for value in arrived])
    return (mesh_out, grid_grad, src_grad, edge_grad)


def solution(mesh):
    torus = Mesh(mesh.devices.reshape(8, 4, 2, mesh.shape["sub"]), ALL)
    return jax.shard_map(
        body,
        mesh=torus,
        in_specs=(
            P(None, ALL),
            P(ALL, None),
            P(),
            P(),
            P(),
            P(),
            P(),
            P(),
            P(ALL, None),
            P(ALL, None),
            P(ALL, None),
        ),
        out_specs=(P(ALL, None), P(None, ALL), P(), P()),
        check_vma=False,
    )
```

```python
import functools
import math

import jax
import jax.numpy as jnp
from jax import lax
from jax.experimental import pallas as pl
from jax.experimental.pallas import tpu as pltpu
from jax.sharding import Mesh
from jax.sharding import PartitionSpec as P

BAND = ("band_0", "band_1", "band_2")
ALL = ("band_0", "band_1", "band_2", "sub")
NEAR = ("band_1", "band_2", "sub")
FAR = "band_0"
SUBS = 4

EPSILON = 1e-05
BF = jnp.bfloat16
F32 = jnp.float32
VMEM = 60 * 1024 * 1024


def sigmoid(value):
    return 0.5 * jnp.tanh(0.5 * value) + 0.5


def silu_and_slope(value):
    sigma = sigmoid(value)
    active = value * sigma
    return active, sigma + active * (1.0 - sigma)


def dot(left, right):
    return jnp.dot(left, right, preferred_element_type=F32)


def dot_t(left, right):
    return lax.dot_general(left, right, (((1,), (1,)), ((), ())), preferred_element_type=F32)


def t_dot(left, right):
    return lax.dot_general(left, right, (((0,), (0,)), ((), ())), preferred_element_type=F32)


def selection(column, width):
    lanes = lax.broadcasted_iota(jnp.int32, (column.shape[0], width), 1)
    return jnp.where(column == lanes, 1.0, 0.0).astype(BF)


def selection_t(row, height):
    lines = lax.broadcasted_iota(jnp.int32, (height, row.shape[1]), 0)
    return jnp.where(row == lines, 1.0, 0.0).astype(BF)


def padded_rows(ref, scratch):
    rows = ref.shape[0]
    scratch[...] = jnp.zeros_like(scratch)
    scratch[:rows, :] = ref[...]
    return scratch[...]


def gather_kernel(blocks, sub_ref, index_ref, *refs):
    *sources, picked_ref, table, pad = refs
    nodes = sources[0].shape[1]
    sub = sub_ref[0]

    @pl.when(pl.program_id(0) == 0)
    def _():
        for place, source in enumerate(sources):
            table[place * nodes : (place + 1) * nodes, :] = padded_rows(source, pad).T

    column = index_ref[...]
    chosen = [
        selection(column - (lax.rem(sub + SUBS - k, SUBS) + 1) * nodes, nodes) for k in blocks
    ]
    picked_ref[...] = dot(jnp.concatenate(chosen, axis=1), table[...]).astype(BF)


def forward_kernel(
    scale,
    sub_ref, index_ref, picked_ref, two_ref, low_ref, high_ref,
    mesh_ref, embed_ref, src_ref, dst_ref, edge_ref,
    hidden_ref, hslope_ref, active_ref, bslope_ref, normed_ref, inverse_ref, mesh_out_ref,
    table, pad, embed, dest, total,
):
    step = pl.program_id(0)
    sources = (two_ref, low_ref, high_ref)
    nodes = low_ref.shape[1]
    rows = mesh_ref.shape[0]
    sub = sub_ref[0]
    bases = [(lax.rem(sub + SUBS - 2, SUBS) + 1) * nodes, 0, (SUBS + 1) * nodes]

    @pl.when(step == 0)
    def _():
        for block, source in enumerate(sources):
            table[block * nodes : (block + 1) * nodes, :] = padded_rows(source, pad).T
        embed[...] = padded_rows(embed_ref, pad)
        dest[...] = dot(mesh_ref[...], dst_ref[...])
        total[...] = jnp.zeros_like(total)

    column = index_ref[...]
    chosen = [selection(column - base, nodes) for base in bases]
    picked = dot(jnp.concatenate(chosen, axis=1), table[...]).astype(BF) + picked_ref[...]
    hidden, hslope = silu_and_slope(dot(picked, embed[...]))
    hidden = hidden.astype(BF)
    hidden_ref[...] = hidden
    hslope_ref[...] = hslope.astype(BF)
    projected = dot(hidden, src_ref[...]).astype(BF).astype(F32)
    before = (projected.reshape(-1, rows, projected.shape[1]) + dest[...][None]).reshape(projected.shape)
    active, bslope = silu_and_slope(before)
    active = active.astype(BF)
    active_ref[...] = active
    bslope_ref[...] = bslope.astype(BF)
    out = dot(active, edge_ref[...])
    centred = out - jnp.mean(out, axis=-1, keepdims=True)
    inverse = lax.rsqrt(jnp.mean(centred * centred, axis=-1, keepdims=True) + EPSILON)
    normed = centred * inverse
    normed_ref[...] = normed.astype(BF)
    inverse_ref[...] = inverse
    total[...] += jnp.sum(normed.reshape(-1, rows, normed.shape[1]), axis=0)

    @pl.when(step == pl.num_programs(0) - 1)
    def _():
        mesh_out_ref[...] = (mesh_ref[...].astype(F32) + total[...] * scale).astype(BF)


def mesh_kernel(
    mesh_scale, scale, count,
    sub_ref, band_ref, far_ref, side_ref, pay_ref, far_pay_ref, proc_ref, recv_ref, edge_ref,
    active_ref, normed_ref, inverse_ref, bslope_ref, hidden_ref,
    out_ref, bgrad_ref, wgrad_ref,
    receiver_all, cots, columns, lines, query_grad, upper_ref, edge_total, src_total,
):
    step = pl.program_id(0)
    rows, latent = side_ref.shape
    wide = band_ref.shape[0]

    @pl.when(step == 0)
    def _():
        sub = sub_ref[0]
        lower = sub < SUBS // 2
        proc = proc_ref[...]
        recv = recv_ref[...]
        own = band_ref[:rows, :]
        window = jnp.concatenate([band_ref[...], far_ref[...], side_ref[...]], axis=0)
        query = dot(window, proc).astype(BF)
        receiver_all[:wide, :] = dot(band_ref[...], recv)
        receiver_all[wide:, :] = dot(far_ref[...], recv)
        receiver = receiver_all[:rows, :]

        tail = pay_ref[:, latent:].astype(F32).astype(jnp.int32)
        far_tail = far_pay_ref[:, latent:].astype(F32).astype(jnp.int32)
        turn = tail.shape[1] // 2
        block, line = tail[:, :turn], tail[:, turn:]
        far_block, far_line = far_tail[:, :turn], far_tail[:, turn:]
        far_wanted = jnp.where(lower, SUBS + 1 + sub, sub - SUBS + 1)
        columns[:wide, :turn] = (block - (sub + 1)) * rows + line
        columns[wide:, :turn] = (far_block - far_wanted) * rows + far_line
        own_block, own_line = block[:rows], line[:rows]
        inside = lax.rem(sub + SUBS + 1 - own_block, SUBS) * rows
        below = jnp.where(lower, wide + lax.rem(sub + 1, SUBS) * rows, 2 * wide)
        above = jnp.where(lower, 2 * wide, wide + sub * rows)
        place = jnp.where(own_block == 0, below, jnp.where(own_block == SUBS + 1, above, inside))
        place = place + own_line
        columns[:, turn:] = jnp.zeros_like(columns[:, turn:])
        lines[...] = columns[...].T
        cots[:wide, :] = pay_ref[:, :latent].astype(F32) * mesh_scale
        cots[wide:, :] = far_pay_ref[:, :latent].astype(F32) * mesh_scale

        summed = jnp.zeros((rows, latent), F32)
        slopes = jnp.zeros((rows, latent), F32)
        for j in range(count):
            sent = dot(selection(place[:, j : j + 1], window.shape[0]), query)
            active, slope = silu_and_slope(sent + receiver)
            summed += active
            slopes += slope
        out_ref[...] = (own.astype(F32) + summed * mesh_scale).astype(BF)
        receiver_grad = cots[:rows, :] * slopes

        own_query = query[:rows]
        query_grad[...] = jnp.zeros_like(query_grad)
        lanes = lax.broadcasted_iota(jnp.int32, columns.shape, 1)

        def one(j, carry):
            column = jnp.sum(jnp.where(lanes == j, columns[...], 0), axis=1, keepdims=True)
            value = dot(selection(column, rows), own_query) + receiver_all[...]
            _, slopes = silu_and_slope(value)
            slopes = (cots[...] * slopes).astype(BF)
            query_grad[...] += dot(selection_t(lines[pl.ds(j, 1), :], rows), slopes)
            return carry

        lax.fori_loop(0, count, one, 0)
        mesh_grad = pay_ref[:rows, :latent].astype(F32) + dot_t(query_grad[...].astype(BF), proc)
        mesh_grad = mesh_grad + dot_t(receiver_grad.astype(BF), recv)
        upper_ref[...] = mesh_grad * scale
        edge_total[...] = jnp.zeros_like(edge_total)
        src_total[...] = jnp.zeros_like(src_total)

    upper = upper_ref[...]
    centred = upper - jnp.mean(upper, axis=-1, keepdims=True)
    normed = normed_ref[...].astype(F32).reshape(-1, rows, latent)
    inverse = inverse_ref[...].reshape(-1, rows, 1)
    along = jnp.mean(upper[None] * normed, axis=-1, keepdims=True)
    ngrad = ((centred[None] - normed * along) * inverse).reshape(-1, latent).astype(BF)
    edge_total[...] += t_dot(active_ref[...], ngrad)
    bgrad = (dot_t(ngrad, edge_ref[...]) * bslope_ref[...].astype(F32)).astype(BF)
    bgrad_ref[...] = bgrad
    src_total[...] += t_dot(hidden_ref[...], bgrad)

    @pl.when(step == pl.num_programs(0) - 1)
    def _():
        wgrad_ref[:latent, :] = edge_total[...].astype(BF)
        wgrad_ref[latent:, :] = src_total[...].astype(BF)


def grid_kernel(
    sub_ref, index_ref, src_ref, embed_ref, bgrad_ref, hslope_ref,
    own_ref, one_ref, two_ref, three_ref, low_ref, high_ref,
    pad, total,
):
    step = pl.program_id(0)
    channels, nodes = low_ref.shape
    targets = (own_ref, one_ref, two_ref, three_ref, low_ref, high_ref)
    sub = sub_ref[0]
    bases = [(lax.rem(sub + k, SUBS) + 1) * nodes for k in range(SUBS)]
    bases += [0, (SUBS + 1) * nodes]

    @pl.when(step == 0)
    def _():
        padded_rows(embed_ref, pad)
        total[...] = jnp.zeros_like(total)

    hgrad = (dot_t(bgrad_ref[...], src_ref[...]) * hslope_ref[...].astype(F32)).astype(BF)
    ggrad = dot_t(pad[...], hgrad).astype(BF)
    column = index_ref[...]
    for block, base in enumerate(bases):
        total[block] += dot(ggrad, selection(column - base, nodes))

    @pl.when(step == pl.num_programs(0) - 1)
    def _():
        for block, target in enumerate(targets):
            target[...] = total[block][:channels].astype(BF)


def whole(shape):
    return pl.BlockSpec(shape, lambda i, n=len(shape): (0,) * n)


def tiled(edges, width):
    return pl.BlockSpec((edges, width), lambda i: (i, 0))


def scalar():
    return pl.BlockSpec(memory_space=pltpu.SMEM)


def params():
    return pltpu.CompilerParams(dimension_semantics=("arbitrary",), vmem_limit_bytes=VMEM)


def from_everyone(shard, axis):
    devices = lax.axis_size(axis)
    return lax.all_to_all(
        jnp.broadcast_to(shard[None], (devices, *shard.shape)), axis, 0, 0, tiled=True
    )


def bands_up(value):
    count = lax.axis_size(BAND)
    return lax.ppermute(value, BAND, [(i, i + 1) for i in range(count - 1)])


def bands_down(value):
    count = lax.axis_size(BAND)
    return lax.ppermute(value, BAND, [(i + 1, i) for i in range(count - 1)])


def outwards(value, near):
    bands, subs = lax.axis_size(BAND), lax.axis_size("sub")
    pairs = []
    for band in range(bands):
        for sub in range(subs):
            up = (sub < subs // 2) == near
            to = band + 1 if up else band - 1
            if 0 <= to < bands:
                pairs.append((band * subs + sub, to * subs + sub))
    return lax.ppermute(value, ALL, pairs)


def along_sub(value, steps):
    count = lax.axis_size("sub")
    return lax.ppermute(value, "sub", [(i, (i + steps) % count) for i in range(count)])


def summed(parts):
    return jnp.sum(parts.astype(F32), axis=0).astype(BF)


def body(
    grid_x, mesh_in, w_embed, w_src, w_dst, w_edge, w_proc, w_recv, g2m_src, mesh_src, cotangent
):
    channels, nodes = grid_x.shape
    latent = w_src.shape[0]
    rows, enc_count = g2m_src.shape
    mesh_count = mesh_src.shape[1]
    band = lax.axis_index(BAND)
    sub = lax.axis_index("sub")
    sub_scalar = sub.astype(jnp.int32).reshape(1)
    wide = -(-channels // 128) * 128
    edges = rows * enc_count
    steps = 4
    tile = edges // steps
    width = SUBS * rows
    scale = 1.0 / math.sqrt(enc_count)
    mesh_scale = 1.0 / math.sqrt(mesh_count)

    grid = [grid_x] + [along_sub(grid_x, k) for k in range(1, SUBS)]
    grid_local = (g2m_src - (band * (nodes * SUBS) - nodes)).T.reshape(edges, 1)

    place = mesh_src - (band * width - rows)
    half = 64
    spare = jnp.zeros((rows, half - mesh_count), BF)
    pay = jnp.concatenate(
        [cotangent, (place // rows).astype(BF), spare, (place % rows).astype(BF), spare], axis=1
    )
    pays = [pay] + [along_sub(pay, k) for k in range(1, SUBS)]

    nearest = (0, 1, 3)
    picked = pl.pallas_call(
        functools.partial(gather_kernel, nearest),
        grid=(2,),
        in_specs=[scalar(), tiled(edges // 2, 1)] + [whole((channels, nodes))] * len(nearest),
        out_specs=tiled(edges // 2, wide),
        out_shape=jax.ShapeDtypeStruct((edges, wide), BF),
        scratch_shapes=[
            pltpu.VMEM((len(nearest) * nodes, wide), BF),
            pltpu.VMEM((wide, nodes), BF),
        ],
        compiler_params=params(),
        cost_estimate=pl.CostEstimate(
            flops=2 * edges * wide * nodes * len(nearest),
            bytes_accessed=2 * edges * wide,
            transcendentals=0,
        ),
        name="gather",
    )(sub_scalar, grid_local, *[grid[k] for k in nearest])

    grid[2], picked, *pays = lax.optimization_barrier((grid[2], picked, *pays))
    last = lax.select_n(lax.rem(sub + 1, SUBS), *grid)
    first = lax.select_n(sub, *grid)
    grid_low = bands_up(last)
    grid_high = bands_down(first)
    pay = jnp.concatenate(pays)
    far_pay = outwards(pay, True)

    hidden, hslope, active, bslope, normed, inverse, hidden_mesh = pl.pallas_call(
        functools.partial(forward_kernel, scale),
        grid=(steps,),
        in_specs=[scalar(), tiled(tile, 1), tiled(tile, wide)]
        + [whole((channels, nodes))] * 3
        + [
            whole((rows, latent)),
            whole((channels, latent)),
            whole((latent, latent)),
            whole((latent, latent)),
            whole((latent, latent)),
        ],
        out_specs=[tiled(tile, latent)] * 5 + [tiled(tile, 1), whole((rows, latent))],
        out_shape=[jax.ShapeDtypeStruct((edges, latent), BF)] * 5
        + [jax.ShapeDtypeStruct((edges, 1), F32), jax.ShapeDtypeStruct((rows, latent), BF)],
        scratch_shapes=[
            pltpu.VMEM((3 * nodes, wide), BF),
            pltpu.VMEM((wide, nodes), BF),
            pltpu.VMEM((wide, latent), BF),
            pltpu.VMEM((rows, latent), F32),
            pltpu.VMEM((rows, latent), F32),
        ],
        compiler_params=params(),
        name="encode",
    )(sub_scalar, grid_local, picked, grid[2], grid_low, grid_high, mesh_in, w_embed, w_src, w_dst, w_edge)

    mesh_band = jnp.concatenate([hidden_mesh] + [along_sub(hidden_mesh, k) for k in range(1, SUBS)])
    mesh_far = outwards(mesh_band, True)
    at = jnp.where(sub < SUBS // 2, sub, lax.rem(sub + 1, SUBS)) * rows
    mesh_side = outwards(lax.dynamic_slice_in_dim(mesh_band, at, rows), False)

    mesh_out, bgrad, part = pl.pallas_call(
        functools.partial(mesh_kernel, mesh_scale, scale, mesh_count),
        grid=(steps // 2,),
        in_specs=[
            scalar(),
            whole((width, latent)),
            whole((width, latent)),
            whole((rows, latent)),
            whole((width, latent + 2 * half)),
            whole((width, latent + 2 * half)),
            whole((latent, latent)),
            whole((latent, latent)),
            whole((latent, latent)),
            tiled(2 * tile, latent),
            tiled(2 * tile, latent),
            tiled(2 * tile, 1),
            tiled(2 * tile, latent),
            tiled(2 * tile, latent),
        ],
        out_specs=[whole((rows, latent)), tiled(2 * tile, latent), whole((2 * latent, latent))],
        out_shape=[
            jax.ShapeDtypeStruct((rows, latent), BF),
            jax.ShapeDtypeStruct((edges, latent), BF),
            jax.ShapeDtypeStruct((2 * latent, latent), BF),
        ],
        scratch_shapes=[
            pltpu.VMEM((2 * width, latent), F32),
            pltpu.VMEM((2 * width, latent), F32),
            pltpu.VMEM((2 * width, 2 * half), jnp.int32),
            pltpu.VMEM((2 * half, 2 * width), jnp.int32),
            pltpu.VMEM((rows, latent), F32),
            pltpu.VMEM((rows, latent), F32),
            pltpu.VMEM((latent, latent), F32),
            pltpu.VMEM((latent, latent), F32),
        ],
        compiler_params=params(),
        name="process",
    )(
        sub_scalar, mesh_band, mesh_far, mesh_side, pay, far_pay, w_proc, w_recv, w_edge,
        active, normed, inverse, bslope, hidden,
    )

    *parts, part_low, part_high = pl.pallas_call(
        grid_kernel,
        grid=(1,),
        in_specs=[
            scalar(),
            tiled(edges, 1),
            whole((latent, latent)),
            whole((channels, latent)),
            tiled(edges, latent),
            tiled(edges, latent),
        ],
        out_specs=[whole((channels, nodes))] * (SUBS + 2),
        out_shape=[jax.ShapeDtypeStruct((channels, nodes), BF)] * (SUBS + 2),
        scratch_shapes=[pltpu.VMEM((wide, latent), BF), pltpu.VMEM((SUBS + 2, wide, nodes), F32)],
        compiler_params=params(),
        name="channels",
    )(sub_scalar, grid_local, w_src, w_embed, bgrad, hslope)

    near = lax.axis_size(NEAR)
    pieces = lax.all_to_all(part.reshape(near, -1, latent), NEAR, 0, 0, tiled=True)
    from_above = bands_down(part_low)
    from_below = bands_up(part_high)
    values = []
    for k in range(SUBS):
        block = lax.rem(sub + k, SUBS)
        value = parts[k].astype(F32)
        value += jnp.where(block == 0, from_below, jnp.zeros_like(from_below)).astype(F32)
        value += jnp.where(block == SUBS - 1, from_above, jnp.zeros_like(from_above)).astype(F32)
        values.append(value.astype(BF) if k else value)
    arrived = values[:1] + [along_sub(values[k], k) for k in range(1, SUBS)]
    pieces = from_everyone(summed(pieces), FAR)
    pieces, arrived[1], arrived[3] = lax.optimization_barrier((pieces, arrived[1], arrived[3]))
    weights = from_everyone(summed(pieces), NEAR).reshape(2 * latent, latent)
    src_grad, edge_grad = weights[latent:].astype(F32), weights[:latent].astype(F32)
    src_grad, edge_grad, arrived[2] = lax.optimization_barrier((src_grad, edge_grad, arrived[2]))
    grid_grad = functools.reduce(jnp.add, [value.astype(F32) for value in arrived])
    return (mesh_out, grid_grad, src_grad, edge_grad)


def solution(mesh):
    torus = Mesh(mesh.devices.reshape(8, 4, 2, mesh.shape["sub"]), ALL)
    return jax.shard_map(
        body,
        mesh=torus,
        in_specs=(
            P(None, ALL),
            P(ALL, None),
            P(),
            P(),
            P(),
            P(),
            P(),
            P(),
            P(ALL, None),
            P(ALL, None),
            P(ALL, None),
        ),
        out_specs=(P(ALL, None), P(None, ALL), P(), P()),
        check_vma=False,
    )
```
